32 devices in a mesh: dp: 8 (over z, y), tensor: 4 (over x, core).
Axes of the slice: x: 2, y: 2, z: 4, core: 2. Of those that a mesh axis runs over, the one named last changes fastest.
Arguments:
- atom_types: int32 [64, 128], P(('dp', 'tensor')), may hold values from 0 to 31
- lengths: int32 [64], P(('dp', 'tensor')), may hold values from 1 to 128, as said below
- atom_feats: float32 [8192, 512], P(('dp', 'tensor')), may hold values from -6 to 6
- pair_bias: bfloat16 [64, 64, 128, 128], P(('dp', 'tensor')), may hold values from -6 to 6
- out_cotangent: float32 [8192, 512], P(('dp', 'tensor')), may hold values from -0.03 to 0.03
- type_table: float32 [32, 512], replicated, may hold values from -4 to 4
- norm_gain: float32 [512], replicated, may hold values from 0.5 to 1.5
- norm_shift: float32 [512], replicated, may hold values from -4 to 4
- w_query: float32 [512, 512], replicated, may hold values from -0.25 to 0.25
- b_query: float32 [512], replicated, may hold values from -4 to 4
- w_key: float32 [512, 512], replicated, may hold values from -0.25 to 0.25
- w_value: float32 [512, 512], replicated, may hold values from -0.25 to 0.25
- b_value: float32 [512], replicated, may hold values from -4 to 4
- w_out: float32 [512, 512], replicated, may hold values from -2 to 2
- b_out: float32 [512], replicated, may hold values from -3 to 3
- ffn_gain: float32 [512], replicated, may hold values from 0.5 to 1.5
- ffn_shift: float32 [512], replicated, may hold values from -4 to 4
- w_up: float32 [512, 2048], P(None, 'tensor'), may hold values from -0.25 to 0.25
- b_up: float32 [2048], P('tensor'), may hold values from -4 to 4
- w_down: float32 [2048, 512], P('tensor'), may hold values from -0.125 to 0.125
- b_down: float32 [512], replicated, may hold values from -3 to 3
Outputs:
- atom_out: float32 [8192, 512], P(('dp', 'tensor'))
- pair_out: float32 [64, 64, 128, 128], P(('dp', 'tensor'))
- penalty: float32 [], replicated
- grad_atoms: float32 [8192, 512], P(('dp', 'tensor'))
- grad_pair: float32 [64, 64, 128, 128], P(('dp', 'tensor'))
- grad_type_table: float32 [32, 512], replicated
- grad_norm_gain: float32 [512], replicated
- grad_norm_shift: float32 [512], replicated
- grad_w_query: float32 [512, 512], replicated
- grad_b_query: float32 [512], replicated
- grad_w_key: float32 [512, 512], replicated
- grad_w_value: float32 [512, 512], replicated
- grad_b_value: float32 [512], replicated
- grad_w_out: float32 [512, 512], replicated
- grad_b_out: float32 [512], replicated
- grad_ffn_gain: float32 [512], replicated
- grad_ffn_shift: float32 [512], replicated
- grad_w_up: float32 [512, 2048], P(None, 'tensor')
- grad_b_up: float32 [2048], P('tensor')
- grad_w_down: float32 [2048, 512], P('tensor')
- grad_b_down: float32 [512], replicated
The draws below stay inside these ranges and needn't reach their ends.
Inputs may be any that keep to these rules, and one draw needn't show every extreme that they name: Molecule m holds real atoms in its first lengths[m] of 128 slots, padding after.
All inputs are finite; a program needn't handle non-finite values.
Results may differ from the reference program's by a relative error of at most 0.0003.
Values sent between devices are 32-bit elements; how exact they have to be, the bound alone decides.
A program may use at most 128 MiB of HBM per device.

```python
import math
import jax
import jax.numpy as jnp
from jax import lax

D = 512
HEADS = 64
FF = 2048
TYPES = 32
ATOMS = 128
MOLS = 64
ROWS = 8192


def draw_lengths(key, part):
    key_large = jax.random.fold_in(key, 101)
    key_small = jax.random.fold_in(key, 202)
    key_choice = jax.random.fold_in(key, 303)
    larger = jax.random.randint(key_large, (MOLS,), ATOMS // 2, ATOMS + 1)
    smaller = jax.random.randint(key_small, (MOLS,), 1, min(8, ATOMS // 2) + 1)
    chosen = jax.random.randint(key_choice, (MOLS,), 0, 2)
    lengths = jnp.where(chosen > 0, larger, smaller)
    return lengths.at[0].set(ATOMS).astype(jnp.int32)


def touch_ends(drawn, key, low, top_value):
    shape = drawn.shape
    spot = [jax.random.randint(jax.random.fold_in(key, axis), (), 0, shape[axis]) for axis in range(len(shape))]
    drawn = drawn.at[tuple(spot)].set(low)
    longest = shape.index(max(shape))
    spot[longest] = (spot[longest] + 1) % shape[longest]
    return drawn.at[tuple(spot)].set(top_value)


def shard_levels(stream_key, shape, pieces, smallest, largest):
    def one(axis_at, parts):
        draws = jax.random.uniform(jax.random.fold_in(jax.random.fold_in(stream_key, 6), axis_at), (parts,), jnp.float32, smallest / len(pieces), largest / len(pieces))
        return jnp.repeat(jnp.exp(draws), shape[axis_at] // parts).reshape((-1,) + (1,) * (len(shape) - axis_at - 1))

    level = one(*pieces[0])
    for cut in pieces[1:]:
        level = level * one(*cut)
    return level


def noise(rng, extent, deviation, limit, cuts=(), held_as=jnp.bfloat16):
    drawn = jax.random.normal(rng, extent, jnp.float32) * deviation
    if len(cuts) > 0:
        drawn = shard_levels(rng, extent, cuts, -0.22, 0.18) * drawn
    return jnp.clip(drawn, min=-limit, max=limit).astype(held_as)


def setup_inputs(seed: int = 0) -> dict:
    arg_keys = jax.random.split(jax.random.key(seed), 22)
    atom_types = touch_ends(jax.random.randint(arg_keys[0], (MOLS, ATOMS), 0, TYPES), jax.random.fold_in(arg_keys[0], 1), 0, TYPES - 1).astype(jnp.int32)
    lengths = draw_lengths(jax.random.fold_in(arg_keys[21], 71), 0)
    atom_feats = noise(arg_keys[2], (ROWS, D), 1.0, 6.0, ((0, 32),), jnp.float32)
    pair_bias = noise(arg_keys[3], (MOLS, HEADS, ATOMS, ATOMS), 1.0, 6.0, ((0, 32),))
    out_cotangent = noise(arg_keys[4], (ROWS, D), 0.005, 0.03, ((0, 32),), jnp.float32)
    type_table = noise(arg_keys[5], (TYPES, D), 0.5, 4.0, (), jnp.float32)
    norm_gain = jnp.clip(jax.random.uniform(arg_keys[6], (D,), jnp.float32, 0.5, 1.5), 0.5, 1.5)
    norm_shift = noise(arg_keys[7], (D,), 0.5, 4.0, (), jnp.float32)
    w_query = noise(arg_keys[8], (D, D), D ** -0.5, 0.25, (), jnp.float32)
    b_query = noise(arg_keys[9], (D,), 0.5, 4.0, (), jnp.float32)
    w_key = noise(arg_keys[10], (D, D), D ** -0.5, 0.25, (), jnp.float32)
    w_value = noise(arg_keys[11], (D, D), D ** -0.5, 0.25, (), jnp.float32)
    b_value = noise(arg_keys[12], (D,), 0.5, 4.0, (), jnp.float32)
    w_out = noise(arg_keys[13], (D, D), (max(D // 64, 4)) ** -0.5, 2.0, (), jnp.float32)
    b_out = noise(arg_keys[14], (D,), 0.3, 3.0, (), jnp.float32)
    ffn_gain = jnp.clip(jax.random.uniform(arg_keys[15], (D,), jnp.float32, 0.5, 1.5), 0.5, 1.5)
    ffn_shift = noise(arg_keys[16], (D,), 0.5, 4.0, (), jnp.float32)
    w_up = noise(arg_keys[17], (D, FF), D ** -0.5, 0.25, ((1, 4),), jnp.float32)
    b_up = noise(arg_keys[18], (FF,), 0.5, 4.0, ((0, 4),), jnp.float32)
    w_down = noise(arg_keys[19], (FF, D), FF ** -0.5, 0.125, ((0, 4),), jnp.float32)
    b_down = noise(arg_keys[20], (D,), 0.3, 3.0, (), jnp.float32)
    return {"atom_types": atom_types, "lengths": lengths, "atom_feats": atom_feats, "pair_bias": pair_bias, "out_cotangent": out_cotangent, "type_table": type_table, "norm_gain": norm_gain, "norm_shift": norm_shift, "w_query": w_query, "b_query": b_query, "w_key": w_key, "w_value": w_value, "b_value": b_value, "w_out": w_out, "b_out": b_out, "ffn_gain": ffn_gain, "ffn_shift": ffn_shift, "w_up": w_up, "b_up": b_up, "w_down": w_down, "b_down": b_down}


PRECISE = lax.Precision.HIGHEST
EPSILON = 1e-05

@jax.custom_vjp
def low(v):
    return lax.optimization_barrier(v.astype(jnp.bfloat16)).astype(jnp.float32)

@jax.custom_vjp
def low_back(v):
    return v

def low_keep(v):
    return (low(v), None)

def low_pass(kept, grad):
    return (grad,)

def back_keep(v):
    return (v, None)

def back_low(kept, grad):
    return (low(grad),)
low.defvjp(low_keep, low_pass)
low_back.defvjp(back_keep, back_low)

def layer_norm(rows_in, gain, shift):
    centered = rows_in - lax.optimization_barrier(jnp.mean(rows_in, axis=-1, keepdims=True))
    variance = lax.optimization_barrier(jnp.mean(centered * centered, axis=-1, keepdims=True))
    return centered * lax.rsqrt(variance + EPSILON) * gain + shift

def gelu_exact(upper):
    return jax.nn.gelu(upper, approximate=False)

def attention_part(first, pair_in, live_atoms, norm_gain, norm_shift, w_query, b_query, w_key, w_value, b_value, w_out, b_out):
    molecules, slots, width = first.shape
    head_count = pair_in.shape[1]
    normed = layer_norm(first, norm_gain, norm_shift).reshape(molecules * slots, width)
    query = (jnp.dot(normed, w_query, precision=PRECISE) + b_query).reshape(molecules, slots, head_count, -1)
    keys = jnp.dot(normed, w_key, precision=PRECISE).reshape(molecules, slots, head_count, -1)
    values = (jnp.dot(normed, w_value, precision=PRECISE) + b_value).reshape(molecules, slots, head_count, -1)
    scale = query.shape[-1] ** (-0.5)
    logits = jnp.einsum('mihd,mjhd->mhij', query, keys, precision=PRECISE) * scale + pair_in
    masked = jnp.where(live_atoms[:, None, None, :] > 0, logits, -1e+30)
    probs = jax.nn.softmax(masked, axis=-1)
    mixed = jnp.einsum('mhij,mjhd->mihd', probs, values, precision=PRECISE).reshape(molecules * slots, width)
    middle = first + (jnp.dot(mixed, w_out, precision=PRECISE) + b_out).reshape(molecules, slots, width)
    return (middle, logits)

def ffn_part(rows_in, ffn_gain, ffn_shift, w_up, b_up, w_down, b_down):
    normed = layer_norm(rows_in, ffn_gain, ffn_shift)
    activated = gelu_exact(jnp.dot(normed, w_up, precision=PRECISE) + b_up)
    return rows_in + (jnp.dot(activated, w_down, precision=PRECISE) + b_down)

def layer_forward(weights, types_blk, live_blk, feats_in, pair_in):
    type_table, norm_gain, norm_shift, w_query, b_query, w_key, w_value, b_value, w_out, b_out, ffn_gain, ffn_shift, w_up, b_up, w_down, b_down = weights
    molecules, slots = types_blk.shape
    width = feats_in.shape[1]
    onehot = (types_blk[:, :, None] == jnp.arange(type_table.shape[0])[None, None, :]).astype(feats_in.dtype)
    first = feats_in.reshape(molecules, slots, width) + jnp.einsum('mat,td->mad', onehot, type_table, precision=PRECISE)
    middle, logits = attention_part(first, pair_in, live_blk, norm_gain, norm_shift, w_query, b_query, w_key, w_value, b_value, w_out, b_out)
    atom_block = ffn_part(middle.reshape(molecules * slots, width), ffn_gain, ffn_shift, w_up, b_up, w_down, b_down)
    pair_mask = live_blk[:, None, :, None] * live_blk[:, None, None, :]
    energy = jnp.sum(logits * logits * pair_mask)
    return (atom_block, logits, energy)

def reference(atom_types, lengths, atom_feats, pair_bias, out_cotangent, type_table, norm_gain, norm_shift, w_query, b_query, w_key, w_value, b_value, w_out, b_out, ffn_gain, ffn_shift, w_up, b_up, w_down, b_down):
    params = (type_table, norm_gain, norm_shift, w_query, b_query, w_key, w_value, b_value, w_out, b_out, ffn_gain, ffn_shift, w_up, b_up, w_down, b_down)
    live_atoms = (jnp.arange(ATOMS)[None, :] < lengths[:, None]).astype(jnp.float32)
    length_f = lengths.astype(jnp.float32)
    pair_total = jnp.sum(length_f * length_f)
    energy_scale = 1.0 / (HEADS * pair_total)
    group_size = math.gcd(MOLS, max(1, 4096 // ATOMS))
    group_steps = MOLS // group_size
    inputs = (atom_types.reshape(group_steps, group_size, ATOMS), live_atoms.reshape(group_steps, group_size, ATOMS), atom_feats.reshape(group_steps, group_size * ATOMS, D), pair_bias.astype(jnp.float32).reshape(group_steps, group_size, HEADS, ATOMS, ATOMS), out_cotangent.reshape(group_steps, group_size * ATOMS, D))

    def one_group(carry, block):
        types_blk, live_blk, feats_blk, pair_blk, cotan_blk = block

        def forward(weights, feats_in, pair_in):
            return layer_forward(weights, types_blk, live_blk, feats_in, pair_in)
        outputs, pullback = jax.vjp(forward, params, feats_blk, pair_blk)
        atom_block, logits, energy = outputs
        grad_weights, grad_feats, grad_pairs = pullback((cotan_blk, jnp.zeros_like(logits), energy_scale))
        new_carry = (jax.tree.map(jnp.add, carry[0], grad_weights), carry[1] + energy)
        return (new_carry, (atom_block, logits, grad_feats, grad_pairs))
    init = (jax.tree.map(jnp.zeros_like, params), jnp.zeros((), jnp.float32))
    (grads, energy), stacked = lax.scan(one_group, init, inputs)
    atom_out = stacked[0].reshape(ROWS, D)
    pair_out = stacked[1].reshape(MOLS, HEADS, ATOMS, ATOMS)
    grad_atoms = stacked[2].reshape(ROWS, D)
    grad_pair = stacked[3].reshape(MOLS, HEADS, ATOMS, ATOMS)
    penalty = energy * energy_scale
    return (atom_out, pair_out, penalty, grad_atoms, grad_pair, grads[0], grads[1], grads[2], grads[3], grads[4], grads[5], grads[6], grads[7], grads[8], grads[9], grads[10], grads[11], grads[12], grads[13], grads[14], grads[15])
```

```python
import functools, math
import jax, jax.numpy as jnp
from jax import lax
from jax.experimental import pallas as pl
from jax.experimental.pallas import tpu as pltpu
from jax.sharding import PartitionSpec as P
F32=jnp.float32; BF=jnp.bfloat16
EPSILON=1e-5

def split(x):
    hi = x.astype(BF)
    lo = (x - hi.astype(F32)).astype(BF)
    return hi, lo

def split3(x):
    hi = x.astype(BF)
    r = x - hi.astype(F32)
    mid = r.astype(BF)
    lo = (r - mid.astype(F32)).astype(BF)
    return hi, mid, lo

def dot(a, b):
    return jnp.dot(a, b, preferred_element_type=F32)

def dot_nt(a, b):
    return lax.dot_general(a, b, (((1,), (1,)), ((), ())), preferred_element_type=F32)

def mm3(a, bhi, blo):
    ahi, alo = split(a)
    return dot(ahi, bhi) + (dot(ahi, blo) + dot(alo, bhi))

def fwd_kernel(len_ref, types_ref, feats_ref, table_ref, gain_ref, shift_ref, wq_ref, bq_ref, wk_ref, wv_ref, bv_ref,
               wo_ref, bo_ref, bias_ref,
               pair_ref, e_ref, first_ref, qt_ref, kt_ref, vt_ref, mixt_ref, linv_ref, middle_ref,
               ql, kthi, ktlo, vthi, vtlo, wo_s):
    s = pl.program_id(0)
    mols, slots = types_ref.shape[0], types_ref.shape[2]
    groups = ql.shape[1]
    @pl.when(s == 0)
    def _():
        tab = split3(table_ref[...])
        types = table_ref.shape[0]
        for m in range(mols):
            ids = types_ref[m]
            oneT = (lax.broadcasted_iota(jnp.int32, (slots, slots), 0) == ids).astype(F32)
            one = jnp.transpose(oneT)[:, :types].astype(BF)
            rows = pl.ds(m*slots, slots)
            first = feats_ref[rows, :] + (dot(one, tab[0]) + (dot(one, tab[1]) + dot(one, tab[2])))
            first_ref[rows, :] = first
        first = first_ref[...]
        cen = first - jnp.mean(first, axis=-1, keepdims=True)
        var = jnp.mean(cen*cen, axis=-1, keepdims=True)
        normed = cen * lax.rsqrt(var + EPSILON) * gain_ref[...] + shift_ref[...]
        nhi, nlo = split(normed)
        def proj(w_ref):
            whi, wlo = split(w_ref[...])
            return dot(nhi, whi) + (dot(nhi, wlo) + dot(nlo, whi))
        q = (proj(wq_ref) + bq_ref[...]) * (8 ** -0.5)
        k = proj(wk_ref)
        v = proj(wv_ref) + bv_ref[...]
        lane = lax.broadcasted_iota(jnp.int32, (slots, 128), 1)
        for m in range(mols):
            sl = slice(m*slots, (m+1)*slots)
            qm = q[sl]
            qt_ref[m] = jnp.transpose(qm)
            kt = jnp.transpose(k[sl])
            kt_ref[m] = kt
            kthi[m], ktlo[m] = split(kt)
            vt = jnp.transpose(v[sl])
            vt_ref[m] = vt
            vthi[m], vtlo[m] = split(vt)
            for t in range(groups // 2):
                tile = qm[:, t*128:(t+1)*128]
                rolled = pltpu.roll(tile, 64, 1)
                for half in range(2):
                    dup = jnp.where(lane < 64, tile, rolled) if half == 0 else jnp.where(lane < 64, rolled, tile)
                    hi, lo = split(dup)
                    hi32, lo32 = hi.astype(F32), lo.astype(F32)
                    ql[m, 2*t+half, :, 0:128] = jnp.where(lane < 64, hi32, lo32).astype(BF)
                    ql[m, 2*t+half, :, 128:256] = jnp.where(lane < 64, hi32, 0.0).astype(BF)
    m = s // groups
    g = s % groups
    length = len_ref[m]
    col_live = lax.broadcasted_iota(jnp.int32, (slots, slots), 1) < length
    lhs = ql[m, g]
    sub = lax.broadcasted_iota(jnp.int32, (16, 128), 0)
    zero16 = jnp.zeros((16, 128), BF)
    ones = jnp.ones((16, 256), BF)
    for p in range(4):
        row = pl.multiple_of(g*64 + 16*p, 16)
        khi = kthi[m, pl.ds(row, 16), :].astype(F32)
        klo = ktlo[m, pl.ds(row, 16), :].astype(F32)
        def blk(x):
            a = jnp.where(sub < 8, x, 0.0).astype(BF)
            b = jnp.where(sub >= 8, x, 0.0).astype(BF)
            return jnp.concatenate([a, b], axis=1)
        bhi, blo = blk(khi), blk(klo)
        z = jnp.concatenate([zero16, zero16], axis=1)
        rows = [bhi if i == p else z for i in range(4)]
        rows += rows
        rows += [blo if i == p else z for i in range(4)]
        rows += [z]*4
        rhs = jnp.concatenate(rows, axis=0)
        lg = dot(lhs, rhs)
        ehl = []
        for half in range(2):
            logits = lg[:, half*128:(half+1)*128] + bias_ref[0, 2*p+half].astype(F32)
            pair_ref[0, 2*p+half] = logits
            masked = jnp.where(col_live, logits, -1e30)
            top = jnp.max(masked, axis=1, keepdims=True)
            e = jnp.exp(masked - top)
            hi, lo = split(e)
            both = jnp.concatenate([hi, lo], axis=1)
            e_ref[0, 2*p+half] = both
            ehl.append(both)
        vhi = vthi[m, pl.ds(row, 16), :]
        vlo = vtlo[m, pl.ds(row, 16), :]
        lv = jnp.concatenate([jnp.concatenate([vhi, vhi], 1), jnp.concatenate([vlo, zero16], 1), ones], 0)
        out = dot_nt(lv, jnp.concatenate(ehl, 0))
        acc = out[0:16] + out[16:32]
        sums = out[32:48]
        inv = 1.0 / jnp.concatenate([sums[0:8, 0:128], sums[8:16, 128:256]], 0)
        linv_ref[m, pl.ds(row, 16), :] = inv
        mixt_ref[m, pl.ds(row, 16), :] = jnp.concatenate([acc[0:8, 0:128], acc[8:16, 128:256]], 0) * inv
    @pl.when(s == mols*groups - 1)
    def _():
        mix = jnp.concatenate([jnp.transpose(mixt_ref[m]) for m in range(mols)], 0)
        whi, wlo = split(wo_ref[...])
        middle_ref[...] = first_ref[...] + (mm3(mix, whi, wlo) + bo_ref[...])

def attention_forward(lengths, types, feats, table, gain, shift, wq, bq, wk, wv, bv, wo, bo, bias):
    mols, slots = types.shape
    width = feats.shape[1]
    heads = bias.shape[1]
    groups = heads // 8
    rows = mols*slots
    full = lambda shape: pl.BlockSpec(shape, lambda s: (0,)*len(shape))
    vec = lambda v: v.reshape(1, -1)
    outs = [jax.ShapeDtypeStruct((mols, heads, slots, slots), F32),
            jax.ShapeDtypeStruct((mols, heads, slots, 2*slots), BF),
            jax.ShapeDtypeStruct((rows, width), F32)] + [jax.ShapeDtypeStruct((mols, width, slots), F32)]*5 + [jax.ShapeDtypeStruct((rows, width), F32)]
    blk = lambda w: pl.BlockSpec((1, 8, slots, w), lambda s: (s // groups, s % groups, 0, 0))
    in_specs = [pl.BlockSpec(memory_space=pltpu.SMEM), full((mols,1,slots)), full((rows,width)), full(table.shape), full((1,width)), full((1,width)),
                full(wq.shape), full((1,width)), full(wk.shape), full(wv.shape), full((1,width)), full(wo.shape), full((1,width)), blk(slots)]
    return pl.pallas_call(fwd_kernel, out_shape=outs, grid=(mols*groups,), in_specs=in_specs,
        out_specs=[blk(slots), blk(2*slots), full((rows,width))] + [full((mols,width,slots))]*5 + [full((rows,width))],
        scratch_shapes=[pltpu.VMEM((mols, groups, slots, 256), BF)] + [pltpu.VMEM((mols,width,slots), BF)]*4 + [pltpu.VMEM((8,128),F32)],
        compiler_params=pltpu.CompilerParams(vmem_limit_bytes=60*1024*1024, dimension_semantics=("arbitrary",)),
        name="attention_forward",
    )(lengths, types.reshape(mols,1,slots), feats, table, vec(gain), vec(shift), wq, vec(bq), wk, wv, vec(bv), wo, vec(bo), bias)

def bwd_kernel(len_ref, types_ref, scale_ref, dn2_ref, cot_ref, middle_ref, first_ref, qt_ref, kt_ref, vt_ref, mixt_ref, linv_ref,
               gain_ref, shift_ref, fgain_ref, wq_ref, wk_ref, wv_ref, wo_ref, pair_ref, e_ref,
               gpair_ref, gatoms_ref, gtable_ref, gwq_ref, gwk_ref, gwv_ref, gwo_ref, small_ref,
               dl, qhi, qlo, khi, klo, vhi, vlo, dmhi, dmlo, dqt, dkt, dvt, maskc, dmid, energy):
    s = pl.program_id(0)
    mols, slots = types_ref.shape[0], types_ref.shape[2]
    groups = dl.shape[1]
    width = wo_ref.shape[0]
    @pl.when(s == 0)
    def _():
        mid = middle_ref[...]
        cen = mid - jnp.mean(mid, axis=-1, keepdims=True)
        rstd = lax.rsqrt(jnp.mean(cen*cen, axis=-1, keepdims=True) + EPSILON)
        xhat = cen * rstd
        c = dn2_ref[...]
        small_ref[0:1, :] = jnp.sum(c*xhat, axis=0, keepdims=True)
        small_ref[1:2, :] = jnp.sum(c, axis=0, keepdims=True)
        cot = cot_ref[...]
        small_ref[2:3, :] = jnp.sum(cot, axis=0, keepdims=True)
        e = c * fgain_ref[...]
        dmiddle = cot + rstd * (e - jnp.mean(e, axis=-1, keepdims=True) - xhat * jnp.mean(e*xhat, axis=-1, keepdims=True))
        dmid[...] = dmiddle
        small_ref[3:4, :] = jnp.sum(dmiddle, axis=0, keepdims=True)
        wohi, wolo = split(wo_ref[...])
        dmi_hi, dmi_lo = split(dmiddle)
        dm = dot_nt(dmi_hi, wohi) + (dot_nt(dmi_hi, wolo) + dot_nt(dmi_lo, wohi))
        mhi, mlo = split(jnp.concatenate([mixt_ref[m] for m in range(mols)], 1))
        gwo_ref[...] = dot(mhi, dmi_hi) + (dot(mhi, dmi_lo) + dot(mlo, dmi_hi))
        lane = lax.broadcasted_iota(jnp.int32, (slots, 128), 1)
        rowi = lax.broadcasted_iota(jnp.int32, (slots, slots), 0)
        coli = lax.broadcasted_iota(jnp.int32, (slots, slots), 1)
        energy[...] = jnp.zeros_like(energy)
        for m in range(mols):
            length = len_ref[m]
            maskc[m] = jnp.where(jnp.logical_and(rowi < length, coli < length), 2.0*scale_ref[0], 0.0)
            dmt = jnp.transpose(dm[m*slots:(m+1)*slots]) * linv_ref[m]
            dmhi[m], dmlo[m] = split(dmt)
            prod = dmt * mixt_ref[m]
            delta = jnp.sum(prod.reshape(groups*8, 8, slots), axis=1)
            qhi[m], qlo[m] = split(qt_ref[m])
            khi[m], klo[m] = split(kt_ref[m])
            vhi[m], vlo[m] = split(vt_ref[m])
            for g in range(groups):
                d8 = -delta[g*8:(g+1)*8]
                x = jnp.concatenate([dmt[g*64:(g+1)*64], d8, d8, jnp.zeros((48, slots), F32)], 0)
                y = jnp.transpose(x)
                yhi = y.astype(BF).astype(F32)
                ylo = y - yhi
                dl[m, g, :, 0:128] = jnp.where(lane < 64, yhi, pltpu.roll(ylo, 64, 1)).astype(BF)
                dl[m, g, :, 128:256] = jnp.where(lane < 72, yhi, ylo).astype(BF)
    g = s // mols
    m = s % mols
    lhs = dl[m, g]
    sub = lax.broadcasted_iota(jnp.int32, (16, 128), 0)
    z = jnp.zeros((16, 256), BF)
    zero16 = jnp.zeros((16, 128), BF)
    mc = maskc[m]
    en = energy[...]
    for p in range(4):
        row = pl.multiple_of(g*64 + 16*p, 16)
        rows16 = pl.ds(row, 16)
        def blk(x):
            x = x.astype(F32)
            a = jnp.where(sub < 8, x, 0.0).astype(BF)
            b = jnp.where(sub >= 8, x, 0.0).astype(BF)
            return jnp.concatenate([a, b], axis=1)
        bhi, blo = blk(vhi[m, rows16, :]), blk(vlo[m, rows16, :])
        sel = jnp.concatenate([jnp.where(sub % 8 == 2*p, 1.0, 0.0), jnp.where(sub % 8 == 2*p+1, 1.0, 0.0)], axis=1).astype(BF)
        rows = [bhi if i == p else z for i in range(4)]
        rows += rows
        rows += [blo if i == p else z for i in range(4)]
        rows += [sel, z, z, z]
        dp = dot(lhs, jnp.concatenate(rows, axis=0))
        gs = []
        es = []
        for half in range(2):
            both = e_ref[0, 2*p+half]
            es.append(both)
            e = both[:, 0:128].astype(F32) + both[:, 128:256].astype(F32)
            logits = pair_ref[0, 2*p+half]
            t = logits * mc
            en = en + t * logits
            gp = e * dp[:, half*128:(half+1)*128] + t
            gpair_ref[0, 2*p+half] = gp
            gs.append(split(gp))
        def rows_lhs(hi, lo):
            return jnp.concatenate([jnp.concatenate([hi, hi], 1), jnp.concatenate([lo, zero16], 1)], 0)
        def take(out):
            acc = out[0:16] + out[16:32]
            return jnp.concatenate([acc[0:8, 0:128], acc[8:16, 128:256]], 0)
        ecol = jnp.concatenate([jnp.concatenate([es[0][:, 0:128], es[1][:, 0:128]], 1), jnp.concatenate([es[0][:, 128:256], es[1][:, 128:256]], 1)], 0)
        dvt[m, rows16, :] = take(dot(rows_lhs(dmhi[m, rows16, :], dmlo[m, rows16, :]), ecol))
        gcol = jnp.concatenate([jnp.concatenate([gs[0][0], gs[1][0]], 1), jnp.concatenate([gs[0][1], gs[1][1]], 1)], 0)
        dkt[m, rows16, :] = take(dot(rows_lhs(qhi[m, rows16, :], qlo[m, rows16, :]), gcol))
        grow = jnp.concatenate([jnp.concatenate(gs[0], 1), jnp.concatenate(gs[1], 1)], 0)
        dqt[m, rows16, :] = take(dot_nt(rows_lhs(khi[m, rows16, :], klo[m, rows16, :]), grow)) * (8 ** -0.5)
    energy[...] = en
    @pl.when(s == mols*groups - 1)
    def _():
        first = first_ref[...]
        cen = first - jnp.mean(first, axis=-1, keepdims=True)
        rstd = lax.rsqrt(jnp.mean(cen*cen, axis=-1, keepdims=True) + EPSILON)
        xhat = cen * rstd
        normed = xhat * gain_ref[...] + shift_ref[...]
        nt = jnp.concatenate([jnp.transpose(normed[m*slots:(m+1)*slots]) for m in range(mols)], 1)
        nhi, nlo = split(nt)
        dn = None
        for i, (t_ref, w_ref, g_ref) in enumerate(((dqt, wq_ref, gwq_ref), (dkt, wk_ref, gwk_ref), (dvt, wv_ref, gwv_ref))):
            thi, tlo = split(jnp.concatenate([t_ref[m] for m in range(mols)], 1))
            g_ref[...] = dot_nt(nhi, thi) + (dot_nt(nhi, tlo) + dot_nt(nlo, thi))
            nat = jnp.concatenate([jnp.transpose(t_ref[m]) for m in range(mols)], 0)
            if i == 0:
                small_ref[4:5, :] = jnp.sum(nat, axis=0, keepdims=True)
            if i == 2:
                small_ref[5:6, :] = jnp.sum(nat, axis=0, keepdims=True)
            ahi, alo = split(nat)
            whi, wlo = split(w_ref[...])
            part = dot_nt(ahi, whi) + (dot_nt(ahi, wlo) + dot_nt(alo, whi))
            dn = part if dn is None else dn + part
        small_ref[6:7, :] = jnp.sum(dn*xhat, axis=0, keepdims=True)
        small_ref[7:8, :] = jnp.sum(dn, axis=0, keepdims=True)
        e = dn * gain_ref[...]
        gat = dmid[...] + rstd * (e - jnp.mean(e, axis=-1, keepdims=True) - xhat * jnp.mean(e*xhat, axis=-1, keepdims=True))
        gatoms_ref[...] = gat
        types = gtable_ref.shape[0]
        acc = None
        for m in range(mols):
            one = (lax.broadcasted_iota(jnp.int32, (types, slots), 0) == types_ref[m]).astype(F32).astype(BF)
            for piece in split3(gat[m*slots:(m+1)*slots]):
                part = dot(one, piece)
                acc = part if acc is None else acc + part
        gtable_ref[...] = acc
        small_ref[8:16, :] = jnp.full((8, width), jnp.sum(energy[...]) * scale_ref[1], F32)

def attention_backward(lengths, types, scales, dn2, cot, middle, first, qt, kt, vt, mixt, linv, gain, shift, fgain, wq, wk, wv, wo, pair, e, ntypes):
    mols, slots = types.shape
    rows, width = first.shape
    heads = pair.shape[1]
    groups = heads // 8
    full = lambda shape: pl.BlockSpec(shape, lambda s: (0,)*len(shape))
    vec = lambda v: v.reshape(1, -1)
    blk = lambda w: pl.BlockSpec((1, 8, slots, w), lambda s: (s % mols, s // mols, 0, 0))
    tt = (mols, width, slots)
    in_specs = [pl.BlockSpec(memory_space=pltpu.SMEM), full((mols,1,slots)), pl.BlockSpec(memory_space=pltpu.SMEM)] + [full((rows,width))]*4 + [full(tt)]*5 + \
        [full((1,width))]*3 + [full((width,width))]*4 + [blk(slots), blk(2*slots)]
    outs = [jax.ShapeDtypeStruct(pair.shape, F32), jax.ShapeDtypeStruct((rows,width),F32), jax.ShapeDtypeStruct((ntypes,width),F32)] + [jax.ShapeDtypeStruct((width,width),F32)]*4 + [jax.ShapeDtypeStruct((16,width),F32)]
    out_specs = [blk(slots), full((rows,width)), full((ntypes,width))] + [full((width,width))]*4 + [full((16,width))]
    V = pltpu.VMEM
    return pl.pallas_call(bwd_kernel, out_shape=outs, grid=(mols*groups,), in_specs=in_specs, out_specs=out_specs,
        scratch_shapes=[V((mols,groups,slots,256),BF)] + [V(tt,BF)]*8 + [V(tt,F32)]*3 + [V((mols,slots,slots),F32), V((rows,width),F32), V((slots,slots),F32)],
        compiler_params=pltpu.CompilerParams(vmem_limit_bytes=63*1024*1024, dimension_semantics=("arbitrary",)),
        name="attention_backward",
    )(lengths, types.reshape(mols,1,slots), scales, dn2, cot, middle, first, qt, kt, vt, mixt, linv, vec(gain), vec(shift), vec(fgain), wq, wk, wv, wo, pair, e)

def layer_norm(rows_in, gain, shift):
    centered = rows_in - jnp.mean(rows_in, axis=-1, keepdims=True)
    variance = jnp.mean(centered * centered, axis=-1, keepdims=True)
    return centered * lax.rsqrt(variance + EPSILON) * gain + shift


def gelu_exact(upper):
    return jax.nn.gelu(upper, approximate=False)


HIGH = lax.Precision.HIGH


def local(atom_types, lengths, atom_feats, pair_bias, out_cotangent, type_table, norm_gain, norm_shift, w_query, b_query,
          w_key, w_value, b_value, w_out, b_out, ffn_gain, ffn_shift, w_up, b_up, w_down, b_down):
    both = ("dp", "tensor")
    heads = pair_bias.shape[1]
    length_f = lengths.astype(jnp.float32)
    pair_total = lax.psum(jnp.sum(length_f * length_f), both)
    energy_scale = 1.0 / (heads * pair_total)
    pair_out, e, first, qt, kt, vt, mixt, linv, middle = attention_forward(
        lengths, atom_types, atom_feats, type_table, norm_gain, norm_shift, w_query, b_query, w_key, w_value, b_value, w_out, b_out, pair_bias)
    normed = layer_norm(middle, ffn_gain, ffn_shift)
    gathered = lax.all_gather(normed, "tensor", axis=0, tiled=True)
    cotan_all = lax.all_gather(out_cotangent, "tensor", axis=0, tiled=True)
    upper = jnp.dot(gathered, w_up, precision=HIGH) + b_up
    activated, gelu_back = jax.vjp(gelu_exact, upper)
    down = lax.psum_scatter(jnp.dot(activated, w_down, precision=HIGH), "tensor", scatter_dimension=0, tiled=True)
    atom_out = middle + down + b_down
    grad_w_down = jnp.dot(activated.T, cotan_all, precision=HIGH)
    (d_upper,) = gelu_back(jnp.dot(cotan_all, w_down.T, precision=HIGH))
    grad_w_up = jnp.dot(gathered.T, d_upper, precision=HIGH)
    grad_b_up = jnp.sum(d_upper, axis=0)
    d_normed = lax.psum_scatter(jnp.dot(d_upper, w_up.T, precision=HIGH), "tensor", scatter_dimension=0, tiled=True)
    scales = jnp.stack([energy_scale, 0.5 / energy_scale])
    grad_pair, grad_atoms, g_table, g_query, g_key, g_value, g_out, small = attention_backward(
        lengths, atom_types, scales, d_normed, out_cotangent, middle, first, qt, kt, vt, mixt, linv, norm_gain, norm_shift, ffn_gain,
        w_query, w_key, w_value, w_out, pair_out, e, type_table.shape[0])
    g_table, g_query, g_key, g_value, g_out, small = lax.psum((g_table, g_query, g_key, g_value, g_out, small), both)
    grad_w_up, grad_b_up, grad_w_down = lax.psum((grad_w_up, grad_b_up, grad_w_down), "dp")
    penalty = small[8, 0] * energy_scale
    return (atom_out, pair_out, penalty, grad_atoms, grad_pair, g_table, small[6], small[7], g_query, small[4], g_key, g_value, small[5],
            g_out, small[3], small[0], small[1], grad_w_up, grad_b_up, grad_w_down, small[2])


def solution(mesh):
    in_specs = (
        P(("dp", "tensor"), None),
        P(("dp", "tensor")),
        P(("dp", "tensor"), None),
        P(("dp", "tensor"), None, None, None),
        P(("dp", "tensor"), None),
        P(),
        P(),
        P(),
        P(),
        P(),
        P(),
        P(),
        P(),
        P(),
        P(),
        P(),
        P(),
        P(None, "tensor"),
        P("tensor"),
        P("tensor", None),
        P(),
    )
    out_specs = (
        P(("dp", "tensor"), None),
        P(("dp", "tensor"), None, None, None),
        P(),
        P(("dp", "tensor"), None),
        P(("dp", "tensor"), None, None, None),
        P(),
        P(),
        P(),
        P(),
        P(),
        P(),
        P(),
        P(),
        P(),
        P(),
        P(),
        P(),
        P(None, "tensor"),
        P("tensor"),
        P("tensor", None),
        P(),
    )
    return jax.shard_map(local, mesh=mesh, in_specs=in_specs, out_specs=out_specs, check_vma=False)
```

```python
import functools, math
import jax, jax.numpy as jnp
from jax import lax
from jax.experimental import pallas as pl
from jax.experimental.pallas import tpu as pltpu
from jax.sharding import PartitionSpec as P
F32=jnp.float32; BF=jnp.bfloat16
EPSILON=1e-5

def split(x):
    hi = x.astype(BF)
    lo = (x - hi.astype(F32)).astype(BF)
    return hi, lo

def split3(x):
    hi = x.astype(BF)
    r = x - hi.astype(F32)
    mid = r.astype(BF)
    lo = (r - mid.astype(F32)).astype(BF)
    return hi, mid, lo

def dot(a, b):
    return jnp.dot(a, b, preferred_element_type=F32)

def dot_nt(a, b):
    return lax.dot_general(a, b, (((1,), (1,)), ((), ())), preferred_element_type=F32)

def mm3(a, bhi, blo):
    ahi, alo = split(a)
    return dot(ahi, bhi) + (dot(ahi, blo) + dot(alo, bhi))

def fwd_kernel(len_ref, types_ref, feats_ref, table_ref, gain_ref, shift_ref, wq_ref, bq_ref, wk_ref, wv_ref, bv_ref,
               wo_ref, bo_ref, fgain_ref, fshift_ref, bias_ref,
               pair_ref, e_ref, first_ref, qt_ref, kt_ref, vt_ref, mixt_ref, linv_ref, middle_ref, normed_ref,
               ql, kthi, ktlo, vthi, vtlo, wo_s):
    s = pl.program_id(0)
    mols, slots = types_ref.shape[0], types_ref.shape[2]
    groups = ql.shape[1]
    @pl.when(s == 0)
    def _():
        tab = split3(table_ref[...])
        types = table_ref.shape[0]
        for m in range(mols):
            ids = types_ref[m]
            oneT = (lax.broadcasted_iota(jnp.int32, (slots, slots), 0) == ids).astype(F32)
            one = jnp.transpose(oneT)[:, :types].astype(BF)
            rows = pl.ds(m*slots, slots)
            first = feats_ref[rows, :] + (dot(one, tab[0]) + (dot(one, tab[1]) + dot(one, tab[2])))
            first_ref[rows, :] = first
        first = first_ref[...]
        cen = first - jnp.mean(first, axis=-1, keepdims=True)
        var = jnp.mean(cen*cen, axis=-1, keepdims=True)
        normed = cen * lax.rsqrt(var + EPSILON) * gain_ref[...] + shift_ref[...]
        nhi, nlo = split(normed)
        def proj(w_ref):
            whi, wlo = split(w_ref[...])
            return dot(nhi, whi) + (dot(nhi, wlo) + dot(nlo, whi))
        q = (proj(wq_ref) + bq_ref[...]) * (8 ** -0.5)
        k = proj(wk_ref)
        v = proj(wv_ref) + bv_ref[...]
        lane = lax.broadcasted_iota(jnp.int32, (slots, 128), 1)
        for m in range(mols):
            sl = slice(m*slots, (m+1)*slots)
            qm = q[sl]
            qt_ref[m] = jnp.transpose(qm)
            kt = jnp.transpose(k[sl])
            kt_ref[m] = kt
            kthi[m], ktlo[m] = split(kt)
            vt = jnp.transpose(v[sl])
            vt_ref[m] = vt
            vthi[m], vtlo[m] = split(vt)
            for t in range(groups // 2):
                tile = qm[:, t*128:(t+1)*128]
                rolled = pltpu.roll(tile, 64, 1)
                for half in range(2):
                    dup = jnp.where(lane < 64, tile, rolled) if half == 0 else jnp.where(lane < 64, rolled, tile)
                    hi, lo = split(dup)
                    hi32, lo32 = hi.astype(F32), lo.astype(F32)
                    ql[m, 2*t+half, :, 0:128] = jnp.where(lane < 64, hi32, lo32).astype(BF)
                    ql[m, 2*t+half, :, 128:256] = jnp.where(lane < 64, hi32, 0.0).astype(BF)
    m = s // groups
    g = s % groups
    length = len_ref[m]
    col_live = lax.broadcasted_iota(jnp.int32, (slots, slots), 1) < length
    lhs = ql[m, g]
    sub = lax.broadcasted_iota(jnp.int32, (16, 128), 0)
    zero16 = jnp.zeros((16, 128), BF)
    ones = jnp.ones((16, 256), BF)
    for p in range(4):
        row = pl.multiple_of(g*64 + 16*p, 16)
        khi = kthi[m, pl.ds(row, 16), :].astype(F32)
        klo = ktlo[m, pl.ds(row, 16), :].astype(F32)
        def blk(x):
            a = jnp.where(sub < 8, x, 0.0).astype(BF)
            b = jnp.where(sub >= 8, x, 0.0).astype(BF)
            return jnp.concatenate([a, b], axis=1)
        bhi, blo = blk(khi), blk(klo)
        z = jnp.concatenate([zero16, zero16], axis=1)
        rows = [bhi if i == p else z for i in range(4)]
        rows += rows
        rows += [blo if i == p else z for i in range(4)]
        rows += [z]*4
        rhs = jnp.concatenate(rows, axis=0)
        lg = dot(lhs, rhs)
        ehl = []
        for half in range(2):
            logits = lg[:, half*128:(half+1)*128] + bias_ref[0, 2*p+half].astype(F32)
            pair_ref[0, 2*p+half] = logits
            masked = jnp.where(col_live, logits, -1e30)
            top = jnp.max(masked, axis=1, keepdims=True)
            e = jnp.exp(masked - top)
            hi, lo = split(e)
            both = jnp.concatenate([hi, lo], axis=1)
            e_ref[0, 2*p+half] = both
            ehl.append(both)
        vhi = vthi[m, pl.ds(row, 16), :]
        vlo = vtlo[m, pl.ds(row, 16), :]
        lv = jnp.concatenate([jnp.concatenate([vhi, vhi], 1), jnp.concatenate([vlo, zero16], 1), ones], 0)
        out = dot_nt(lv, jnp.concatenate(ehl, 0))
        acc = out[0:16] + out[16:32]
        sums = out[32:48]
        inv = 1.0 / jnp.concatenate([sums[0:8, 0:128], sums[8:16, 128:256]], 0)
        linv_ref[m, pl.ds(row, 16), :] = inv
        mixt_ref[m, pl.ds(row, 16), :] = jnp.concatenate([acc[0:8, 0:128], acc[8:16, 128:256]], 0) * inv
    @pl.when(s == mols*groups - 1)
    def _():
        mix = jnp.concatenate([jnp.transpose(mixt_ref[m]) for m in range(mols)], 0)
        whi, wlo = split(wo_ref[...])
        mid = first_ref[...] + (mm3(mix, whi, wlo) + bo_ref[...])
        middle_ref[...] = mid
        mcen = mid - jnp.mean(mid, axis=-1, keepdims=True)
        mvar = jnp.mean(mcen*mcen, axis=-1, keepdims=True)
        normed_ref[...] = mcen * lax.rsqrt(mvar + EPSILON) * fgain_ref[...] + fshift_ref[...]

def attention_forward(lengths, types, feats, table, gain, shift, wq, bq, wk, wv, bv, wo, bo, fgain, fshift, bias):
    mols, slots = types.shape
    width = feats.shape[1]
    heads = bias.shape[1]
    groups = heads // 8
    rows = mols*slots
    full = lambda shape: pl.BlockSpec(shape, lambda s: (0,)*len(shape))
    vec = lambda v: v.reshape(1, -1)
    outs = [jax.ShapeDtypeStruct((mols, heads, slots, slots), F32),
            jax.ShapeDtypeStruct((mols, heads, slots, 2*slots), BF),
            jax.ShapeDtypeStruct((rows, width), F32)] + [jax.ShapeDtypeStruct((mols, width, slots), F32)]*5 + [jax.ShapeDtypeStruct((rows, width), F32)]*2
    blk = lambda w: pl.BlockSpec((1, 8, slots, w), lambda s: (s // groups, s % groups, 0, 0))
    in_specs = [pl.BlockSpec(memory_space=pltpu.SMEM), full((mols,1,slots)), full((rows,width)), full(table.shape), full((1,width)), full((1,width)),
                full(wq.shape), full((1,width)), full(wk.shape), full(wv.shape), full((1,width)), full(wo.shape), full((1,width)), full((1,width)), full((1,width)), blk(slots)]
    return pl.pallas_call(fwd_kernel, out_shape=outs, grid=(mols*groups,), in_specs=in_specs,
        out_specs=[blk(slots), blk(2*slots), full((rows,width))] + [full((mols,width,slots))]*5 + [full((rows,width))]*2,
        scratch_shapes=[pltpu.VMEM((mols, groups, slots, 256), BF)] + [pltpu.VMEM((mols,width,slots), BF)]*4 + [pltpu.VMEM((8,128),F32)],
        compiler_params=pltpu.CompilerParams(vmem_limit_bytes=60*1024*1024, dimension_semantics=("arbitrary",)),
        name="attention_forward",
    )(lengths, types.reshape(mols,1,slots), feats, table, vec(gain), vec(shift), wq, vec(bq), wk, wv, vec(bv), wo, vec(bo), vec(fgain), vec(fshift), bias)


MESH_ID = pl.DeviceIdType.MESH


def bit_of(axis, bit):
    return (lax.axis_index(axis) // (1 << bit)) % 2


def partner(axis, bit):
    return {axis: lax.axis_index(axis) + (1 - 2 * bit_of(axis, bit)) * (1 << bit)}


class Exchange:
    def __init__(self, src, dst, sems, slot, stage):
        self.copy = lambda: pltpu.make_async_remote_copy(
            src_ref=src(), dst_ref=dst(), send_sem=sems.at[0, slot], recv_sem=sems.at[1, slot],
            device_id=partner(*stage), device_id_type=MESH_ID)

    def start(self):
        self.copy().start()

    def wait(self):
        self.copy().wait()


class Job:
    def __init__(self, buf, res, recv, sems, first_slot, rows, stages):
        self.slots = 0
        self.recv_rows = 0
        self.steps = []
        plan = []
        length = rows
        for stage in stages:
            halve = (length // 2) % 8 == 0
            part = length // 2 if halve else length
            plan.append((stage, halve, length, part, self.recv_rows))
            self.recv_rows += part
            length = part
        halved = [p[0] for p in plan if p[1]]

        def offset(count):
            off, size = 0, rows
            for axis, bit in halved[:count]:
                size //= 2
                off = off + bit_of(axis, bit) * size
            return off if isinstance(off, int) else pl.multiple_of(off, 8)

        depth = 0
        for stage, halve, length, part, place in plan:
            here = depth
            if halve:
                depth += 1

                def src(stage=stage, here=here, part=part):
                    return buf.at[pl.ds(pl.multiple_of(offset(here) + (1 - bit_of(*stage)) * part, 8), part)]
            else:
                def src(here=here, part=part):
                    return buf.at[pl.ds(offset(here), part)]

            def dst(place=place, part=part):
                return recv.at[pl.ds(place, part)]

            def add(depth=depth, place=place, part=part, to=res if stage == stages[-1] else buf):
                mine = pl.ds(offset(depth), part)
                to[mine, :] = buf[mine, :] + recv[pl.ds(place, part), :]

            self.steps.append((Exchange(src, dst, sems, first_slot + self.slots, stage), add))
            self.slots += 1
        for stage, halve, length, part, place in reversed(plan):
            if not halve:
                continue

            def region(depth=depth, part=part):
                return res.at[pl.ds(offset(depth), part)]

            self.steps.append((Exchange(region, region, sems, first_slot + self.slots, stage), None))
            self.slots += 1
            depth -= 1
        self.ticks = len(self.steps) + 1

    def tick(self, k):
        if k > 0:
            exchange, add = self.steps[k - 1]
            exchange.wait()
            if add is not None:
                add()
        if k < len(self.steps):
            self.steps[k][0].start()


def job_need(rows, stages):
    job = Job(None, None, None, None, 0, rows, stages)
    return job.recv_rows, job.slots


def gelu_and_slope(x):
    cdf = 0.5 + 0.5 * lax.erf(x * (0.5 ** 0.5))
    return x * cdf, cdf + x * (jnp.exp(-0.5 * x * x) * (1.0 / math.sqrt(2.0 * math.pi)))


def mm3_nt(ahi, alo, bhi, blo):
    return dot_nt(ahi, bhi) + (dot_nt(ahi, blo) + dot_nt(alo, bhi))


def mm3_nn(ahi, alo, bhi, blo):
    return dot(ahi, bhi) + (dot(ahi, blo) + dot(alo, bhi))


def main_kernel(plan, *refs):
    refs = list(refs)
    take_n = lambda n: [refs.pop(0) for _ in range(n)]
    len_ref, types_ref, normed2_ref = take_n(3)
    cot_refs = take_n(4)
    middle_ref, first_ref, qt_ref, kt_ref, vt_ref, mixt_ref, linv_ref = take_n(7)
    gain_ref, shift_ref, fgain_ref, bup_ref, bdown_ref = take_n(5)
    wup_any, wdown_any, wq_any, wk_any, wv_any, wo_any, pair_ref, e_ref = take_n(8)
    gpair_ref, atom_out, gatoms_out, small_out, gbup_out, gwup_out, gwdown_out, gwq_out, gwk_out, gwv_out, gwo_out = take_n(11)
    dl, qhi, qlo, khi, klo, vhi, vlo, dmhi, dmlo, dqt, dkt, dvt, maskc, dmid, energy = take_n(15)
    wup, wdown, wq, wk, wv, wo, wuhi, wulo, wdhi, wdlo = take_n(10)
    gath, cots, dact, act, duhi, dulo, pn, rsn, rsd, nt, dn1 = take_n(11)
    pd = dact
    ebuf, eres, erecv, obuf, ores, orecv, fbuf, fres, frecv, sbuf, sres, srecv, tbuf, tres, trecv, bbuf, bres, brecv = take_n(18)
    outv, gatv = take_n(2)
    rsems, lsems = take_n(2)
    assert not refs
    s = pl.program_id(0)
    mols, slots = types_ref.shape[0], types_ref.shape[2]
    groups = dl.shape[1]
    heads = groups * 8
    width = wo.shape[0]
    rows = mols * slots
    last = mols * groups - 1
    core, xbit = ("tensor", 0), ("tensor", 1)
    dpbits = [("dp", i) for i in range(plan["dpbits"])]
    tensor = [core, xbit]
    chunks = plan["chunks"]
    per = groups // chunks
    fcols = per * 64

    slot = [0]

    def new_slots(n):
        slot[0] += n
        return slot[0] - n

    def make(buf, res, recv, nrows, stages):
        job = Job(buf, res, recv, rsems, slot[0], nrows, stages)
        slot[0] += job.slots
        return job

    def swap(src, dst, stage):
        return Exchange(lambda: src, lambda: dst, rsems, new_slots(1), stage)

    n_core = swap(normed2_ref, gath.at[1], core)
    n_x = swap(normed2_ref, gath.at[2], xbit)
    n_diag = swap(gath.at[2], gath.at[3], core)
    dn_core = swap(pn.at[1], rsn.at[0], core)
    dn_diag = swap(pn.at[3], rsn.at[1], core)
    dn_x = swap(pn.at[2], rsn.at[2], xbit)
    dd_core = swap(pd.at[1], rsd.at[0], core)
    dd_diag = swap(pd.at[3], rsd.at[1], core)
    dd_x = swap(pd.at[2], rsd.at[2], xbit)

    total_job = make(tbuf, tres, trecv, 8, tensor + dpbits)
    half = width // 2
    e_jobs = [make(ebuf.at[i], eres.at[i], erecv.at[i], half, dpbits) for i in range(4)]
    b_job = make(bbuf, bres, brecv, 8, dpbits)
    wide = tensor + dpbits
    o_jobs = [make(obuf.at[i], ores.at[i], orecv.at[i], half, wide) for i in range(2)]
    f_jobs = [make(fbuf.at[i], fres.at[i], frecv.at[i], 3 * width, wide) for i in range(chunks)]
    s_job = make(sbuf, sres, srecv, sbuf.shape[0], wide)
    assert slot[0] == plan["slots"], slot[0]

    waiting = {}
    tail = []

    def place(job, start, gap, done=None):
        for k in range(1, job.ticks):
            at = start + int(math.ceil(k * gap))
            fn = functools.partial(job.tick, k)
            fns = [fn] + ([done] if done is not None and k == job.ticks - 1 else [])
            if at <= last:
                waiting.setdefault(at, []).extend(fns)
            else:
                tail.append((at, fns))

    local = []

    def put(src, dst):
        copy = pltpu.make_async_copy(src, dst, lsems.at[10 + len(local)])
        local.append(copy)
        return copy

    def put_e(i):
        out = (gwdown_out, gwdown_out, gwup_out, gwup_out)[i]
        copy = put(eres.at[i], out.at[pl.ds((i % 2) * half, half), :])
        return copy.start

    def put_o(i):
        copy = put(ores.at[i], gwo_out.at[pl.ds(i * half, half), :])
        return copy.start

    def put_f(i):
        copies = [put(fres.at[i, pl.ds(j * width, width), :], out.at[:, pl.ds(i * fcols, fcols)])
                  for j, out in enumerate((gwq_out, gwk_out, gwv_out))]

        def go():
            for copy in copies:
                copy.start()
        return go

    done_e = [put_e(i) for i in range(4)]
    done_o = [put_o(i) for i in range(2)]
    done_f = [put_f(i) for i in range(chunks)]
    put_s = put(sres, small_out)
    put_b = put(bres, gbup_out)
    put_out = put(outv, atom_out)
    put_gat = put(gatv, gatoms_out)

    for i, job in enumerate(e_jobs):
        place(job, plan["e_start"][i], plan["e_gap"], done_e[i])
    place(b_job, 0, 1.0, put_b.start)
    for i, job in enumerate(o_jobs):
        place(job, plan["o_start"][i], plan["o_gap"], done_o[i])
    chunk_end = [(c + 1) * per * mols - 1 for c in range(chunks)]
    for c, job in enumerate(f_jobs):
        place(job, chunk_end[c], plan["f_gap"], done_f[c])

    loads = [(wup_any, wup), (wdown_any, wdown), (wo_any, wo), (wq_any, wq), (wk_any, wk), (wv_any, wv)]
    load = [pltpu.make_async_copy(a, b, lsems.at[i]) for i, (a, b) in enumerate(loads)]

    cot_load = [pltpu.make_async_copy(cot_refs[b], cots.at[b], lsems.at[6 + b]) for b in range(4)]

    @pl.when(s == 0)
    def _():
        barrier = pltpu.get_barrier_semaphore()
        for stage in wide:
            pl.semaphore_signal(barrier, inc=1, device_id=partner(*stage), device_id_type=MESH_ID)
        pl.semaphore_wait(barrier, len(wide))
        n_core.start()
        n_x.start()
        for copy in cot_load + load:
            copy.start()
        square = jnp.zeros((1, 1), F32)
        for m in range(mols):
            f = jnp.full((1, 1), len_ref[m], jnp.int32).astype(F32)
            square = square + f * f
        tbuf[...] = jnp.broadcast_to(square, tbuf.shape)
        total_job.tick(0)
        for copy in cot_load:
            copy.wait()
        gath[0] = normed2_ref[...]
        load[1].wait()
        wdhi[...], wdlo[...] = split(wdown[...])
        load[0].wait()
        wuhi[...], wulo[...] = split(wup[...])
        total_job.tick(1)

        def p1(b, carry):
            hi, lo = split(cots[b])
            dact[b] = mm3_nt(hi, lo, wdhi[...], wdlo[...])
            return carry

        lax.fori_loop(0, 4, p1, 0)
        n_core.wait()
        total_job.tick(2)

        def p2(b):
            hi, lo = split(gath[b])
            upper = mm3_nn(hi, lo, wuhi[...], wulo[...]) + bup_ref[...]
            a, slope = gelu_and_slope(upper)
            act[b] = a
            du = dact[b] * slope
            dhi, dlo = split(du)
            duhi[b] = dhi
            dulo[b] = dlo
            part = jnp.sum(du, axis=0, keepdims=True)
            bbuf[...] = bbuf[...] + jnp.broadcast_to(part, bbuf.shape)
            pn[b] = mm3_nt(dhi, dlo, wuhi[...], wulo[...])

        bbuf[...] = jnp.zeros_like(bbuf)
        def p2_loop(b, carry):
            @pl.when(b == 2)
            def _():
                dn_core.start()
                n_x.wait()
                n_diag.start()
                total_job.tick(3)

            @pl.when(b == 3)
            def _():
                n_diag.wait()
                total_job.tick(4)
            p2(b)
            return carry

        lax.fori_loop(0, 4, p2_loop, 0)
        dn_diag.start()
        b_job.tick(0)
        for k in range(5, total_job.ticks):
            total_job.tick(k)

        def p3a(b, carry):
            ahi, alo = split(jnp.transpose(act[b]))
            chi, clo = split(cots[b])
            for i in range(2):
                part = slice(i * half, (i + 1) * half)
                g = mm3_nn(ahi[part], alo[part], chi, clo)

                @pl.when(b == 0)
                def _():
                    ebuf[i] = g

                @pl.when(b > 0)
                def _():
                    ebuf[i] = ebuf[i] + g
            return carry

        def p3b(b, carry):
            ahi, alo = split(jnp.transpose(gath[b]))
            for i in range(2):
                part = slice(i * half, (i + 1) * half)
                g = mm3_nn(ahi[part], alo[part], duhi[b], dulo[b])

                @pl.when(b == 0)
                def _():
                    ebuf[2 + i] = g

                @pl.when(b > 0)
                def _():
                    ebuf[2 + i] = ebuf[2 + i] + g
            return carry

        def p3c(b, carry):
            hi, lo = split(act[b])
            pd[b] = mm3_nn(hi, lo, wdhi[...], wdlo[...])
            return carry

        dn_diag.wait()
        pn[2] = pn[2] + rsn[1]
        dn_x.start()
        lax.fori_loop(0, 4, p3a, 0)
        e_jobs[0].tick(0)
        e_jobs[1].tick(0)
        lax.fori_loop(0, 4, p3b, 0)
        e_jobs[2].tick(0)
        e_jobs[3].tick(0)
        lax.fori_loop(0, 4, p3c, 0)
        dn_core.wait()
        dn_x.wait()
        dd_core.start()
        dd_diag.start()
        mid = middle_ref[...]
        cen = mid - jnp.mean(mid, axis=-1, keepdims=True)
        rstd = lax.rsqrt(jnp.mean(cen * cen, axis=-1, keepdims=True) + EPSILON)
        xhat = cen * rstd
        c = pn[0] + (rsn[0] + rsn[2])
        types = plan["types"]
        sbuf[...] = jnp.zeros_like(sbuf)

        def small(i, value):
            sbuf[types + i:types + i + 1, :] = value

        small(0, jnp.sum(c * xhat, axis=0, keepdims=True))
        small(1, jnp.sum(c, axis=0, keepdims=True))
        cot = cots[0]
        small(2, jnp.sum(cot, axis=0, keepdims=True))
        ce = c * fgain_ref[...]
        dmiddle = cot + rstd * (ce - jnp.mean(ce, axis=-1, keepdims=True) - xhat * jnp.mean(ce * xhat, axis=-1, keepdims=True))
        dmid[...] = dmiddle
        small(3, jnp.sum(dmiddle, axis=0, keepdims=True))
        dd_diag.wait()
        pd[2] = pd[2] + rsd[1]
        dd_x.start()
        load[2].wait()
        wohi, wolo = split(wo[...])
        dhi, dlo = split(dmiddle)
        dm = mm3_nt(dhi, dlo, wohi, wolo)
        mhi, mlo = split(jnp.concatenate([mixt_ref[m] for m in range(mols)], 1))
        for i in range(2):
            part = slice(i * half, (i + 1) * half)
            obuf[i] = mm3_nn(mhi[part], mlo[part], dhi, dlo)
            o_jobs[i].tick(0)
        lane = lax.broadcasted_iota(jnp.int32, (slots, 128), 1)
        rowi = lax.broadcasted_iota(jnp.int32, (slots, slots), 0)
        coli = lax.broadcasted_iota(jnp.int32, (slots, slots), 1)
        energy[...] = jnp.zeros_like(energy)
        twice = 2.0 / (heads * tres[0:1, 0:slots])
        for m in range(mols):
            length = len_ref[m]
            maskc[m] = jnp.where(jnp.logical_and(rowi < length, coli < length), twice, 0.0)
            dmt = jnp.transpose(dm[m * slots:(m + 1) * slots]) * linv_ref[m]
            dmhi[m], dmlo[m] = split(dmt)
            prod = dmt * mixt_ref[m]
            delta = jnp.sum(prod.reshape(heads, 8, slots), axis=1)
            qhi[m], qlo[m] = split(qt_ref[m])
            khi[m], klo[m] = split(kt_ref[m])
            vhi[m], vlo[m] = split(vt_ref[m])
            for g in range(groups):
                d8 = -delta[g * 8:(g + 1) * 8]
                x = jnp.concatenate([dmt[g * 64:(g + 1) * 64], d8, d8, jnp.zeros((48, slots), F32)], 0)
                y = jnp.transpose(x)
                yhi = y.astype(BF).astype(F32)
                ylo = y - yhi
                dl[m, g, :, 0:128] = jnp.where(lane < 64, yhi, pltpu.roll(ylo, 64, 1)).astype(BF)
                dl[m, g, :, 128:256] = jnp.where(lane < 72, yhi, ylo).astype(BF)
        first = first_ref[...]
        cen = first - jnp.mean(first, axis=-1, keepdims=True)
        rstd = lax.rsqrt(jnp.mean(cen * cen, axis=-1, keepdims=True) + EPSILON)
        normed = cen * rstd * gain_ref[...] + shift_ref[...]
        for m in range(mols):
            nt[:, m * slots:(m + 1) * slots] = jnp.transpose(normed[m * slots:(m + 1) * slots])
        dn1[...] = jnp.zeros_like(dn1)
        for i in (3, 4, 5):
            load[i].wait()

    g = s // mols
    m = s % mols
    lhs = dl[m, g]
    sub = lax.broadcasted_iota(jnp.int32, (16, 128), 0)
    z = jnp.zeros((16, 256), BF)
    zero16 = jnp.zeros((16, 128), BF)
    mc = maskc[m]
    en = energy[...]
    for p in range(4):
        row = pl.multiple_of(g * 64 + 16 * p, 16)
        rows16 = pl.ds(row, 16)

        def blk(x):
            x = x.astype(F32)
            a = jnp.where(sub < 8, x, 0.0).astype(BF)
            b = jnp.where(sub >= 8, x, 0.0).astype(BF)
            return jnp.concatenate([a, b], axis=1)
        bhi, blo = blk(vhi[m, rows16, :]), blk(vlo[m, rows16, :])
        sel = jnp.concatenate([jnp.where(sub % 8 == 2 * p, 1.0, 0.0), jnp.where(sub % 8 == 2 * p + 1, 1.0, 0.0)], axis=1).astype(BF)
        rws = [bhi if i == p else z for i in range(4)]
        rws += rws
        rws += [blo if i == p else z for i in range(4)]
        rws += [sel, z, z, z]
        dp = dot(lhs, jnp.concatenate(rws, axis=0))
        gs = []
        es = []
        for hf in range(2):
            both = e_ref[0, 2 * p + hf]
            es.append(both)
            e = both[:, 0:128].astype(F32) + both[:, 128:256].astype(F32)
            logits = pair_ref[0, 2 * p + hf]
            t = logits * mc
            en = en + t * logits
            gp = e * dp[:, hf * 128:(hf + 1) * 128] + t
            gpair_ref[0, 2 * p + hf] = gp
            gs.append(split(gp))

        def rows_lhs(hi, lo):
            return jnp.concatenate([jnp.concatenate([hi, hi], 1), jnp.concatenate([lo, zero16], 1)], 0)

        def take(out):
            acc = out[0:16] + out[16:32]
            return jnp.concatenate([acc[0:8, 0:128], acc[8:16, 128:256]], 0)
        ecol = jnp.concatenate([jnp.concatenate([es[0][:, 0:128], es[1][:, 0:128]], 1), jnp.concatenate([es[0][:, 128:256], es[1][:, 128:256]], 1)], 0)
        dvt[m, rows16, :] = take(dot(rows_lhs(dmhi[m, rows16, :], dmlo[m, rows16, :]), ecol))
        gcol = jnp.concatenate([jnp.concatenate([gs[0][0], gs[1][0]], 1), jnp.concatenate([gs[0][1], gs[1][1]], 1)], 0)
        dkt[m, rows16, :] = take(dot(rows_lhs(qhi[m, rows16, :], qlo[m, rows16, :]), gcol))
        grow = jnp.concatenate([jnp.concatenate(gs[0], 1), jnp.concatenate(gs[1], 1)], 0)
        dqt[m, rows16, :] = take(dot_nt(rows_lhs(khi[m, rows16, :], klo[m, rows16, :]), grow)) * (8 ** -0.5)
    energy[...] = en

    def chunk_grads(c):
        part = slice(c * fcols, (c + 1) * fcols)
        nhi, nlo = split(nt[...])
        for i, t_ref in enumerate((dqt, dkt, dvt)):
            thi, tlo = split(jnp.concatenate([t_ref[mm, part, :] for mm in range(mols)], 1))
            fbuf[c, i * width:(i + 1) * width, :] = mm3_nt(nhi, nlo, thi, tlo)
        f_jobs[c].tick(0)
        acc = dn1[...]
        for i, (t_ref, w) in enumerate(((dqt, wq), (dkt, wk), (dvt, wv))):
            nat = jnp.concatenate([jnp.transpose(t_ref[mm, part, :]) for mm in range(mols)], 0)
            if i != 1:
                r = plan["types"] + (4 if i == 0 else 5)
                sbuf[r:r + 1, part] = jnp.sum(nat, axis=0, keepdims=True)
            ahi, alo = split(nat)
            whi, wlo = split(w[:, part])
            acc = acc + mm3_nt(ahi, alo, whi, wlo)
        dn1[...] = acc

    for at in sorted(set(waiting) | set(chunk_end)):
        def body(at=at):
            for fn in waiting.get(at, []):
                fn()
            if at in chunk_end:
                chunk_grads(chunk_end.index(at))
        pl.when(s == at)(body)

    @pl.when(s == last)
    def _():
        types = plan["types"]
        first = first_ref[...]
        cen = first - jnp.mean(first, axis=-1, keepdims=True)
        rstd = lax.rsqrt(jnp.mean(cen * cen, axis=-1, keepdims=True) + EPSILON)
        xhat = cen * rstd
        dn = dn1[...]
        sbuf[types + 6:types + 7, :] = jnp.sum(dn * xhat, axis=0, keepdims=True)
        sbuf[types + 7:types + 8, :] = jnp.sum(dn, axis=0, keepdims=True)
        ge = dn * gain_ref[...]
        gat = dmid[...] + rstd * (ge - jnp.mean(ge, axis=-1, keepdims=True) - xhat * jnp.mean(ge * xhat, axis=-1, keepdims=True))
        gatv[...] = gat
        put_gat.start()
        acc = None
        for mm in range(mols):
            one = (lax.broadcasted_iota(jnp.int32, (types, slots), 0) == types_ref[mm]).astype(F32).astype(BF)
            for piece in split3(gat[mm * slots:(mm + 1) * slots]):
                part = dot(one, piece)
                acc = part if acc is None else acc + part
        sbuf[0:types, :] = acc
        total = jnp.sum(jnp.sum(energy[...], axis=0, keepdims=True), axis=1, keepdims=True) * 0.5
        sbuf[types + 8:types + 9, :] = jnp.broadcast_to(total, (1, width))
        s_job.tick(0)
        place(s_job, last, plan["f_gap"], put_s.start)
        order = sorted(range(len(tail)), key=lambda i: tail[i][0])
        rest = [tail[i][1] for i in order]
        for i, fns in enumerate(rest):
            for fn in fns:
                fn()
            if i == len(rest) // 2:
                dd_core.wait()
                dd_x.wait()
                outv[...] = middle_ref[...] + bdown_ref[...] + (pd[0] + (rsd[0] + rsd[2]))
                put_out.start()
        for copy in local:
            copy.wait()


def main_call(mesh, lengths, types, normed2, cots, middle, first, qt, kt, vt, mixt, linv, gain, shift, fgain, bup, bdown,
              wup, wdown, wq, wk, wv, wo, pair, e, ntypes):
    mols, slots = types.shape
    rows, width = first.shape
    heads = pair.shape[1]
    groups = heads // 8
    hidden = wup.shape[1]
    dp = mesh.shape["dp"]
    dpbits = dp.bit_length() - 1
    assert (1 << dpbits) == dp and mesh.shape["tensor"] == 4
    chunks = 4 if dpbits <= 4 else 1
    fcols = width // chunks
    stages = [("tensor", 0), ("tensor", 1)] + [("dp", i) for i in range(dpbits)]
    small = -(-(ntypes + 9) // 64) * 64
    half = width // 2
    t_need = job_need(8, stages)
    e_need = job_need(half, stages[2:])
    b_need = job_need(8, stages[2:])
    o_need = job_need(half, stages)
    f_need = job_need(3 * width, stages)
    s_need = job_need(small, stages)
    nslots = 9 + t_need[1] + 4 * e_need[1] + b_need[1] + 2 * o_need[1] + chunks * f_need[1] + s_need[1]
    plan = dict(dpbits=dpbits, chunks=chunks, types=ntypes, slots=nslots,
                e_start=[-1, 0, 1, 2], e_gap=2.0, o_start=[1, 2], o_gap=1.5, f_gap=1.5)
    nlocal = 10 + 4 + 2 + 3 * chunks + 4
    V = pltpu.VMEM
    one = lambda shape: pl.BlockSpec(shape, lambda s: (0,) * len(shape), pipeline_mode=pl.Buffered(1))
    any_ = pl.BlockSpec(memory_space=pl.ANY)
    smem = pl.BlockSpec(memory_space=pltpu.SMEM)
    vec = lambda v: v.reshape(1, -1)
    blk = lambda w: pl.BlockSpec((1, 8, slots, w), lambda s: (s % mols, s // mols, 0, 0))
    tt = (mols, width, slots)
    rw = (rows, width)
    in_specs = [smem, one((mols, 1, slots)), one(rw)] + [any_] * 4 + [one(rw)] * 2 + [one(tt)] * 5 + \
        [one((1, width))] * 3 + [one((1, hidden)), one((1, width))] + [any_] * 6 + [blk(slots), blk(2 * slots)]
    S = jax.ShapeDtypeStruct
    ww = (width, width)
    outs = [S(pair.shape, F32), S(rw, F32), S(rw, F32), S((small, width), F32), S((8, hidden), F32), S((width, hidden), F32), S((hidden, width), F32)] + [S(ww, F32)] * 4
    out_specs = [blk(slots)] + [any_] * 10
    four = (4, rows, width)
    scratch = [V((mols, groups, slots, 256), BF)] + [V(tt, BF)] * 8 + [V(tt, F32)] * 3 + [V((mols, slots, slots), F32), V(rw, F32), V((slots, slots), F32)]
    scratch += [V((width, hidden), F32), V((hidden, width), F32)] + [V(ww, F32)] * 4 + [V((width, hidden), BF)] * 2 + [V((hidden, width), BF)] * 2
    scratch += [V(four, F32)] * 4 + [V(four, BF)] * 2 + [V(four, F32)] + [V((3, rows, width), F32)] * 2 + [V((width, rows), F32), V(rw, F32)]
    scratch += [V((4, half, width), F32)] * 2 + [V((4, e_need[0], width), F32)] + [V((2, half, width), F32)] * 2 + [V((2, o_need[0], width), F32)]
    scratch += [V((chunks, 3 * width, fcols), F32)] * 2 + [V((chunks, f_need[0], fcols), F32)] + [V((small, width), F32)] * 2 + [V((s_need[0], width), F32)]
    scratch += [V((8, 128), F32)] * 2 + [V((t_need[0], 128), F32)] + [V((8, hidden), F32)] * 2 + [V((b_need[0], hidden), F32)]
    scratch += [V(rw, F32)] * 2
    scratch += [pltpu.SemaphoreType.DMA((2, nslots)), pltpu.SemaphoreType.DMA((nlocal,))]
    return pl.pallas_call(functools.partial(main_kernel, plan), out_shape=outs, grid=(mols * groups,), in_specs=in_specs, out_specs=out_specs,
        scratch_shapes=scratch,
        compiler_params=pltpu.CompilerParams(vmem_limit_bytes=67043328, dimension_semantics=("arbitrary",), collective_id=0, has_side_effects=True),
        name="feed_forward_and_backward",
    )(lengths, types.reshape(mols, 1, slots), normed2, *cots, middle, first, qt, kt, vt, mixt, linv, vec(gain), vec(shift), vec(fgain), vec(bup), vec(bdown),
      wup, wdown, wq, wk, wv, wo, pair, e)


def flip(index, n, mask):
    return [(i, i ^ mask) for i in range(n)]


def local(mesh, atom_types, lengths, atom_feats, pair_bias, out_cotangent, type_table, norm_gain, norm_shift, w_query, b_query,
          w_key, w_value, b_value, w_out, b_out, ffn_gain, ffn_shift, w_up, b_up, w_down, b_down):
    tensor = mesh.shape["tensor"]
    cots = [out_cotangent] + [lax.ppermute(out_cotangent, "tensor", [(i, i ^ d) for i in range(tensor)]) for d in (1, 2, 3)]
    pair_out, e, first, qt, kt, vt, mixt, linv, middle, normed2 = attention_forward(
        lengths, atom_types, atom_feats, type_table, norm_gain, norm_shift, w_query, b_query, w_key, w_value, b_value, w_out, b_out,
        ffn_gain, ffn_shift, pair_bias)
    types = type_table.shape[0]
    grad_pair, atom_out, grad_atoms, small, gbup, gwup, gwdown, gwq, gwk, gwv, gwo = main_call(
        mesh, lengths, atom_types, normed2, cots, middle, first, qt, kt, vt, mixt, linv, norm_gain, norm_shift, ffn_gain, b_up, b_down,
        w_up, w_down, w_query, w_key, w_value, w_out, pair_out, e, types)
    row = lambda i: small[types + i]
    return (atom_out, pair_out, small[types + 8, 0], grad_atoms, grad_pair, small[:types], row(6), row(7), gwq, row(4), gwk, gwv, row(5),
            gwo, row(3), row(0), row(1), gwup, gbup[0], gwdown, row(2))


def solution(mesh):
    in_specs = (
        P(("dp", "tensor"), None),
        P(("dp", "tensor")),
        P(("dp", "tensor"), None),
        P(("dp", "tensor"), None, None, None),
        P(("dp", "tensor"), None),
        P(),
        P(),
        P(),
        P(),
        P(),
        P(),
        P(),
        P(),
        P(),
        P(),
        P(),
        P(),
        P(None, "tensor"),
        P("tensor"),
        P("tensor", None),
        P(),
    )
    out_specs = (
        P(("dp", "tensor"), None),
        P(("dp", "tensor"), None, None, None),
        P(),
        P(("dp", "tensor"), None),
        P(("dp", "tensor"), None, None, None),
        P(),
        P(),
        P(),
        P(),
        P(),
        P(),
        P(),
        P(),
        P(),
        P(),
        P(),
        P(),
        P(None, "tensor"),
        P("tensor"),
        P("tensor", None),
        P(),
    )
    return jax.shard_map(functools.partial(local, mesh), mesh=mesh, in_specs=in_specs, out_specs=out_specs, check_vma=False)
```

```python
import functools, math
import jax, jax.numpy as jnp
from jax import lax
from jax.experimental import pallas as pl
from jax.experimental.pallas import tpu as pltpu
from jax.sharding import PartitionSpec as P
F32=jnp.float32; BF=jnp.bfloat16
EPSILON=1e-5

def split(x):
    hi = x.astype(BF)
    lo = (x - hi.astype(F32)).astype(BF)
    return hi, lo

def split3(x):
    hi = x.astype(BF)
    r = x - hi.astype(F32)
    mid = r.astype(BF)
    lo = (r - mid.astype(F32)).astype(BF)
    return hi, mid, lo

def dot(a, b):
    return jnp.dot(a, b, preferred_element_type=F32)

def dot_nt(a, b):
    return lax.dot_general(a, b, (((1,), (1,)), ((), ())), preferred_element_type=F32)

def mm3(a, bhi, blo):
    ahi, alo = split(a)
    return dot(ahi, bhi) + (dot(ahi, blo) + dot(alo, bhi))

def fwd_kernel(len_ref, types_ref, feats_ref, table_ref, gain_ref, shift_ref, wq_ref, bq_ref, wk_ref, wv_ref, bv_ref,
               wo_ref, bo_ref, fgain_ref, fshift_ref, bias_ref,
               pair_ref, e_ref, first_ref, qt_ref, kt_ref, vt_ref, mixt_ref, linv_ref, middle_ref, normed_ref,
               ql, kthi, ktlo, vthi, vtlo, wo_s):
    s = pl.program_id(0)
    mols, slots = types_ref.shape[0], types_ref.shape[2]
    groups = ql.shape[1]
    @pl.when(s == 0)
    def _():
        tab = split3(table_ref[...])
        types = table_ref.shape[0]
        for m in range(mols):
            ids = types_ref[m]
            oneT = (lax.broadcasted_iota(jnp.int32, (slots, slots), 0) == ids).astype(F32)
            one = jnp.transpose(oneT)[:, :types].astype(BF)
            rows = pl.ds(m*slots, slots)
            first = feats_ref[rows, :] + (dot(one, tab[0]) + (dot(one, tab[1]) + dot(one, tab[2])))
            first_ref[rows, :] = first
        first = first_ref[...]
        cen = first - jnp.mean(first, axis=-1, keepdims=True)
        var = jnp.mean(cen*cen, axis=-1, keepdims=True)
        normed = cen * lax.rsqrt(var + EPSILON) * gain_ref[...] + shift_ref[...]
        nhi, nlo = split(normed)
        def proj(w_ref):
            whi, wlo = split(w_ref[...])
            return dot(nhi, whi) + (dot(nhi, wlo) + dot(nlo, whi))
        q = (proj(wq_ref) + bq_ref[...]) * (8 ** -0.5)
        k = proj(wk_ref)
        v = proj(wv_ref) + bv_ref[...]
        lane = lax.broadcasted_iota(jnp.int32, (slots, 128), 1)
        for m in range(mols):
            sl = slice(m*slots, (m+1)*slots)
            qm = q[sl]
            qt_ref[m] = jnp.transpose(qm)
            kt = jnp.transpose(k[sl])
            kt_ref[m] = kt
            kthi[m], ktlo[m] = split(kt)
            vt = jnp.transpose(v[sl])
            vt_ref[m] = vt
            vthi[m], vtlo[m] = split(vt)
            for t in range(groups // 2):
                tile = qm[:, t*128:(t+1)*128]
                rolled = pltpu.roll(tile, 64, 1)
                for half in range(2):
                    dup = jnp.where(lane < 64, tile, rolled) if half == 0 else jnp.where(lane < 64, rolled, tile)
                    hi, lo = split(dup)
                    hi32, lo32 = hi.astype(F32), lo.astype(F32)
                    ql[m, 2*t+half, :, 0:128] = jnp.where(lane < 64, hi32, lo32).astype(BF)
                    ql[m, 2*t+half, :, 128:256] = jnp.where(lane < 64, hi32, 0.0).astype(BF)
    m = s // groups
    g = s % groups
    length = len_ref[m]
    col_live = lax.broadcasted_iota(jnp.int32, (slots, slots), 1) < length
    lhs = ql[m, g]
    sub = lax.broadcasted_iota(jnp.int32, (16, 128), 0)
    zero16 = jnp.zeros((16, 128), BF)
    ones = jnp.ones((16, 256), BF)
    for p in range(4):
        row = pl.multiple_of(g*64 + 16*p, 16)
        khi = kthi[m, pl.ds(row, 16), :].astype(F32)
        klo = ktlo[m, pl.ds(row, 16), :].astype(F32)
        def blk(x):
            a = jnp.where(sub < 8, x, 0.0).astype(BF)
            b = jnp.where(sub >= 8, x, 0.0).astype(BF)
            return jnp.concatenate([a, b], axis=1)
        bhi, blo = blk(khi), blk(klo)
        z = jnp.concatenate([zero16, zero16], axis=1)
        rows = [bhi if i == p else z for i in range(4)]
        rows += rows
        rows += [blo if i == p else z for i in range(4)]
        rows += [z]*4
        rhs = jnp.concatenate(rows, axis=0)
        lg = dot(lhs, rhs)
        ehl = []
        for half in range(2):
            logits = lg[:, half*128:(half+1)*128] + bias_ref[0, 2*p+half].astype(F32)
            pair_ref[0, 2*p+half] = logits
            masked = jnp.where(col_live, logits, -1e30)
            top = jnp.max(masked, axis=1, keepdims=True)
            e = jnp.exp(masked - top)
            hi, lo = split(e)
            both = jnp.concatenate([hi, lo], axis=1)
            e_ref[0, 2*p+half] = both
            ehl.append(both)
        vhi = vthi[m, pl.ds(row, 16), :]
        vlo = vtlo[m, pl.ds(row, 16), :]
        lv = jnp.concatenate([jnp.concatenate([vhi, vhi], 1), jnp.concatenate([vlo, zero16], 1), ones], 0)
        out = dot_nt(lv, jnp.concatenate(ehl, 0))
        acc = out[0:16] + out[16:32]
        sums = out[32:48]
        inv = 1.0 / jnp.concatenate([sums[0:8, 0:128], sums[8:16, 128:256]], 0)
        linv_ref[m, pl.ds(row, 16), :] = inv
        mixt_ref[m, pl.ds(row, 16), :] = jnp.concatenate([acc[0:8, 0:128], acc[8:16, 128:256]], 0) * inv
    @pl.when(s == mols*groups - 1)
    def _():
        mix = jnp.concatenate([jnp.transpose(mixt_ref[m]) for m in range(mols)], 0)
        whi, wlo = split(wo_ref[...])
        mid = first_ref[...] + (mm3(mix, whi, wlo) + bo_ref[...])
        middle_ref[...] = mid
        mcen = mid - jnp.mean(mid, axis=-1, keepdims=True)
        mvar = jnp.mean(mcen*mcen, axis=-1, keepdims=True)
        normed_ref[...] = mcen * lax.rsqrt(mvar + EPSILON) * fgain_ref[...] + fshift_ref[...]

def attention_forward(lengths, types, feats, table, gain, shift, wq, bq, wk, wv, bv, wo, bo, fgain, fshift, bias):
    mols, slots = types.shape
    width = feats.shape[1]
    heads = bias.shape[1]
    groups = heads // 8
    rows = mols*slots
    full = lambda shape: pl.BlockSpec(shape, lambda s: (0,)*len(shape))
    vec = lambda v: v.reshape(1, -1)
    outs = [jax.ShapeDtypeStruct((mols, heads, slots, slots), F32),
            jax.ShapeDtypeStruct((mols, heads, slots, 2*slots), BF),
            jax.ShapeDtypeStruct((rows, width), F32)] + [jax.ShapeDtypeStruct((mols, width, slots), F32)]*5 + [jax.ShapeDtypeStruct((rows, width), F32)]*2
    blk = lambda w: pl.BlockSpec((1, 8, slots, w), lambda s: (s // groups, s % groups, 0, 0))
    in_specs = [pl.BlockSpec(memory_space=pltpu.SMEM), full((mols,1,slots)), full((rows,width)), full(table.shape), full((1,width)), full((1,width)),
                full(wq.shape), full((1,width)), full(wk.shape), full(wv.shape), full((1,width)), full(wo.shape), full((1,width)), full((1,width)), full((1,width)), blk(slots)]
    return pl.pallas_call(fwd_kernel, out_shape=outs, grid=(mols*groups,), in_specs=in_specs,
        out_specs=[blk(slots), blk(2*slots), full((rows,width))] + [full((mols,width,slots))]*5 + [full((rows,width))]*2,
        scratch_shapes=[pltpu.VMEM((mols, groups, slots, 256), BF)] + [pltpu.VMEM((mols,width,slots), BF)]*4 + [pltpu.VMEM((8,128),F32)],
        compiler_params=pltpu.CompilerParams(vmem_limit_bytes=60*1024*1024, dimension_semantics=("arbitrary",)),
        name="attention_forward",
    )(lengths, types.reshape(mols,1,slots), feats, table, vec(gain), vec(shift), wq, vec(bq), wk, wv, vec(bv), wo, vec(bo), vec(fgain), vec(fshift), bias)


MESH_ID = pl.DeviceIdType.MESH


def bit_of(axis, bit):
    return (lax.axis_index(axis) // (1 << bit)) % 2


def partner(axis, bit):
    return {axis: lax.axis_index(axis) + (1 - 2 * bit_of(axis, bit)) * (1 << bit)}


class Exchange:
    def __init__(self, src, dst, sems, slot, stage, before=None, after=None):
        self.before, self.after = before, after
        self.copy = lambda: pltpu.make_async_remote_copy(
            src_ref=src(), dst_ref=dst(), send_sem=sems.at[0, slot], recv_sem=sems.at[1, slot],
            device_id=partner(*stage), device_id_type=MESH_ID)

    def start(self):
        if self.before is not None:
            self.before()
        self.copy().start()

    def wait(self):
        self.copy().wait()
        if self.after is not None:
            self.after()


class Job:
    def __init__(self, buf, recv, sems, free, first_slot, rows, stages, done=None):
        self.done = done
        self.slots = 0
        self.recv_rows = 0
        self.steps = []
        plan = []
        numbers = []
        length = rows
        for stage in stages:
            halve = (length // 2) % 8 == 0
            part = length // 2 if halve else length
            plan.append((stage, halve, length, part, self.recv_rows))
            self.recv_rows += part
            length = part
        halved = [p[0] for p in plan if p[1]]

        def offset(count):
            off, size = 0, rows
            for axis, bit in halved[:count]:
                size //= 2
                off = off + bit_of(axis, bit) * size
            return off if isinstance(off, int) else pl.multiple_of(off, 8)

        depth = 0
        for stage, halve, length, part, place in plan:
            here = depth
            if halve:
                depth += 1

                def src(stage=stage, here=here, part=part):
                    return buf.at[pl.ds(pl.multiple_of(offset(here) + (1 - bit_of(*stage)) * part, 8), part)]
            else:
                def src(here=here, part=part):
                    return buf.at[pl.ds(offset(here), part)]

            def dst(place=place, part=part):
                return recv.at[pl.ds(place, part)]

            def add(depth=depth, place=place, part=part, to=buf):
                mine = pl.ds(offset(depth), part)
                to[mine, :] = buf[mine, :] + recv[pl.ds(place, part), :]

            number = first_slot + self.slots

            def tell(number=number, stage=stage):
                pl.semaphore_signal(free.at[number], inc=1, device_id=partner(*stage), device_id_type=MESH_ID)

            self.steps.append((Exchange(src, dst, sems, number, stage, after=tell if halve else None), add))
            numbers.append(number)
            self.slots += 1
        for (stage, halve, length, part, place), number in zip(reversed(plan), reversed(numbers)):
            if not halve:
                continue

            def freed(number=number):
                pl.semaphore_wait(free.at[number], 1)

            def region(depth=depth, part=part):
                return buf.at[pl.ds(offset(depth), part)]

            self.steps.append((Exchange(region, region, sems, first_slot + self.slots, stage, before=freed), None))
            self.slots += 1
            depth -= 1
        self.ticks = len(self.steps) + 1

    def tick(self, k):
        if k > 0:
            exchange, add = self.steps[k - 1]
            exchange.wait()
            if add is not None:
                add()
        if k < len(self.steps):
            self.steps[k][0].start()
        elif self.done is not None:
            self.done()


def job_need(rows, stages):
    job = Job(None, None, None, None, 0, rows, stages)
    return job.recv_rows, job.slots


ORDERS = ("CXYZW", "CXZWY", "CYXZW", "CYZWX", "CZWXY", "CXZYW", "CZXYW", "CZYXW")
E_ORDERS = ("YZW", "ZWY", "ZYW")


def stages_of(order, dpbits):
    table = {"C": [("tensor", 0)], "X": [("tensor", 1)], "Y": [("dp", i) for i in range(dpbits - 2)],
             "Z": [("dp", dpbits - 2)], "W": [("dp", dpbits - 1)]}
    return [stage for token in order for stage in table[token]]


def stage_cost(stage, size):
    rate = 43.0e3
    axis, bit = stage
    if axis == "tensor":
        return ([("core", size / 700e3)], 0.9) if bit == 0 else ([("x", size / rate)], 2.0)
    if bit == 0:
        return [("y", size / rate)], 2.0
    if bit == 1:
        return [("outer", size / rate)], 2.0
    return [("outer", size / rate), ("inner", 2 * size / rate)], 2.5


def tick_order(segments, jobs):
    now, free, flying, points, current = 0.0, {}, [], [], []
    segments = list(segments)

    def start(name, k):
        stage, size, _ = jobs[name][k]
        links, latency = stage_cost(stage, size)
        begin = max([now] + [free.get(link, 0.0) for link, _ in links])
        for link, length in links:
            free[link] = begin + length
        flying.append((begin + max(length for _, length in links) + latency, name, k))

    while segments or flying:
        ready = [f for f in flying if f[0] <= now]
        if ready:
            first = min(ready)
            flying.remove(first)
            _, name, k = first
            now += 0.05 + (jobs[name][k][1] / 1.5e6 if jobs[name][k][2] else 0.0)
            current.append((name, k + 1))
            if k + 1 < len(jobs[name]):
                start(name, k + 1)
        elif segments:
            points.append(current)
            current = []
            _, length, released = segments.pop(0)
            now += length
            for name in released:
                start(name, 0)
        else:
            now = min(f[0] for f in flying)
    points.append(current)
    return points[1:]


def job_steps(rows, width, stages):
    length, out, back = rows, [], []
    for stage in stages:
        halve = (length // 2) % 8 == 0
        length = length // 2 if halve else length
        out.append((stage, length * width * 4, True))
        if halve:
            back.append((stage, length * width * 4, False))
    return out + back[::-1]


def make_plan(config, dpbits, mols, groups, width, hidden, small):
    ne, ch, fs, no = config["ne"], config["ch"], config["fs"], config["no"]
    jobs, steps = {}, {}

    def add(name, kind, index, first, rows, stages, cols):
        jobs[name] = (kind, index, first, rows, stages)
        steps[name] = job_steps(rows, cols, stages)

    for i in range(ne):
        n = (width + hidden) // ne
        add("e%d" % i, "e", 0, i * n, n, stages_of(E_ORDERS[config["eo"][i]], dpbits), width)
    for i in range(no):
        n = width // no
        add("o%d" % i, "o", 0, i * n, n, stages_of(ORDERS[config["oo"][i]], dpbits), width)
    for c in range(ch):
        for h in range(fs):
            n = 3 * width // fs
            add("f%d_%d" % (c, h), "f", c, h * n, n, stages_of(ORDERS[config["fo"][c * fs + h]], dpbits), width // ch)
    add("s", "s", 0, 0, small, stages_of(ORDERS[config["so"]], dpbits), width)
    add("b", "b", 0, 0, 8, stages_of("YZW", dpbits), hidden)
    q = ne // 4
    pos = config["pos"]
    segments = []

    def put(at):
        for k in range(4):
            if pos[k] == at:
                segments.append((("e", k), 1.6, ["e%d" % i for i in range(k * q, (k + 1) * q)]))
        if pos[4] == at:
            segments.append((("down",), 3.2, []))

    segments.append((("ffn",), 0.0, ["b"]))
    put(-2)
    segments.append((("pro1",), 4.0, ["o%d" % i for i in range(no)]))
    segments.append((("pro2",), 6.0, []))
    put(-1)
    per = groups // ch
    for s in range(mols * groups):
        segments.append((("step", s), 1.35, []))
        if (s + 1) % (per * mols) == 0:
            c = s // (per * mols)
            segments.append((("chunk", c), 4.0 / ch, ["f%d_%d" % (c, h) for h in range(fs)]))
        put(s)
    segments.append((("end",), 2.0, ["s"]))
    put(16)
    return jobs, segments, tick_order(segments, steps)


def gelu_and_slope(x):
    cdf = 0.5 + 0.5 * lax.erf(x * (0.5 ** 0.5))
    return x * cdf, cdf + x * (jnp.exp(-0.5 * x * x) * (1.0 / math.sqrt(2.0 * math.pi)))


def mm3_nt(ahi, alo, bhi, blo):
    return dot_nt(ahi, bhi) + (dot_nt(ahi, blo) + dot_nt(alo, bhi))


def mm3_nn(ahi, alo, bhi, blo):
    return dot(ahi, bhi) + (dot(ahi, blo) + dot(alo, bhi))


def main_kernel(plan, *refs):
    refs = list(refs)
    take_n = lambda n: [refs.pop(0) for _ in range(n)]
    len_ref, types_ref, normed2_ref = take_n(3)
    cot_refs = take_n(4)
    middle_ref, first_ref, qt_ref, kt_ref, vt_ref, mixt_ref, linv_ref = take_n(7)
    gain_ref, shift_ref, fgain_ref, bup_ref, bdown_ref = take_n(5)
    wup_any, wdown_any, wq_any, wk_any, wv_any, wo_any, pair_ref, e_ref = take_n(8)
    gpair, outv, gatv, eres, ores, fres, sres, bres = take_n(8)
    dl, qhi, qlo, khi, klo, vhi, vlo, dmhi, dmlo, dqt, dkt, dvt, maskc, dmid, energy = take_n(15)
    wq, wk, wv, wo, wuhi, wulo, wdhi, wdlo = take_n(8)
    gath, cots, duhi, dulo, pn, pd, rsn, rsd, nt, dn1 = take_n(10)
    ebuf, erecv, obuf, orecv, fbuf, frecv, sbuf, srecv, tbuf, tres, trecv, bbuf, brecv = take_n(13)
    rsems, free, lsems = take_n(3)
    assert not refs
    s = pl.program_id(0)
    mols, slots = types_ref.shape[0], types_ref.shape[2]
    groups = dl.shape[1]
    heads = groups * 8
    width = wo.shape[0]
    hidden = wuhi.shape[1]
    rows = mols * slots
    types = plan["types"]
    last = mols * groups - 1
    core, xbit = ("tensor", 0), ("tensor", 1)
    dpbits = [("dp", i) for i in range(plan["dpbits"])]
    wide = [core, xbit] + dpbits
    jobs, segments, points = plan["jobs"], plan["segments"], plan["points"]
    chunks = plan["chunks"]
    fcols = width // chunks

    tiles = [(r, c) for r in range(rows // 128) for c in range(hidden // 128)]

    def keep(base, b, x):
        for i, (r, c) in enumerate(tiles):
            gpair[0, base + b * len(tiles) + i] = x[r * 128:(r + 1) * 128, c * 128:(c + 1) * 128]

    def kept(base, b):
        across = hidden // 128
        parts = [gpair[0, base + b * len(tiles) + i] for i in range(len(tiles))]
        return jnp.concatenate([jnp.concatenate(parts[r * across:(r + 1) * across], 1) for r in range(rows // 128)], 0)

    ACT, DACT = 0, 4 * len(tiles)
    slot = [0]

    def swap(src, dst, stage):
        slot[0] += 1
        return Exchange(lambda: src, lambda: dst, rsems, slot[0] - 1, stage)

    n_core = swap(normed2_ref, gath.at[1], core)
    n_x = swap(normed2_ref, gath.at[2], xbit)
    n_diag = swap(gath.at[2], gath.at[3], core)
    dn_core = swap(pn.at[1], rsn.at[0], core)
    dn_diag = swap(pn.at[3], rsn.at[1], core)
    dn_x = swap(pn.at[2], rsn.at[2], xbit)
    dd_core = swap(pd.at[1], rsd.at[0], core)
    dd_diag = swap(pd.at[3], rsd.at[1], core)
    dd_x = swap(pd.at[2], rsd.at[2], xbit)

    def make(buf, res, recv, nrows, stages):
        def done():
            res[...] = buf[...]
        job = Job(buf, recv, rsems, free, slot[0], nrows, stages, done)
        slot[0] += job.slots
        return job

    total_job = make(tbuf, tres, trecv, 8, wide)
    running = {}
    place = {"e": 0, "o": 0, "f": 0}
    for name, (kind, index, first_row, nrows, stages) in jobs.items():
        if kind == "s":
            running[name] = make(sbuf, sres, srecv, nrows, stages)
        elif kind == "b":
            running[name] = make(bbuf, bres, brecv, nrows, stages)
        else:
            need = job_need(nrows, stages)[0]
            if kind == "f":
                buf, res, recv = fbuf.at[index], fres.at[index], frecv
            else:
                buf, res, recv = {"e": (ebuf, eres, erecv), "o": (obuf, ores, orecv)}[kind]
            running[name] = make(buf.at[pl.ds(first_row, nrows)], res.at[pl.ds(first_row, nrows)], recv.at[pl.ds(place[kind], need)], nrows, stages)
            place[kind] += need
    assert slot[0] == plan["slots"], slot[0]
    half = width // 2

    cot_load = [pltpu.make_async_copy(cot_refs[b], cots.at[b], lsems.at[b]) for b in range(4)]
    piece = width // rows
    up_load = [pltpu.make_async_copy(wup_any.at[pl.ds(i * rows, rows)], pn.at[i], lsems.at[4 + i]) for i in range(piece)]
    down_load = [pltpu.make_async_copy(wdown_any.at[pl.ds(i * rows, rows)], pn.at[2 + i], lsems.at[6 + i]) for i in range(piece)]
    load = [pltpu.make_async_copy(a, b, lsems.at[8 + i]) for i, (a, b) in enumerate(((wo_any, wo), (wq_any, wq), (wk_any, wk), (wv_any, wv)))]

    def seg_ffn():
        barrier = pltpu.get_barrier_semaphore()
        for stage in wide:
            pl.semaphore_signal(barrier, inc=1, device_id=partner(*stage), device_id_type=MESH_ID)
        pl.semaphore_wait(barrier, len(wide))
        n_x.start()
        n_core.start()
        for copy in down_load + cot_load + up_load + load:
            copy.start()
        square = jnp.zeros((1, 1), F32)
        for m in range(mols):
            f = jnp.full((1, 1), len_ref[m], jnp.int32).astype(F32)
            square = square + f * f
        tbuf[...] = jnp.broadcast_to(square, tbuf.shape)
        total_job.tick(0)
        gath[0] = normed2_ref[...]
        bbuf[...] = jnp.zeros_like(bbuf)
        sbuf[...] = jnp.zeros_like(sbuf)
        for copy in down_load:
            copy.wait()
        for i in range(piece):
            part = pl.ds(i * rows, rows)
            wdhi[part, :], wdlo[part, :] = split(pn[2 + i])
        for copy in cot_load + up_load:
            copy.wait()
        for i in range(piece):
            part = pl.ds(i * rows, rows)
            wuhi[part, :], wulo[part, :] = split(pn[i])
        total_job.tick(1)

        def p1(b, carry):
            hi, lo = split(cots[b])
            keep(DACT, b, mm3_nt(hi, lo, wdhi[...], wdlo[...]))
            return carry

        lax.fori_loop(0, 4, p1, 0)
        n_core.wait()
        total_job.tick(2)

        def p2(b):
            hi, lo = split(gath[b])
            upper = mm3_nn(hi, lo, wuhi[...], wulo[...]) + bup_ref[...]
            a, slope = gelu_and_slope(upper)
            keep(ACT, b, a)
            du = kept(DACT, b) * slope
            dhi, dlo = split(du)
            duhi[b] = dhi
            dulo[b] = dlo
            part = jnp.sum(du, axis=0, keepdims=True)
            bbuf[...] = bbuf[...] + jnp.broadcast_to(part, bbuf.shape)
            pn[b] = mm3_nt(dhi, dlo, wuhi[...], wulo[...])

        def p2_loop(b, carry):
            @pl.when(b == 2)
            def _():
                dn_core.start()
                first_work()
                n_x.wait()
                n_diag.start()
                total_job.tick(3)

            @pl.when(b == 3)
            def _():
                n_diag.wait()
                total_job.tick(4)
            p2(b)
            return carry

        def first_work():
            first = first_ref[...]
            cen = first - jnp.mean(first, axis=-1, keepdims=True)
            rstd = lax.rsqrt(jnp.mean(cen * cen, axis=-1, keepdims=True) + EPSILON)
            normed = cen * rstd * gain_ref[...] + shift_ref[...]
            for m in range(mols):
                nt[:, m * slots:(m + 1) * slots] = jnp.transpose(normed[m * slots:(m + 1) * slots])
                qhi[m], qlo[m] = split(qt_ref[m])
                khi[m], klo[m] = split(kt_ref[m])
                vhi[m], vlo[m] = split(vt_ref[m])
            dn1[...] = jnp.zeros_like(dn1)
            energy[...] = jnp.zeros_like(energy)
            lax.fori_loop(0, 2, down_part, 0)
            for k in range(4):
                lax.fori_loop(0, 2, functools.partial(weight_part, k), 0)

        lax.fori_loop(0, 4, p2_loop, 0)
        dn_diag.start()
        running["b"].tick(0)
        for k in range(5, total_job.ticks):
            total_job.tick(k)
        dn_diag.wait()
        pn[2] = pn[2] + rsn[1]
        dn_x.start()

    def down_part(b, carry):
        hi, lo = split(kept(ACT, b))
        pd[b] = mm3_nn(hi, lo, wdhi[...], wdlo[...])
        return carry

    def weight_part(k, b, carry):
        part = slice((k % 2) * half, (k % 2 + 1) * half)
        left = kept(ACT, b)[:, part] if k < 2 else gath[b, :, part]
        ahi, alo = split(jnp.transpose(left))
        if k < 2:
            chi, clo = split(cots[b])
        else:
            chi, clo = duhi[b], dulo[b]
        g = mm3_nn(ahi, alo, chi, clo)
        to = pl.ds(k * half, half)

        @pl.when(b == 0)
        def _():
            ebuf[to, :] = g

        @pl.when(b > 0)
        def _():
            ebuf[to, :] = ebuf[to, :] + g
        return carry

    def seg_e(k):
        lax.fori_loop(2, 4, functools.partial(weight_part, k), 0)
        q = plan["ne"] // 4
        for i in range(k * q, (k + 1) * q):
            running["e%d" % i].tick(0)

    def seg_down():
        lax.fori_loop(2, 4, down_part, 0)
        dd_core.start()
        dd_diag.start()
        dd_diag.wait()
        pd[2] = pd[2] + rsd[1]
        dd_x.start()

    def small(i, value):
        sbuf[types + i:types + i + 1, :] = value

    def seg_pro1():
        dn_core.wait()
        dn_x.wait()
        mid = middle_ref[...]
        cen = mid - jnp.mean(mid, axis=-1, keepdims=True)
        rstd = lax.rsqrt(jnp.mean(cen * cen, axis=-1, keepdims=True) + EPSILON)
        xhat = cen * rstd
        c = pn[0] + (rsn[0] + rsn[2])
        small(0, jnp.sum(c * xhat, axis=0, keepdims=True))
        small(1, jnp.sum(c, axis=0, keepdims=True))
        cot = cots[0]
        small(2, jnp.sum(cot, axis=0, keepdims=True))
        ce = c * fgain_ref[...]
        dmiddle = cot + rstd * (ce - jnp.mean(ce, axis=-1, keepdims=True) - xhat * jnp.mean(ce * xhat, axis=-1, keepdims=True))
        dmid[...] = dmiddle
        small(3, jnp.sum(dmiddle, axis=0, keepdims=True))
        for copy in load:
            copy.wait()
        dhi, dlo = split(dmiddle)
        mhi, mlo = split(jnp.concatenate([mixt_ref[m] for m in range(mols)], 1))
        obuf[...] = mm3_nn(mhi, mlo, dhi, dlo)
        for i in range(plan["no"]):
            running["o%d" % i].tick(0)

    def seg_pro2():
        wohi, wolo = split(wo[...])
        dhi, dlo = split(dmid[...])
        dm = mm3_nt(dhi, dlo, wohi, wolo)
        lane = lax.broadcasted_iota(jnp.int32, (slots, 128), 1)
        rowi = lax.broadcasted_iota(jnp.int32, (slots, slots), 0)
        coli = lax.broadcasted_iota(jnp.int32, (slots, slots), 1)
        twice = 2.0 / (heads * tres[0:1, 0:slots])
        for m in range(mols):
            length = len_ref[m]
            maskc[m] = jnp.where(jnp.logical_and(rowi < length, coli < length), twice, 0.0)
            dmt = jnp.transpose(dm[m * slots:(m + 1) * slots]) * linv_ref[m]
            dmhi[m], dmlo[m] = split(dmt)
            prod = dmt * mixt_ref[m]
            delta = jnp.sum(prod.reshape(heads, 8, slots), axis=1)
            for g in range(groups):
                d8 = -delta[g * 8:(g + 1) * 8]
                x = jnp.concatenate([dmt[g * 64:(g + 1) * 64], d8, d8, jnp.zeros((48, slots), F32)], 0)
                y = jnp.transpose(x)
                yhi = y.astype(BF).astype(F32)
                ylo = y - yhi
                dl[m, g, :, 0:128] = jnp.where(lane < 64, yhi, pltpu.roll(ylo, 64, 1)).astype(BF)
                dl[m, g, :, 128:256] = jnp.where(lane < 72, yhi, ylo).astype(BF)

    def seg_chunk(c):
        part = slice(c * fcols, (c + 1) * fcols)
        nhi, nlo = split(nt[...])
        for i, t_ref in enumerate((dqt, dkt, dvt)):
            thi, tlo = split(jnp.concatenate([t_ref[mm, part, :] for mm in range(mols)], 1))
            fbuf[c, i * width:(i + 1) * width, :] = mm3_nt(nhi, nlo, thi, tlo)
        for h in range(plan["fs"]):
            running["f%d_%d" % (c, h)].tick(0)
        acc = dn1[...]
        for i, (t_ref, w) in enumerate(((dqt, wq), (dkt, wk), (dvt, wv))):
            nat = jnp.concatenate([jnp.transpose(t_ref[mm, part, :]) for mm in range(mols)], 0)
            if i != 1:
                r = types + (4 if i == 0 else 5)
                sbuf[r:r + 1, part] = jnp.sum(nat, axis=0, keepdims=True)
            ahi, alo = split(nat)
            whi, wlo = split(w[:, part])
            acc = acc + mm3_nt(ahi, alo, whi, wlo)
        dn1[...] = acc

    def seg_end():
        first = first_ref[...]
        cen = first - jnp.mean(first, axis=-1, keepdims=True)
        rstd = lax.rsqrt(jnp.mean(cen * cen, axis=-1, keepdims=True) + EPSILON)
        xhat = cen * rstd
        dn = dn1[...]
        small(6, jnp.sum(dn * xhat, axis=0, keepdims=True))
        small(7, jnp.sum(dn, axis=0, keepdims=True))
        ge = dn * gain_ref[...]
        gat = dmid[...] + rstd * (ge - jnp.mean(ge, axis=-1, keepdims=True) - xhat * jnp.mean(ge * xhat, axis=-1, keepdims=True))
        gatv[...] = gat
        acc = None
        for mm in range(mols):
            one = (lax.broadcasted_iota(jnp.int32, (types, slots), 0) == types_ref[mm]).astype(F32).astype(BF)
            for bits in split3(gat[mm * slots:(mm + 1) * slots]):
                part = dot(one, bits)
                acc = part if acc is None else acc + part
        sbuf[0:types, :] = acc
        total = jnp.sum(jnp.sum(energy[...], axis=0, keepdims=True), axis=1, keepdims=True) * 0.5
        small(8, jnp.broadcast_to(total, (1, width)))
        running["s"].tick(0)

    work = {"ffn": seg_ffn, "e": seg_e, "down": seg_down, "pro1": seg_pro1, "pro2": seg_pro2, "chunk": seg_chunk, "end": seg_end}
    before, after = [], {}
    step_now = None
    for (name, _, _), ticks in zip(segments, points):
        if name[0] == "step":
            step_now = name[1]
        else:
            to = before if step_now is None else after.setdefault(step_now, [])
            to.append(functools.partial(work[name[0]], *name[1:]))
        to = before if step_now is None else after.setdefault(step_now, [])
        to += [functools.partial(running[job].tick, k) for job, k in ticks]

    @pl.when(s == 0)
    def _():
        for fn in before:
            fn()

    g = s // mols
    m = s % mols
    lhs = dl[m, g]
    sub = lax.broadcasted_iota(jnp.int32, (16, 128), 0)
    z = jnp.zeros((16, 256), BF)
    zero16 = jnp.zeros((16, 128), BF)
    mc = maskc[m]
    en = energy[...]
    for p in range(4):
        row = pl.multiple_of(g * 64 + 16 * p, 16)
        rows16 = pl.ds(row, 16)

        def blk(x):
            x = x.astype(F32)
            a = jnp.where(sub < 8, x, 0.0).astype(BF)
            b = jnp.where(sub >= 8, x, 0.0).astype(BF)
            return jnp.concatenate([a, b], axis=1)
        bhi, blo = blk(vhi[m, rows16, :]), blk(vlo[m, rows16, :])
        sel = jnp.concatenate([jnp.where(sub % 8 == 2 * p, 1.0, 0.0), jnp.where(sub % 8 == 2 * p + 1, 1.0, 0.0)], axis=1).astype(BF)
        rws = [bhi if i == p else z for i in range(4)]
        rws += rws
        rws += [blo if i == p else z for i in range(4)]
        rws += [sel, z, z, z]
        dp = dot(lhs, jnp.concatenate(rws, axis=0))
        gs = []
        es = []
        for hf in range(2):
            both = e_ref[0, 2 * p + hf]
            es.append(both)
            e = both[:, 0:128].astype(F32) + both[:, 128:256].astype(F32)
            logits = pair_ref[0, 2 * p + hf]
            t = logits * mc
            en = en + t * logits
            gp = e * dp[:, hf * 128:(hf + 1) * 128] + t
            gpair[m, g * 8 + 2 * p + hf] = gp
            gs.append(split(gp))

        def rows_lhs(hi, lo):
            return jnp.concatenate([jnp.concatenate([hi, hi], 1), jnp.concatenate([lo, zero16], 1)], 0)

        def take(out):
            acc = out[0:16] + out[16:32]
            return jnp.concatenate([acc[0:8, 0:128], acc[8:16, 128:256]], 0)
        ecol = jnp.concatenate([jnp.concatenate([es[0][:, 0:128], es[1][:, 0:128]], 1), jnp.concatenate([es[0][:, 128:256], es[1][:, 128:256]], 1)], 0)
        dvt[m, rows16, :] = take(dot(rows_lhs(dmhi[m, rows16, :], dmlo[m, rows16, :]), ecol))
        gcol = jnp.concatenate([jnp.concatenate([gs[0][0], gs[1][0]], 1), jnp.concatenate([gs[0][1], gs[1][1]], 1)], 0)
        dkt[m, rows16, :] = take(dot(rows_lhs(qhi[m, rows16, :], qlo[m, rows16, :]), gcol))
        grow = jnp.concatenate([jnp.concatenate(gs[0], 1), jnp.concatenate(gs[1], 1)], 0)
        dqt[m, rows16, :] = take(dot_nt(rows_lhs(khi[m, rows16, :], klo[m, rows16, :]), grow)) * (8 ** -0.5)
    energy[...] = en

    for at in sorted(after):
        def body(at=at):
            for fn in after[at]:
                fn()
            if at == last:
                dd_core.wait()
                dd_x.wait()
                outv[...] = middle_ref[...] + bdown_ref[...] + (pd[0] + (rsd[0] + rsd[2]))
        pl.when(s == at)(body)


CONFIG = dict(ne=8, ch=4, fs=3, no=2, eo=[2, 0, 0, 0, 0, 0, 0, 0], fo=[2, 2, 2, 5, 2, 0, 0, 0, 2, 5, 6, 1], oo=[2, 0], so=5, pos=[-2, -2, 15, 2, -1])


def main_call(mesh, lengths, types, normed2, cots, middle, first, qt, kt, vt, mixt, linv, gain, shift, fgain, bup, bdown,
              wup, wdown, wq, wk, wv, wo, pair, e, ntypes):
    mols, slots = types.shape
    rows, width = first.shape
    heads = pair.shape[1]
    groups = heads // 8
    hidden = wup.shape[1]
    dp = mesh.shape["dp"]
    dpbits = dp.bit_length() - 1
    assert (1 << dpbits) == dp and mesh.shape["tensor"] == 4
    small = -(-(ntypes + 9) // 64) * 64
    config = CONFIG if dpbits <= 3 else dict(ne=4, ch=1, fs=1, no=1, eo=[0] * 4, fo=[0], oo=[0], so=0, pos=[-2, -2, -2, -2, -2])
    jobs, segments, points = make_plan(config, dpbits, mols, groups, width, hidden, small)
    chunks = config["ch"]
    fcols = width // chunks
    needs = {"e": 0, "o": 0, "f": 0, "s": 0, "b": 0}
    stages = stages_of("CXYZW", dpbits)
    t_need = job_need(8, stages)
    nslots = 9 + t_need[1]
    for kind, index, first_row, nrows, order in jobs.values():
        need = job_need(nrows, order)
        needs[kind] += need[0]
        nslots += need[1]
    plan = dict(dpbits=dpbits, chunks=chunks, types=ntypes, slots=nslots, jobs=jobs, segments=segments, points=points,
                ne=config["ne"], no=config["no"], fs=config["fs"])
    V = pltpu.VMEM
    one = lambda shape: pl.BlockSpec(shape, lambda s: (0,) * len(shape), pipeline_mode=pl.Buffered(1))
    any_ = pl.BlockSpec(memory_space=pl.ANY)
    smem = pl.BlockSpec(memory_space=pltpu.SMEM)
    vmem = pl.BlockSpec(memory_space=pltpu.VMEM)
    vec = lambda v: v.reshape(1, -1)
    blk = lambda w: pl.BlockSpec((1, 8, slots, w), lambda s: (s % mols, s // mols, 0, 0))
    tt = (mols, width, slots)
    rw = (rows, width)
    in_specs = [smem, one((mols, 1, slots)), one(rw)] + [any_] * 4 + [one(rw)] * 2 + [one(tt)] * 5 + \
        [one((1, width))] * 3 + [one((1, hidden)), one((1, width))] + [any_] * 6 + [blk(slots), blk(2 * slots)]
    ww = (width, width)
    ff = (width + hidden, width)
    outs = [V(pair.shape, F32), V(rw, F32), V(rw, F32), V(ff, F32), V(ww, F32), V((chunks, 3 * width, fcols), F32), V((small, width), F32), V((8, hidden), F32)]
    four = (4, rows, width)
    scratch = [V((mols, groups, slots, 256), BF)] + [V(tt, BF)] * 8 + [V(tt, F32)] * 3 + [V((mols, slots, slots), F32), V(rw, F32), V((slots, slots), F32)]
    scratch += [V(ww, F32)] * 4 + [V((width, hidden), BF)] * 2 + [V((hidden, width), BF)] * 2
    scratch += [V(four, F32)] * 2 + [V(four, BF)] * 2 + [V(four, F32)] * 2 + [V((3, rows, width), F32)] * 2 + [V((width, rows), F32), V(rw, F32)]
    scratch += [V(ff, F32), V((needs["e"], width), F32), V(ww, F32), V((needs["o"], width), F32)]
    scratch += [V((chunks, 3 * width, fcols), F32), V((needs["f"], fcols), F32), V((small, width), F32), V((needs["s"], width), F32)]
    scratch += [V((8, 128), F32)] * 2 + [V((t_need[0], 128), F32), V((8, hidden), F32), V((needs["b"], hidden), F32)]
    scratch += [pltpu.SemaphoreType.DMA((2, nslots)), pltpu.SemaphoreType.REGULAR((nslots,)), pltpu.SemaphoreType.DMA((12,))]
    return pl.pallas_call(functools.partial(main_kernel, plan), out_shape=outs, grid=(mols * groups,), in_specs=in_specs, out_specs=[vmem] * 8,
        scratch_shapes=scratch,
        compiler_params=pltpu.CompilerParams(vmem_limit_bytes=VLIMIT, dimension_semantics=("arbitrary",), collective_id=0, has_side_effects=True),
        name="feed_forward_and_backward",
    )(lengths, types.reshape(mols, 1, slots), normed2, *cots, middle, first, qt, kt, vt, mixt, linv, vec(gain), vec(shift), vec(fgain), vec(bup), vec(bdown),
      wup, wdown, wq, wk, wv, wo, pair, e)


VLIMIT = 47 * 1024 * 1024
SMALL_ROWS = (0, 1, 2, 3, 4, 5, 6, 7)


def finish_kernel(types, gpair, outv, gatv, eres, ores, fres, sres, bres, *refs):
    refs = list(refs)
    gp_out, atom_out, gatoms_out, gdown_out, gup_out, gwo_out, gwq_out, gwk_out, gwv_out, table_out = [refs.pop(0) for _ in range(10)]
    rows_out = [refs.pop(0) for _ in range(len(SMALL_ROWS))]
    gbup_out, pen_out, sems = refs
    width = outv.shape[1]
    hidden = eres.shape[0] - width
    copies = []

    def go(src, dst):
        copy = pltpu.make_async_copy(src, dst, sems.at[len(copies)])
        copy.start()
        copies.append(copy)

    for m in range(gpair.shape[0]):
        for h in range(0, gpair.shape[1], 16):
            go(gpair.at[m, pl.ds(h, 16)], gp_out.at[m, pl.ds(h, 16)])
    go(eres.at[pl.ds(0, hidden)], gdown_out)
    go(eres.at[pl.ds(hidden, width)], gup_out)
    go(ores, gwo_out)
    chunks, _, fcols = fres.shape
    for c in range(chunks):
        for j, out in enumerate((gwq_out, gwk_out, gwv_out)):
            go(fres.at[c, pl.ds(j * width, width)], out.at[:, pl.ds(c * fcols, fcols)])
    go(outv, atom_out)
    go(gatv, gatoms_out)
    go(sres.at[pl.ds(0, types)], table_out)
    for i, out in zip(SMALL_ROWS, rows_out):
        out[...] = sres[types + i, :]
    gbup_out[...] = bres[0, :]
    pen_out[0, 0] = jnp.sum(sres[types + 8:types + 9, 0:1])
    for copy in copies:
        copy.wait()


def finish(types, parts, width, hidden):
    gpair, outv, gatv, eres, ores, fres, sres, bres = parts
    S = jax.ShapeDtypeStruct
    any_ = pl.BlockSpec(memory_space=pl.ANY)
    vmem = pl.BlockSpec(memory_space=pltpu.VMEM)
    shapes = [gpair.shape, outv.shape, gatv.shape, (hidden, width), (width, hidden)] + [(width, width)] * 4 + [(types, width)]
    outs = [S(shape, F32) for shape in shapes] + [S((width,), F32)] * len(SMALL_ROWS) + [S((hidden,), F32), S((1, 1), F32)]
    ncopies = gpair.shape[0] * gpair.shape[1] // 16 + 6 + 3 * fres.shape[0]
    return pl.pallas_call(functools.partial(finish_kernel, types), out_shape=outs, in_specs=[vmem] * 8,
        out_specs=[any_] * 10 + [vmem] * (len(SMALL_ROWS) + 1) + [pl.BlockSpec(memory_space=pltpu.SMEM)],
        scratch_shapes=[pltpu.SemaphoreType.DMA((ncopies,))], compiler_params=pltpu.CompilerParams(vmem_limit_bytes=4 * 1024 * 1024),
        name="finish")(*parts)


def local(mesh, atom_types, lengths, atom_feats, pair_bias, out_cotangent, type_table, norm_gain, norm_shift, w_query, b_query,
          w_key, w_value, b_value, w_out, b_out, ffn_gain, ffn_shift, w_up, b_up, w_down, b_down):
    tensor = mesh.shape["tensor"]
    cots = [out_cotangent] + [lax.ppermute(out_cotangent, "tensor", [(i, i ^ d) for i in range(tensor)]) for d in (1, 2, 3)]
    pair_out, e, first, qt, kt, vt, mixt, linv, middle, normed2 = attention_forward(
        lengths, atom_types, atom_feats, type_table, norm_gain, norm_shift, w_query, b_query, w_key, w_value, b_value, w_out, b_out,
        ffn_gain, ffn_shift, pair_bias)
    types = type_table.shape[0]
    parts = main_call(
        mesh, lengths, atom_types, normed2, cots, middle, first, qt, kt, vt, mixt, linv, norm_gain, norm_shift, ffn_gain, b_up, b_down,
        w_up, w_down, w_query, w_key, w_value, w_out, pair_out, e, types)
    (grad_pair, atom_out, grad_atoms, gwdown, gwup, gwo, gwq, gwk, gwv, table, g_fgain, g_fshift, g_bdown, g_bout, g_bq, g_bv, g_gain, g_shift,
     gbup, penalty) = finish(types, parts, w_up.shape[0], w_up.shape[1])
    return (atom_out, pair_out, penalty.reshape(()), grad_atoms, grad_pair, table, g_gain, g_shift, gwq, g_bq, gwk, gwv, g_bv,
            gwo, g_bout, g_fgain, g_fshift, gwup, gbup, gwdown, g_bdown)


def solution(mesh):
    in_specs = (
        P(("dp", "tensor"), None),
        P(("dp", "tensor")),
        P(("dp", "tensor"), None),
        P(("dp", "tensor"), None, None, None),
        P(("dp", "tensor"), None),
        P(),
        P(),
        P(),
        P(),
        P(),
        P(),
        P(),
        P(),
        P(),
        P(),
        P(),
        P(),
        P(None, "tensor"),
        P("tensor"),
        P("tensor", None),
        P(),
    )
    out_specs = (
        P(("dp", "tensor"), None),
        P(("dp", "tensor"), None, None, None),
        P(),
        P(("dp", "tensor"), None),
        P(("dp", "tensor"), None, None, None),
        P(),
        P(),
        P(),
        P(),
        P(),
        P(),
        P(),
        P(),
        P(),
        P(),
        P(),
        P(),
        P(None, "tensor"),
        P("tensor"),
        P("tensor", None),
        P(),
    )
    return jax.shard_map(functools.partial(local, mesh), mesh=mesh, in_specs=in_specs, out_specs=out_specs, check_vma=False)
```

```python
import functools, math
import jax, jax.numpy as jnp
from jax import lax
from jax.experimental import pallas as pl
from jax.experimental.pallas import tpu as pltpu
from jax.sharding import PartitionSpec as P
F32=jnp.float32; BF=jnp.bfloat16
EPSILON=1e-5
SPAN=2

def split(x):
    hi = x.astype(BF)
    lo = (x - hi.astype(F32)).astype(BF)
    return hi, lo

def split3(x):
    hi = x.astype(BF)
    r = x - hi.astype(F32)
    mid = r.astype(BF)
    lo = (r - mid.astype(F32)).astype(BF)
    return hi, mid, lo

def dot(a, b):
    return jnp.dot(a, b, preferred_element_type=F32)

def dot_nt(a, b):
    return lax.dot_general(a, b, (((1,), (1,)), ((), ())), preferred_element_type=F32)

def mm3(a, bhi, blo):
    ahi, alo = split(a)
    return dot(ahi, bhi) + (dot(ahi, blo) + dot(alo, bhi))

def fwd_kernel(len_ref, types_ref, feats_ref, table_ref, gain_ref, shift_ref, wq_ref, bq_ref, wk_ref, wv_ref, bv_ref,
               wo_ref, bo_ref, fgain_ref, fshift_ref, bias_ref,
               pair_ref, e_ref, first_ref, qthi, qtlo, kthi, ktlo, vthi, vtlo, mixt_ref, linv_ref, middle_ref, normed_ref,
               ql, *, span):
    s = pl.program_id(0)
    mols, slots = types_ref.shape[0], types_ref.shape[2]
    groups = ql.shape[1]
    @pl.when(s == 0)
    def _():
        tab = split3(table_ref[...])
        types = table_ref.shape[0]
        for m in range(mols):
            ids = types_ref[m]
            oneT = (lax.broadcasted_iota(jnp.int32, (slots, slots), 0) == ids).astype(F32)
            one = jnp.transpose(oneT)[:, :types].astype(BF)
            rows = pl.ds(m*slots, slots)
            first = feats_ref[rows, :] + (dot(one, tab[0]) + (dot(one, tab[1]) + dot(one, tab[2])))
            first_ref[rows, :] = first
        first = first_ref[...]
        cen = first - jnp.mean(first, axis=-1, keepdims=True)
        var = jnp.mean(cen*cen, axis=-1, keepdims=True)
        normed = cen * lax.rsqrt(var + EPSILON) * gain_ref[...] + shift_ref[...]
        nhi, nlo = split(normed)
        def proj(w_ref):
            whi, wlo = split(w_ref[...])
            return dot(nhi, whi) + (dot(nhi, wlo) + dot(nlo, whi))
        q = (proj(wq_ref) + bq_ref[...]) * (8 ** -0.5)
        k = proj(wk_ref)
        v = proj(wv_ref) + bv_ref[...]
        lane = lax.broadcasted_iota(jnp.int32, (slots, 128), 1)
        for m in range(mols):
            sl = slice(m*slots, (m+1)*slots)
            qm = q[sl]
            qthi[m], qtlo[m] = split(jnp.transpose(qm))
            kt = jnp.transpose(k[sl])
            kthi[m], ktlo[m] = split(kt)
            vt = jnp.transpose(v[sl])
            vthi[m], vtlo[m] = split(vt)
            for t in range(groups // 2):
                tile = qm[:, t*128:(t+1)*128]
                rolled = pltpu.roll(tile, 64, 1)
                for half in range(2):
                    dup = jnp.where(lane < 64, tile, rolled) if half == 0 else jnp.where(lane < 64, rolled, tile)
                    hi, lo = split(dup)
                    hi32, lo32 = hi.astype(F32), lo.astype(F32)
                    ql[m, 2*t+half, :, 0:128] = jnp.where(lane < 64, hi32, lo32).astype(BF)
                    ql[m, 2*t+half, :, 128:256] = jnp.where(lane < 64, hi32, 0.0).astype(BF)
    per = groups // span
    m = s // per
    length = len_ref[m]
    col_live = lax.broadcasted_iota(jnp.int32, (slots, slots), 1) < length
    sub = lax.broadcasted_iota(jnp.int32, (16, 128), 0)
    zero16 = jnp.zeros((16, 128), BF)
    ones = jnp.ones((16, 256), BF)
    def one(i, carry):
        g = (s % per) * span + i
        h0 = i * 8
        lhs = ql[m, g]
        for p in range(4):
            row = pl.multiple_of(g*64 + 16*p, 16)
            khi = kthi[m, pl.ds(row, 16), :].astype(F32)
            klo = ktlo[m, pl.ds(row, 16), :].astype(F32)
            def blk(x):
                a = jnp.where(sub < 8, x, 0.0).astype(BF)
                b = jnp.where(sub >= 8, x, 0.0).astype(BF)
                return jnp.concatenate([a, b], axis=1)
            bhi, blo = blk(khi), blk(klo)
            z = jnp.concatenate([zero16, zero16], axis=1)
            rows = [bhi if i == p else z for i in range(4)]
            rows += rows
            rows += [blo if i == p else z for i in range(4)]
            rows += [z]*4
            rhs = jnp.concatenate(rows, axis=0)
            lg = dot(lhs, rhs)
            ehl = []
            for half in range(2):
                logits = lg[:, half*128:(half+1)*128] + bias_ref[0, h0 + 2*p+half].astype(F32)
                pair_ref[0, h0 + 2*p+half] = logits
                masked = jnp.where(col_live, logits, -1e30)
                top = jnp.max(masked, axis=1, keepdims=True)
                e = jnp.exp(masked - top)
                hi, lo = split(e)
                both = jnp.concatenate([hi, lo], axis=1)
                e_ref[0, h0 + 2*p+half] = both
                ehl.append(both)
            vhi = vthi[m, pl.ds(row, 16), :]
            vlo = vtlo[m, pl.ds(row, 16), :]
            lv = jnp.concatenate([jnp.concatenate([vhi, vhi], 1), jnp.concatenate([vlo, zero16], 1), ones], 0)
            out = dot_nt(lv, jnp.concatenate(ehl, 0))
            acc = out[0:16] + out[16:32]
            sums = out[32:48]
            inv = 1.0 / jnp.concatenate([sums[0:8, 0:128], sums[8:16, 128:256]], 0)
            linv_ref[m, pl.ds(row, 16), :] = inv
            mixt_ref[m, pl.ds(row, 16), :] = jnp.concatenate([acc[0:8, 0:128], acc[8:16, 128:256]], 0) * inv
        return carry

    if span == 1:
        one(0, 0)
    else:
        lax.fori_loop(0, span, one, 0)
    @pl.when(s == mols*groups // span - 1)
    def _():
        mix = jnp.concatenate([jnp.transpose(mixt_ref[m]) for m in range(mols)], 0)
        whi, wlo = split(wo_ref[...])
        mid = first_ref[...] + (mm3(mix, whi, wlo) + bo_ref[...])
        middle_ref[...] = mid
        mcen = mid - jnp.mean(mid, axis=-1, keepdims=True)
        mvar = jnp.mean(mcen*mcen, axis=-1, keepdims=True)
        normed_ref[...] = mcen * lax.rsqrt(mvar + EPSILON) * fgain_ref[...] + fshift_ref[...]

def attention_forward(lengths, types, feats, table, gain, shift, wq, bq, wk, wv, bv, wo, bo, fgain, fshift, bias):
    mols, slots = types.shape
    width = feats.shape[1]
    heads = bias.shape[1]
    groups = heads // 8
    rows = mols*slots
    full = lambda shape: pl.BlockSpec(shape, lambda s: (0,)*len(shape))
    vec = lambda v: v.reshape(1, -1)
    outs = [jax.ShapeDtypeStruct((mols, heads, slots, slots), F32),
            jax.ShapeDtypeStruct((mols, heads, slots, 2*slots), BF),
            jax.ShapeDtypeStruct((rows, width), F32)] + [jax.ShapeDtypeStruct((mols, width, slots), BF)]*6 + [jax.ShapeDtypeStruct((mols, width, slots), F32)]*2 + [jax.ShapeDtypeStruct((rows, width), F32)]*2
    blk = lambda w: pl.BlockSpec((1, 8*SPAN, slots, w), lambda s: (s // (groups // SPAN), s % (groups // SPAN), 0, 0))
    in_specs = [pl.BlockSpec(memory_space=pltpu.SMEM), full((mols,1,slots)), full((rows,width)), full(table.shape), full((1,width)), full((1,width)),
                full(wq.shape), full((1,width)), full(wk.shape), full(wv.shape), full((1,width)), full(wo.shape), full((1,width)), full((1,width)), full((1,width)), blk(slots)]
    return pl.pallas_call(functools.partial(fwd_kernel, span=SPAN), out_shape=outs, grid=(mols*groups // SPAN,), in_specs=in_specs,
        out_specs=[blk(slots), blk(2*slots), full((rows,width))] + [full((mols,width,slots))]*8 + [full((rows,width))]*2,
        scratch_shapes=[pltpu.VMEM((mols, groups, slots, 256), BF)],
        compiler_params=pltpu.CompilerParams(vmem_limit_bytes=60*1024*1024, dimension_semantics=("arbitrary",)),
        name="attention_forward",
    )(lengths, types.reshape(mols,1,slots), feats, table, vec(gain), vec(shift), wq, vec(bq), wk, wv, vec(bv), wo, vec(bo), vec(fgain), vec(fshift), bias)


LOGICAL = pl.DeviceIdType.LOGICAL


class Place:
    def __init__(self, dpbits):
        tensor, dp = lax.axis_index("tensor"), lax.axis_index("dp")
        me = dp * 4 + tensor
        self.bits, self.partners = {}, {}
        for axis, index, count, stride in (("tensor", tensor, 2, 1), ("dp", dp, dpbits, 4)):
            for bit in range(count):
                value = lax.rem(lax.div(index, 1 << bit), 2)
                self.bits[axis, bit] = value
                self.partners[axis, bit] = me + (1 - 2 * value) * (stride << bit)


class Exchange:
    def __init__(self, at, src, dst, sems, slot, stage, before=None, after=None):
        self.before, self.after = before, after
        self.copy = lambda: pltpu.make_async_remote_copy(
            src_ref=src(), dst_ref=dst(), send_sem=sems.at[0, slot], recv_sem=sems.at[1, slot],
            device_id=at.partners[stage], device_id_type=LOGICAL)

    def start(self):
        if self.before is not None:
            self.before()
        self.copy().start()

    def wait(self):
        self.copy().wait()
        if self.after is not None:
            self.after()


class Pause:
    def __init__(self, wait):
        self.wait = wait

    def start(self):
        pass


class Job:
    def __init__(self, at, buf, recv, sems, free, first_slot, rows, stages, done=None):
        self.done = done
        self.slots = 0
        self.recv_rows = 0
        self.steps = []
        plan = []
        numbers = []
        length = rows
        for stage in stages:
            halve = (length // 2) % 8 == 0
            part = length // 2 if halve else length
            plan.append((stage, halve, length, part, self.recv_rows))
            self.recv_rows += part
            length = part
        halved = [p[0] for p in plan if p[1]]

        def offset(count):
            off, size = 0, rows
            for axis, bit in halved[:count]:
                size //= 2
                off = off + at.bits[axis, bit] * size
            return off if isinstance(off, int) else pl.multiple_of(off, 8)

        depth = 0
        for stage, halve, length, part, place in plan:
            here = depth
            if halve:
                depth += 1

                def src(stage=stage, here=here, part=part):
                    return buf.at[pl.ds(pl.multiple_of(offset(here) + (1 - at.bits[stage]) * part, 8), part)]
            else:
                def src(here=here, part=part):
                    return buf.at[pl.ds(offset(here), part)]

            def dst(place=place, part=part):
                return recv.at[pl.ds(place, part)]

            def add(depth=depth, place=place, part=part, to=buf):
                mine = pl.ds(offset(depth), part)
                to[mine, :] = buf[mine, :] + recv[pl.ds(place, part), :]

            number = first_slot + self.slots

            def tell(number=number, stage=stage):
                pl.semaphore_signal(free.at[number], inc=1, device_id=at.partners[stage], device_id_type=LOGICAL)

            self.steps.append((Exchange(at, src, dst, sems, number, stage, after=tell if halve else None), add))
            numbers.append(number)
            self.slots += 1
        if plan[-1][1]:
            self.steps.append((Pause(lambda number=numbers[-1]: pl.semaphore_wait(free.at[number], 1)), None))
        for (stage, halve, length, part, place), number in zip(reversed(plan), reversed(numbers)):
            if not halve:
                continue

            def freed(number=number):
                pl.semaphore_wait(free.at[number], 1)

            def region(depth=depth, part=part):
                return buf.at[pl.ds(offset(depth), part)]

            if number == numbers[-1]:
                freed = None
            self.steps.append((Exchange(at, region, region, sems, first_slot + self.slots, stage, before=freed), None))
            self.slots += 1
            depth -= 1
        self.ticks = len(self.steps) + 1

    def tick(self, k):
        if k > 0:
            exchange, add = self.steps[k - 1]
            exchange.wait()
            if add is not None:
                add()
        if k < len(self.steps):
            self.steps[k][0].start()
        elif self.done is not None:
            self.done()


class Actions:
    def __init__(self, *functions):
        self.tick = lambda k: functions[k]()


def job_need(rows, stages):
    job = Job(None, None, None, None, None, 0, rows, stages)
    return job.recv_rows, job.slots


ORDERS = ("CXYZW", "CXZWY", "CYXZW", "CYZWX", "CZWXY", "CXZYW", "CZXYW", "CZYXW")
E_ORDERS = ("YZW", "ZWY", "ZYW")


def stages_of(order, dpbits):
    table = {"C": [("tensor", 0)], "X": [("tensor", 1)], "Y": [("dp", i) for i in range(dpbits - 2)],
             "Z": [("dp", dpbits - 2)], "W": [("dp", dpbits - 1)]}
    return [stage for token in order for stage in table[token]]


def stage_cost(stage, size):
    rate = 43.0e3
    if stage is None:
        return [], 1.0
    axis, bit = stage
    if axis == "tensor":
        return ([("core", size / 700e3)], 0.9) if bit == 0 else ([("x", size / rate)], 2.0)
    if bit == 0:
        return [("y", size / rate)], 2.0
    if bit == 1:
        return [("outer", size / rate)], 2.0
    return [("outer", size / rate), ("inner", 2 * size / rate)], 2.5


def tick_order(segments, jobs):
    now, free, flying, points, current = 0.0, {}, [], [], []
    segments = list(segments)
    ended = set()

    def start(name, k):
        stage, size, _ = jobs[name][k]
        links, latency = stage_cost(stage, size)
        begin = max([now] + [free.get(link, 0.0) for link, _ in links])
        for link, length in links:
            free[link] = begin + length
        flying.append((begin + max([length for _, length in links], default=0.0) + latency, name, k))

    while segments or flying:
        ready = [f for f in flying if f[0] <= now]
        if ready:
            first = min(ready)
            flying.remove(first)
            _, name, k = first
            now += 0.05 + (jobs[name][k][1] / 1.5e6 if jobs[name][k][2] else 0.0)
            current.append((name, k + 1))
            if k + 1 < len(jobs[name]):
                start(name, k + 1)
            else:
                ended.add(name)
        elif segments and all(name in ended for name in segments[0][3]):
            points.append(current)
            current = []
            _, length, released, _ = segments.pop(0)
            now += length
            for name in released:
                start(name, 0)
        else:
            now = min(f[0] for f in flying)
    points.append(current)
    return points[1:]


def job_steps(rows, width, stages):
    length, out, back = rows, [], []
    for stage in stages:
        halve = (length // 2) % 8 == 0
        length = length // 2 if halve else length
        out.append((stage, length * width * 4, True))
        if halve:
            back.append((stage, length * width * 4, False))
    return out + ([(None, 0, False)] if halve else []) + back[::-1]


def make_plan(config, dpbits, mols, groups, width, hidden, small):
    ne, ch, fs, no = config["ne"], config["ch"], config["fs"], config["no"]
    jobs, steps = {}, {}

    def add(name, kind, index, first, rows, stages, cols):
        jobs[name] = (kind, index, first, rows, stages)
        steps[name] = job_steps(rows, cols, stages)

    for i in range(ne):
        n = (width + hidden) // ne
        add("e%d" % i, "e", 0, i * n, n, stages_of(E_ORDERS[config["eo"][i]], dpbits), width)
    for i in range(no):
        n = width // no
        add("o%d" % i, "o", 0, i * n, n, stages_of(ORDERS[config["oo"][i]], dpbits), width)
    for c in range(ch):
        for h in range(fs):
            n = 3 * width // fs
            add("f%d_%d" % (c, h), "f", c, h * n, n, stages_of(ORDERS[config["fo"][c * fs + h]], dpbits), width // ch)
    add("s", "s", 0, 0, small, stages_of(ORDERS[config["so"]], dpbits), width)
    add("b", "b", 0, 0, 8, stages_of("YZW", dpbits), hidden)
    q = ne // 4
    pos = config["pos"]
    segments = []

    def put(moment):
        for k in range(4):
            if pos[k] == moment:
                segments.append((("e", k), 0.65 if k < 2 else 1.3, ["e%d" % i for i in range(k * q, (k + 1) * q)], []))
        if pos[4] == moment:
            segments.append((("down",), 2.3, ["d"], []))

    swap = width * width * 2
    steps["d"] = [(("tensor", 0), swap, True), (("tensor", 1), swap, False)]
    steps["n"] = [(("tensor", 0), swap // 2, True), (("tensor", 1), swap // 2, False)]
    segments.append((("ffn",), 0.0, ["n", "b"], []))
    put(-2)
    segments.append((("pro1",), 1.2, ["o%d" % i for i in range(no)], ["n"]))
    put(-1)
    segments.append((("pro2",), 1.0, [], []))
    per = groups // ch
    for s in range(mols * groups):
        segments.append((("step", s), 0.8, [], []))
        if (s + 1) % (per * mols) == 0:
            c = s // (per * mols)
            segments.append((("chunk", c), 5.0 / ch, ["f%d_%d" % (c, h) for h in range(fs)], []))
        put(s)
    segments.append((("end",), 0.6, ["s"], []))
    return jobs, segments, tick_order(segments, steps)


def gelu_and_slope(x):
    cdf = 0.5 + 0.5 * lax.erf(x * (0.5 ** 0.5))
    return x * cdf, cdf + x * (jnp.exp(-0.5 * x * x) * (1.0 / math.sqrt(2.0 * math.pi)))


def mm3_nt(ahi, alo, bhi, blo):
    return dot_nt(ahi, bhi) + (dot_nt(ahi, blo) + dot_nt(alo, bhi))


def mm3_nn(ahi, alo, bhi, blo):
    return dot(ahi, bhi) + (dot(ahi, blo) + dot(alo, bhi))


def main_kernel(plan, *refs):
    refs = list(refs)
    take_n = lambda n: [refs.pop(0) for _ in range(n)]
    len_ref, types_ref, normed2_any = take_n(3)
    cot_refs = take_n(4)
    held_any = take_n(10)
    gain_ref, shift_ref, fgain_ref, bup_ref, bdown_ref = take_n(5)
    wup_any, wdown_any, wq_any, wk_any, wv_any, wo_any, pair_any, e_any = take_n(8)
    gpair, outv, gatv, eres, ores, fres, sres, bres = take_n(8)
    dl, qhi, qlo, khi, klo, vhi, vlo, dmhi, dmlo, dqt, dkt, dvt, maskc, dmid, energy = take_n(15)
    wq, wk, wv, wo, wuhi, wulo, wdhi, wdlo = take_n(8)
    gath, cots, duhi, dulo, pn, pd, rsn, rsd, nt, dn1 = take_n(10)
    ebuf, erecv, obuf, orecv, fbuf, frecv, sbuf, srecv, tbuf, tres, trecv, bbuf, brecv = take_n(13)
    middle_ref, first_ref, mixt_ref, linv_ref, pring, ering = take_n(6)
    rsems, free, lsems = take_n(3)
    assert not refs
    s = pl.program_id(0)
    mols, slots = types_ref.shape[0], types_ref.shape[2]
    groups = dl.shape[1]
    heads = groups * 8
    width = wo.shape[0]
    hidden = wuhi.shape[1]
    rows = mols * slots
    types = plan["types"]
    last = mols * groups - 1
    at = Place(plan["dpbits"])
    core, xbit = ("tensor", 0), ("tensor", 1)
    dpbits = [("dp", i) for i in range(plan["dpbits"])]
    wide = [core, xbit] + dpbits
    jobs, segments, points = plan["jobs"], plan["segments"], plan["points"]
    chunks = plan["chunks"]
    fcols = width // chunks

    tiles = [(r, c) for r in range(rows // 128) for c in range(hidden // 128)]

    across = hidden // 128

    def keep(base, b, x, top=0):
        for i, (r, c) in enumerate(tiles):
            if r < x.shape[0] // 128:
                gpair[0, base + b * len(tiles) + top * across + i] = x[r * 128:(r + 1) * 128, c * 128:(c + 1) * 128]

    def kept(base, b, top=0, n=rows // 128):
        parts = [gpair[0, base + b * len(tiles) + top * across + i] for i in range(n * across)]
        return jnp.concatenate([jnp.concatenate(parts[r * across:(r + 1) * across], 1) for r in range(n)], 0)

    ACT, DACT = 0, 4 * len(tiles)
    slot = [0]

    def swap(src, dst, stage):
        slot[0] += 1
        return Exchange(at, lambda: src, lambda: dst, rsems, slot[0] - 1, stage)

    hrows = rows // 2
    hpart = [pl.ds(i * hrows, hrows) for i in range(2)]
    n_core = swap(normed2_any, gath.at[1], core)
    n_x = [swap(normed2_any.at[h], gath.at[2, h], xbit) for h in hpart]
    n_diag = [swap(gath.at[2, h], gath.at[3, h], core) for h in hpart]
    dn_core = swap(pn.at[1], rsn.at[0], core)
    dn_diag = [swap(pn.at[3, h], rsn.at[1, h], core) for h in hpart]
    dn_x = [swap(pn.at[2, h], rsn.at[2, h], xbit) for h in hpart]
    dd_core = swap(pd.at[1], rsd.at[0], core)
    dd_diag = swap(pd.at[3], rsd.at[1], core)
    dd_x = swap(pd.at[2], rsd.at[2], xbit)

    def make(buf, res, recv, nrows, stages):
        def done():
            res[...] = buf[...]
        job = Job(at, buf, recv, rsems, free, slot[0], nrows, stages, done)
        slot[0] += job.slots
        return job

    total_job = make(tbuf, tres, trecv, 8, wide)
    running = {}
    place = {"e": 0, "o": 0, "f": 0}
    for name, (kind, index, first_row, nrows, stages) in jobs.items():
        if kind == "s":
            running[name] = make(sbuf, sres, srecv, nrows, stages)
        elif kind == "b":
            running[name] = make(bbuf, bres, brecv, nrows, stages)
        else:
            need = job_need(nrows, stages)[0]
            if kind == "f":
                buf, res, recv = fbuf.at[index], fres.at[index], frecv
            else:
                buf, res, recv = {"e": (ebuf, eres, erecv), "o": (obuf, ores, orecv)}[kind]
            running[name] = make(buf.at[pl.ds(first_row, nrows)], res.at[pl.ds(first_row, nrows)], recv.at[pl.ds(place[kind], need)], nrows, stages)
            place[kind] += need
    assert slot[0] == plan["slots"], slot[0]
    half = width // 2

    def n_sum(i):
        dn_diag[i].wait()
        pn[2, hpart[i], :] = pn[2, hpart[i], :] + rsn[1, hpart[i], :]
        dn_x[i].start()

    def n_end():
        dn_core.wait()
        dn_x[0].wait()
        dn_x[1].wait()

    def d_begin():
        dd_diag.start()
        dd_core.start()

    def d_sum():
        dd_diag.wait()
        pd[2] = pd[2] + rsd[1]
        dd_x.start()

    def d_end():
        dd_core.wait()
        dd_x.wait()
        outv[...] = middle_ref[...] + bdown_ref[...] + (pd[0] + (rsd[0] + rsd[2]))

    running["n"] = Actions(dn_diag[1].start, functools.partial(n_sum, 1), n_end)
    running["d"] = Actions(d_begin, d_sum, d_end)

    cot_load = [pltpu.make_async_copy(cot_refs[b], cots.at[b], lsems.at[b]) for b in range(4)]
    piece = width // rows
    up_load = [pltpu.make_async_copy(wup_any.at[pl.ds(i * rows, rows)], pn.at[i], lsems.at[4 + i]) for i in range(piece)]
    down_load = [pltpu.make_async_copy(wdown_any.at[pl.ds(i * rows, rows)], pn.at[2 + i], lsems.at[6 + i]) for i in range(piece)]
    load = [pltpu.make_async_copy(a, b, lsems.at[8 + i]) for i, (a, b) in enumerate(((wo_any, wo), (wq_any, wq), (wk_any, wk), (wv_any, wv)))]
    own_load = pltpu.make_async_copy(normed2_any, gath.at[0], lsems.at[12])
    held = (first_ref, middle_ref, qhi, qlo, khi, klo, vhi, vlo, mixt_ref, linv_ref)
    held_load = [pltpu.make_async_copy(a, b, lsems.at[13 + i]) for i, (a, b) in enumerate(zip(held_any, held))]
    depth = pring.shape[0]

    def ring(step):
        which = lax.rem(step, depth)
        mol, first_head = lax.rem(step, mols), lax.div(step, mols) * 8
        return [pltpu.make_async_copy(a.at[mol, pl.ds(first_head, 8)], r.at[which], lsems.at[23 + i * depth + which])
                for i, (a, r) in enumerate(((pair_any, pring), (e_any, ering)))]

    def seg_ffn():
        barrier = pltpu.get_barrier_semaphore()
        for stage in wide:
            pl.semaphore_signal(barrier, inc=1, device_id=at.partners[stage], device_id_type=LOGICAL)
        pl.semaphore_wait(barrier, len(wide))
        for copy in n_x:
            copy.start()
        n_core.start()
        for copy in down_load + cot_load + up_load + [own_load] + held_load + load:
            copy.start()
        for step in range(depth - 1):
            for copy in ring(step):
                copy.start()
        square = jnp.zeros((1, 1), F32)
        for m in range(mols):
            f = jnp.full((1, 1), len_ref[m], jnp.int32).astype(F32)
            square = square + f * f
        tbuf[...] = jnp.broadcast_to(square, tbuf.shape)
        total_job.tick(0)
        bbuf[...] = jnp.zeros_like(bbuf)
        sbuf[...] = jnp.zeros_like(sbuf)
        for copy in down_load:
            copy.wait()
        for i in range(piece):
            part = pl.ds(i * rows, rows)
            wdhi[part, :], wdlo[part, :] = split(pn[2 + i])
        for copy in cot_load + up_load:
            copy.wait()
        for i in range(piece):
            part = pl.ds(i * rows, rows)
            wuhi[part, :], wulo[part, :] = split(pn[i])
        total_job.tick(1)

        def p1(b, carry):
            hi, lo = split(cots[b])
            keep(DACT, b, mm3_nt(hi, lo, wdhi[...], wdlo[...]))
            return carry

        lax.fori_loop(0, 4, p1, 0)
        own_load.wait()
        n_core.wait()
        total_job.tick(2)

        def p2(b, top=0, n=rows // 128):
            part = pl.ds(top * 128, n * 128)
            hi, lo = split(gath[b, part, :])
            upper = mm3_nn(hi, lo, wuhi[...], wulo[...]) + bup_ref[...]
            a, slope = gelu_and_slope(upper)
            keep(ACT, b, a, top)
            du = kept(DACT, b, top, n) * slope
            dhi, dlo = split(du)
            duhi[b, part, :] = dhi
            dulo[b, part, :] = dlo
            bbuf[...] = bbuf[...] + jnp.broadcast_to(jnp.sum(du, axis=0, keepdims=True), bbuf.shape)
            pn[b, part, :] = mm3_nt(dhi, dlo, wuhi[...], wulo[...])

        def p2_loop(b, carry):
            p2(b)
            return carry

        lax.fori_loop(0, 2, p2_loop, 0)
        dn_core.start()
        first_work()
        n = hrows // 128
        for i in range(2):
            n_x[i].wait()
            n_diag[i].start()
            p2(2, i * n, n)
            n_diag[i].wait()
            p2(3, i * n, n)
            total_job.tick(3 + i)
            if i == 0:
                dn_diag[0].start()
                n_sum(0)
        running["n"].tick(0)
        running["b"].tick(0)
        for k in range(5, total_job.ticks):
            total_job.tick(k)

    def first_work():
        for copy in held_load:
            copy.wait()
        first = first_ref[...]
        cen = first - jnp.mean(first, axis=-1, keepdims=True)
        rstd = lax.rsqrt(jnp.mean(cen * cen, axis=-1, keepdims=True) + EPSILON)
        normed = cen * rstd * gain_ref[...] + shift_ref[...]
        for m in range(mols):
            nt[:, m * slots:(m + 1) * slots] = jnp.transpose(normed[m * slots:(m + 1) * slots])
        dn1[...] = jnp.zeros_like(dn1)
        energy[...] = jnp.zeros_like(energy)
        for k in range(2):
            lax.fori_loop(0, 2, functools.partial(weight_part, k), 0)

    def down_part(b, carry):
        hi, lo = split(kept(ACT, b))
        pd[b] = mm3_nn(hi, lo, wdhi[...], wdlo[...])
        return carry

    def weight_part(k, b, carry):
        part = slice((k % 2) * half, (k % 2 + 1) * half)
        left = kept(ACT, b)[:, part] if k < 2 else gath[b, :, part]
        ahi, alo = split(jnp.transpose(left))
        if k < 2:
            chi, clo = split(cots[b])
        else:
            chi, clo = duhi[b], dulo[b]
        g = mm3_nn(ahi, alo, chi, clo)
        to = pl.ds(k * half, half)

        @pl.when(b == 0)
        def _():
            ebuf[to, :] = g

        @pl.when(b > 0)
        def _():
            ebuf[to, :] = ebuf[to, :] + g
        return carry

    def seg_e(k):
        lax.fori_loop(2 if k < 2 else 0, 4, functools.partial(weight_part, k), 0)
        q = plan["ne"] // 4
        for i in range(k * q, (k + 1) * q):
            running["e%d" % i].tick(0)

    def seg_down():
        lax.fori_loop(0, 4, down_part, 0)
        running["d"].tick(0)

    def small(i, value):
        sbuf[types + i:types + i + 1, :] = value

    def seg_pro1():
        mid = middle_ref[...]
        cen = mid - jnp.mean(mid, axis=-1, keepdims=True)
        rstd = lax.rsqrt(jnp.mean(cen * cen, axis=-1, keepdims=True) + EPSILON)
        xhat = cen * rstd
        c = pn[0] + (rsn[0] + rsn[2])
        small(0, jnp.sum(c * xhat, axis=0, keepdims=True))
        small(1, jnp.sum(c, axis=0, keepdims=True))
        cot = cots[0]
        small(2, jnp.sum(cot, axis=0, keepdims=True))
        ce = c * fgain_ref[...]
        dmiddle = cot + rstd * (ce - jnp.mean(ce, axis=-1, keepdims=True) - xhat * jnp.mean(ce * xhat, axis=-1, keepdims=True))
        dmid[...] = dmiddle
        small(3, jnp.sum(dmiddle, axis=0, keepdims=True))
        for copy in load:
            copy.wait()
        dhi, dlo = split(dmiddle)
        mhi, mlo = split(jnp.concatenate([mixt_ref[m] for m in range(mols)], 1))
        obuf[...] = mm3_nn(mhi, mlo, dhi, dlo)
        for i in range(plan["no"]):
            running["o%d" % i].tick(0)

    def seg_pro2():
        wohi, wolo = split(wo[...])
        dhi, dlo = split(dmid[...])
        dm = mm3_nt(dhi, dlo, wohi, wolo)
        lane = lax.broadcasted_iota(jnp.int32, (slots, 128), 1)
        rowi = lax.broadcasted_iota(jnp.int32, (slots, slots), 0)
        coli = lax.broadcasted_iota(jnp.int32, (slots, slots), 1)
        twice = 2.0 / (heads * tres[0:1, 0:slots])
        for m in range(mols):
            length = len_ref[m]
            maskc[m] = jnp.where(jnp.logical_and(rowi < length, coli < length), twice, 0.0)
            dmt = jnp.transpose(dm[m * slots:(m + 1) * slots]) * linv_ref[m]
            dmhi[m], dmlo[m] = split(dmt)
            prod = dmt * mixt_ref[m]
            delta = jnp.sum(prod.reshape(heads, 8, slots), axis=1)
            for g in range(groups):
                d8 = -delta[g * 8:(g + 1) * 8]
                x = jnp.concatenate([dmt[g * 64:(g + 1) * 64], d8, d8, jnp.zeros((48, slots), F32)], 0)
                y = jnp.transpose(x)
                yhi = y.astype(BF).astype(F32)
                ylo = y - yhi
                dl[m, g, :, 0:128] = jnp.where(lane < 64, yhi, pltpu.roll(ylo, 64, 1)).astype(BF)
                dl[m, g, :, 128:256] = jnp.where(lane < 72, yhi, ylo).astype(BF)

    def seg_chunk(c):
        part = slice(c * fcols, (c + 1) * fcols)
        nhi, nlo = split(nt[...])
        for i, t_ref in enumerate((dqt, dkt, dvt)):
            thi, tlo = split(jnp.concatenate([t_ref[mm, part, :] for mm in range(mols)], 1))
            fbuf[c, i * width:(i + 1) * width, :] = mm3_nt(nhi, nlo, thi, tlo)
        for h in range(plan["fs"]):
            running["f%d_%d" % (c, h)].tick(0)
        acc = dn1[...]
        for i, (t_ref, w) in enumerate(((dqt, wq), (dkt, wk), (dvt, wv))):
            nat = jnp.concatenate([jnp.transpose(t_ref[mm, part, :]) for mm in range(mols)], 0)
            if i != 1:
                r = types + (4 if i == 0 else 5)
                sbuf[r:r + 1, part] = jnp.sum(nat, axis=0, keepdims=True)
            ahi, alo = split(nat)
            whi, wlo = split(w[:, part])
            acc = acc + mm3_nt(ahi, alo, whi, wlo)
        dn1[...] = acc

    def seg_end():
        first = first_ref[...]
        cen = first - jnp.mean(first, axis=-1, keepdims=True)
        rstd = lax.rsqrt(jnp.mean(cen * cen, axis=-1, keepdims=True) + EPSILON)
        xhat = cen * rstd
        dn = dn1[...]
        small(6, jnp.sum(dn * xhat, axis=0, keepdims=True))
        small(7, jnp.sum(dn, axis=0, keepdims=True))
        ge = dn * gain_ref[...]
        gat = dmid[...] + rstd * (ge - jnp.mean(ge, axis=-1, keepdims=True) - xhat * jnp.mean(ge * xhat, axis=-1, keepdims=True))
        gatv[...] = gat
        acc = None
        for mm in range(mols):
            one = (lax.broadcasted_iota(jnp.int32, (types, slots), 0) == types_ref[mm]).astype(F32).astype(BF)
            for bits in split3(gat[mm * slots:(mm + 1) * slots]):
                part = dot(one, bits)
                acc = part if acc is None else acc + part
        sbuf[0:types, :] = acc
        total = jnp.sum(jnp.sum(energy[...], axis=0, keepdims=True), axis=1, keepdims=True) * 0.5
        small(8, jnp.broadcast_to(total, (1, width)))
        running["s"].tick(0)

    work = {"ffn": seg_ffn, "e": seg_e, "down": seg_down, "pro1": seg_pro1, "pro2": seg_pro2, "chunk": seg_chunk, "end": seg_end}
    before, after = [], {}
    step_now = None
    for (name, _, _, _), ticks in zip(segments, points):
        if name[0] == "step":
            step_now = name[1]
        else:
            to = before if step_now is None else after.setdefault(step_now, [])
            to.append(functools.partial(work[name[0]], *name[1:]))
        to = before if step_now is None else after.setdefault(step_now, [])
        to += [functools.partial(running[job].tick, k) for job, k in ticks]

    @pl.when(s == 0)
    def _():
        for fn in before:
            fn()

    g = s // mols
    m = s % mols
    lhs = dl[m, g]
    which = lax.rem(s, depth)
    for copy in ring(s):
        copy.wait()

    @pl.when(s + depth - 1 <= last)
    def _():
        for copy in ring(s + depth - 1):
            copy.start()

    sub = lax.broadcasted_iota(jnp.int32, (16, 128), 0)
    z = jnp.zeros((16, 256), BF)
    zero16 = jnp.zeros((16, 128), BF)
    mc = maskc[m]
    en = energy[...]
    for p in range(4):
        row = pl.multiple_of(g * 64 + 16 * p, 16)
        rows16 = pl.ds(row, 16)

        def blk(x):
            x = x.astype(F32)
            a = jnp.where(sub < 8, x, 0.0).astype(BF)
            b = jnp.where(sub >= 8, x, 0.0).astype(BF)
            return jnp.concatenate([a, b], axis=1)
        bhi, blo = blk(vhi[m, rows16, :]), blk(vlo[m, rows16, :])
        sel = jnp.concatenate([jnp.where(sub % 8 == 2 * p, 1.0, 0.0), jnp.where(sub % 8 == 2 * p + 1, 1.0, 0.0)], axis=1).astype(BF)
        rws = [bhi if i == p else z for i in range(4)]
        rws += rws
        rws += [blo if i == p else z for i in range(4)]
        rws += [sel, z, z, z]
        dp = dot(lhs, jnp.concatenate(rws, axis=0))
        gs = []
        es = []
        for hf in range(2):
            both = ering[which, 2 * p + hf]
            es.append(both)
            e = both[:, 0:128].astype(F32) + both[:, 128:256].astype(F32)
            logits = pring[which, 2 * p + hf]
            t = logits * mc
            en = en + t * logits
            gp = e * dp[:, hf * 128:(hf + 1) * 128] + t
            gpair[m, g * 8 + 2 * p + hf] = gp
            gs.append(split(gp))

        def rows_lhs(hi, lo):
            return jnp.concatenate([jnp.concatenate([hi, hi], 1), jnp.concatenate([lo, zero16], 1)], 0)

        def take(out):
            acc = out[0:16] + out[16:32]
            return jnp.concatenate([acc[0:8, 0:128], acc[8:16, 128:256]], 0)
        ecol = jnp.concatenate([jnp.concatenate([es[0][:, 0:128], es[1][:, 0:128]], 1), jnp.concatenate([es[0][:, 128:256], es[1][:, 128:256]], 1)], 0)
        dvt[m, rows16, :] = take(dot(rows_lhs(dmhi[m, rows16, :], dmlo[m, rows16, :]), ecol))
        gcol = jnp.concatenate([jnp.concatenate([gs[0][0], gs[1][0]], 1), jnp.concatenate([gs[0][1], gs[1][1]], 1)], 0)
        dkt[m, rows16, :] = take(dot(rows_lhs(qhi[m, rows16, :], qlo[m, rows16, :]), gcol))
        grow = jnp.concatenate([jnp.concatenate(gs[0], 1), jnp.concatenate(gs[1], 1)], 0)
        dqt[m, rows16, :] = take(dot_nt(rows_lhs(khi[m, rows16, :], klo[m, rows16, :]), grow)) * (8 ** -0.5)
    energy[...] = en

    for moment in sorted(after):
        def body(moment=moment):
            for fn in after[moment]:
                fn()
        pl.when(s == moment)(body)


CONFIG = dict(ne=8, ch=4, fs=2, no=2, eo=[0, 0, 2, 0, 0, 0, 0, 0], fo=[2, 0, 0, 0, 2, 2, 1, 5], oo=[2, 2], so=2, pos=[-2, -2, 15, -1, -2])


def main_call(mesh, lengths, types, normed2, cots, held, gain, shift, fgain, bup, bdown,
              wup, wdown, wq, wk, wv, wo, pair, e, ntypes):
    mols, slots = types.shape
    rows, width = normed2.shape
    heads = pair.shape[1]
    groups = heads // 8
    hidden = wup.shape[1]
    dp = mesh.shape["dp"]
    dpbits = dp.bit_length() - 1
    assert (1 << dpbits) == dp and mesh.shape["tensor"] == 4
    small = -(-(ntypes + 9) // 64) * 64
    config = CONFIG if dpbits <= 3 else dict(ne=4, ch=1, fs=1, no=1, eo=[0] * 4, fo=[0], oo=[0], so=0, pos=[-2, -2, -2, -2, -2])
    jobs, segments, points = make_plan(config, dpbits, mols, groups, width, hidden, small)
    chunks = config["ch"]
    fcols = width // chunks
    needs = {"e": 0, "o": 0, "f": 0, "s": 0, "b": 0}
    stages = stages_of("CXYZW", dpbits)
    t_need = job_need(8, stages)
    nslots = 13 + t_need[1]
    for kind, index, first_row, nrows, order in jobs.values():
        need = job_need(nrows, order)
        needs[kind] += need[0]
        nslots += need[1]
    plan = dict(dpbits=dpbits, chunks=chunks, types=ntypes, slots=nslots, jobs=jobs, segments=segments, points=points,
                ne=config["ne"], no=config["no"], fs=config["fs"])
    V = pltpu.VMEM
    one = lambda shape: pl.BlockSpec(shape, lambda s: (0,) * len(shape), pipeline_mode=pl.Buffered(1))
    any_ = pl.BlockSpec(memory_space=pl.ANY)
    smem = pl.BlockSpec(memory_space=pltpu.SMEM)
    vmem = pl.BlockSpec(memory_space=pltpu.VMEM)
    vec = lambda v: v.reshape(1, -1)
    tt = (mols, width, slots)
    rw = (rows, width)
    in_specs = [smem, one((mols, 1, slots))] + [any_] * 15 + \
        [one((1, width))] * 3 + [one((1, hidden)), one((1, width))] + [any_] * 8
    ww = (width, width)
    ff = (width + hidden, width)
    outs = [V(pair.shape, F32), V(rw, F32), V(rw, F32), V(ff, F32), V(ww, F32), V((chunks, 3 * width, fcols), F32), V((small, width), F32), V((8, hidden), F32)]
    four = (4, rows, width)
    scratch = [V((mols, groups, slots, 256), BF)] + [V(tt, BF)] * 8 + [V(tt, F32)] * 3 + [V((mols, slots, slots), F32), V(rw, F32), V((slots, slots), F32)]
    scratch += [V(ww, F32)] * 4 + [V((width, hidden), BF)] * 2 + [V((hidden, width), BF)] * 2
    scratch += [V(four, F32)] * 2 + [V(four, BF)] * 2 + [V(four, F32)] * 2 + [V((3, rows, width), F32)] * 2 + [V((width, rows), F32), V(rw, F32)]
    scratch += [V(ff, F32), V((needs["e"], width), F32), V(ww, F32), V((needs["o"], width), F32)]
    scratch += [V((chunks, 3 * width, fcols), F32), V((needs["f"], fcols), F32), V((small, width), F32), V((needs["s"], width), F32)]
    scratch += [V((8, 128), F32)] * 2 + [V((t_need[0], 128), F32), V((8, hidden), F32), V((needs["b"], hidden), F32)]
    scratch += [V(rw, F32)] * 2 + [V(tt, F32)] * 2 + [V((DEPTH, 8, slots, slots), F32), V((DEPTH, 8, slots, 2 * slots), BF)]
    scratch += [pltpu.SemaphoreType.DMA((2, nslots)), pltpu.SemaphoreType.REGULAR((nslots,)), pltpu.SemaphoreType.DMA((23 + 2 * DEPTH,))]
    return pl.pallas_call(functools.partial(main_kernel, plan), out_shape=outs, grid=(mols * groups,), in_specs=in_specs, out_specs=[vmem] * 8,
        scratch_shapes=scratch,
        compiler_params=pltpu.CompilerParams(vmem_limit_bytes=VLIMIT, dimension_semantics=("arbitrary",), collective_id=0, has_side_effects=True),
        name="feed_forward_and_backward",
    )(lengths, types.reshape(mols, 1, slots), normed2, *cots, *held, vec(gain), vec(shift), vec(fgain), vec(bup), vec(bdown),
      wup, wdown, wq, wk, wv, wo, pair, e)


DEPTH = 4
VLIMIT = 47 * 1024 * 1024
SMALL_ROWS = (0, 1, 2, 3, 4, 5, 6, 7)


def finish_kernel(types, gpair, outv, gatv, eres, ores, fres, sres, bres, *refs):
    refs = list(refs)
    gp_out, atom_out, gatoms_out, gdown_out, gup_out, gwo_out, gwq_out, gwk_out, gwv_out, table_out = [refs.pop(0) for _ in range(10)]
    rows_out = [refs.pop(0) for _ in range(len(SMALL_ROWS))]
    gbup_out, pen_out, sems = refs
    width = outv.shape[1]
    hidden = eres.shape[0] - width
    copies = []

    def go(src, dst):
        copy = pltpu.make_async_copy(src, dst, sems.at[len(copies)])
        copy.start()
        copies.append(copy)

    for m in range(gpair.shape[0]):
        for h in range(0, gpair.shape[1], 16):
            go(gpair.at[m, pl.ds(h, 16)], gp_out.at[m, pl.ds(h, 16)])
    go(eres.at[pl.ds(0, hidden)], gdown_out)
    go(eres.at[pl.ds(hidden, width)], gup_out)
    go(ores, gwo_out)
    chunks, _, fcols = fres.shape
    for c in range(chunks):
        for j, out in enumerate((gwq_out, gwk_out, gwv_out)):
            go(fres.at[c, pl.ds(j * width, width)], out.at[:, pl.ds(c * fcols, fcols)])
    go(outv, atom_out)
    go(gatv, gatoms_out)
    go(sres.at[pl.ds(0, types)], table_out)
    for i, out in zip(SMALL_ROWS, rows_out):
        out[...] = sres[types + i, :]
    gbup_out[...] = bres[0, :]
    pen_out[0, 0] = jnp.sum(sres[types + 8:types + 9, 0:1])
    for copy in copies:
        copy.wait()


def finish(types, parts, width, hidden):
    gpair, outv, gatv, eres, ores, fres, sres, bres = parts
    S = jax.ShapeDtypeStruct
    any_ = pl.BlockSpec(memory_space=pl.ANY)
    vmem = pl.BlockSpec(memory_space=pltpu.VMEM)
    shapes = [gpair.shape, outv.shape, gatv.shape, (hidden, width), (width, hidden)] + [(width, width)] * 4 + [(types, width)]
    outs = [S(shape, F32) for shape in shapes] + [S((width,), F32)] * len(SMALL_ROWS) + [S((hidden,), F32), S((1, 1), F32)]
    ncopies = gpair.shape[0] * gpair.shape[1] // 16 + 6 + 3 * fres.shape[0]
    return pl.pallas_call(functools.partial(finish_kernel, types), out_shape=outs, in_specs=[vmem] * 8,
        out_specs=[any_] * 10 + [vmem] * (len(SMALL_ROWS) + 1) + [pl.BlockSpec(memory_space=pltpu.SMEM)],
        scratch_shapes=[pltpu.SemaphoreType.DMA((ncopies,))], compiler_params=pltpu.CompilerParams(vmem_limit_bytes=4 * 1024 * 1024),
        name="finish")(*parts)


def local(mesh, atom_types, lengths, atom_feats, pair_bias, out_cotangent, type_table, norm_gain, norm_shift, w_query, b_query,
          w_key, w_value, b_value, w_out, b_out, ffn_gain, ffn_shift, w_up, b_up, w_down, b_down):
    tensor = mesh.shape["tensor"]
    cots = [out_cotangent] + [lax.ppermute(out_cotangent, "tensor", [(i, i ^ d) for i in range(tensor)]) for d in (1, 2, 3)]
    pair_out, e, first, qhi, qlo, khi, klo, vhi, vlo, mixt, linv, middle, normed2 = attention_forward(
        lengths, atom_types, atom_feats, type_table, norm_gain, norm_shift, w_query, b_query, w_key, w_value, b_value, w_out, b_out,
        ffn_gain, ffn_shift, pair_bias)
    types = type_table.shape[0]
    parts = main_call(
        mesh, lengths, atom_types, normed2, cots, (first, middle, qhi, qlo, khi, klo, vhi, vlo, mixt, linv), norm_gain, norm_shift, ffn_gain, b_up, b_down,
        w_up, w_down, w_query, w_key, w_value, w_out, pair_out, e, types)
    (grad_pair, atom_out, grad_atoms, gwdown, gwup, gwo, gwq, gwk, gwv, table, g_fgain, g_fshift, g_bdown, g_bout, g_bq, g_bv, g_gain, g_shift,
     gbup, penalty) = finish(types, parts, w_up.shape[0], w_up.shape[1])
    return (atom_out, pair_out, penalty.reshape(()), grad_atoms, grad_pair, table, g_gain, g_shift, gwq, g_bq, gwk, gwv, g_bv,
            gwo, g_bout, g_fgain, g_fshift, gwup, gbup, gwdown, g_bdown)


def solution(mesh):
    in_specs = (
        P(("dp", "tensor"), None),
        P(("dp", "tensor")),
        P(("dp", "tensor"), None),
        P(("dp", "tensor"), None, None, None),
        P(("dp", "tensor"), None),
        P(),
        P(),
        P(),
        P(),
        P(),
        P(),
        P(),
        P(),
        P(),
        P(),
        P(),
        P(),
        P(None, "tensor"),
        P("tensor"),
        P("tensor", None),
        P(),
    )
    out_specs = (
        P(("dp", "tensor"), None),
        P(("dp", "tensor"), None, None, None),
        P(),
        P(("dp", "tensor"), None),
        P(("dp", "tensor"), None, None, None),
        P(),
        P(),
        P(),
        P(),
        P(),
        P(),
        P(),
        P(),
        P(),
        P(),
        P(),
        P(),
        P(None, "tensor"),
        P("tensor"),
        P("tensor", None),
        P(),
    )
    return jax.shard_map(functools.partial(local, mesh), mesh=mesh, in_specs=in_specs, out_specs=out_specs, check_vma=False)
```

```python
import functools, math
import jax, jax.numpy as jnp
from jax import lax
from jax.experimental import pallas as pl
from jax.experimental.pallas import tpu as pltpu
from jax.sharding import PartitionSpec as P
F32=jnp.float32; BF=jnp.bfloat16
EPSILON=1e-5
SPAN=2

def split(x):
    hi = x.astype(BF)
    lo = (x - hi.astype(F32)).astype(BF)
    return hi, lo

def split3(x):
    hi = x.astype(BF)
    r = x - hi.astype(F32)
    mid = r.astype(BF)
    lo = (r - mid.astype(F32)).astype(BF)
    return hi, mid, lo

def dot(a, b):
    return jnp.dot(a, b, preferred_element_type=F32)

def dot_nt(a, b):
    return lax.dot_general(a, b, (((1,), (1,)), ((), ())), preferred_element_type=F32)

def mm3(a, bhi, blo):
    ahi, alo = split(a)
    return dot(ahi, bhi) + (dot(ahi, blo) + dot(alo, bhi))

def fwd_kernel(len_ref, types_ref, feats_ref, table_ref, gain_ref, shift_ref, wq_ref, bq_ref, wk_ref, wv_ref, bv_ref,
               wo_ref, bo_ref, fgain_ref, fshift_ref, bias_ref,
               pair_ref, e_ref, first_ref, qthi, qtlo, kthi, ktlo, vthi, vtlo, mixt_ref, linv_ref, middle_ref, normed_ref,
               ql, *, span):
    s = pl.program_id(0)
    mols, slots = types_ref.shape[0], types_ref.shape[2]
    groups = ql.shape[1]
    @pl.when(s == 0)
    def _():
        tab = split3(table_ref[...])
        types = table_ref.shape[0]
        for m in range(mols):
            ids = types_ref[m]
            oneT = (lax.broadcasted_iota(jnp.int32, (slots, slots), 0) == ids).astype(F32)
            one = jnp.transpose(oneT)[:, :types].astype(BF)
            rows = pl.ds(m*slots, slots)
            first = feats_ref[rows, :] + (dot(one, tab[0]) + (dot(one, tab[1]) + dot(one, tab[2])))
            first_ref[rows, :] = first
        first = first_ref[...]
        cen = first - jnp.mean(first, axis=-1, keepdims=True)
        var = jnp.mean(cen*cen, axis=-1, keepdims=True)
        normed = cen * lax.rsqrt(var + EPSILON) * gain_ref[...] + shift_ref[...]
        nhi, nlo = split(normed)
        def proj(w_ref):
            whi, wlo = split(w_ref[...])
            return dot(nhi, whi) + (dot(nhi, wlo) + dot(nlo, whi))
        q = (proj(wq_ref) + bq_ref[...]) * (8 ** -0.5)
        k = proj(wk_ref)
        v = proj(wv_ref) + bv_ref[...]
        lane = lax.broadcasted_iota(jnp.int32, (slots, 128), 1)
        for m in range(mols):
            sl = slice(m*slots, (m+1)*slots)
            qm = q[sl]
            qthi[m], qtlo[m] = split(jnp.transpose(qm))
            kt = jnp.transpose(k[sl])
            kthi[m], ktlo[m] = split(kt)
            vt = jnp.transpose(v[sl])
            vthi[m], vtlo[m] = split(vt)
            for t in range(groups // 2):
                tile = qm[:, t*128:(t+1)*128]
                rolled = pltpu.roll(tile, 64, 1)
                for half in range(2):
                    dup = jnp.where(lane < 64, tile, rolled) if half == 0 else jnp.where(lane < 64, rolled, tile)
                    hi, lo = split(dup)
                    hi32, lo32 = hi.astype(F32), lo.astype(F32)
                    ql[m, 2*t+half, :, 0:128] = jnp.where(lane < 64, hi32, lo32).astype(BF)
                    ql[m, 2*t+half, :, 128:256] = jnp.where(lane < 64, hi32, 0.0).astype(BF)
    per = groups // span
    m = s // per
    length = len_ref[m]
    col_live = lax.broadcasted_iota(jnp.int32, (slots, slots), 1) < length
    sub = lax.broadcasted_iota(jnp.int32, (16, 128), 0)
    zero16 = jnp.zeros((16, 128), BF)
    ones = jnp.ones((16, 256), BF)
    def one(i, carry):
        g = (s % per) * span + i
        h0 = i * 8
        lhs = ql[m, g]
        for p in range(4):
            row = pl.multiple_of(g*64 + 16*p, 16)
            khi = kthi[m, pl.ds(row, 16), :].astype(F32)
            klo = ktlo[m, pl.ds(row, 16), :].astype(F32)
            def blk(x):
                a = jnp.where(sub < 8, x, 0.0).astype(BF)
                b = jnp.where(sub >= 8, x, 0.0).astype(BF)
                return jnp.concatenate([a, b], axis=1)
            bhi, blo = blk(khi), blk(klo)
            z = jnp.concatenate([zero16, zero16], axis=1)
            rows = [bhi if i == p else z for i in range(4)]
            rows += rows
            rows += [blo if i == p else z for i in range(4)]
            rows += [z]*4
            rhs = jnp.concatenate(rows, axis=0)
            lg = dot(lhs, rhs)
            ehl = []
            for half in range(2):
                logits = lg[:, half*128:(half+1)*128] + bias_ref[0, h0 + 2*p+half].astype(F32)
                pair_ref[0, h0 + 2*p+half] = logits
                masked = jnp.where(col_live, logits, -1e30)
                top = jnp.max(masked, axis=1, keepdims=True)
                e = jnp.exp(masked - top)
                hi, lo = split(e)
                both = jnp.concatenate([hi, lo], axis=1)
                e_ref[0, h0 + 2*p+half] = both
                ehl.append(both)
            vhi = vthi[m, pl.ds(row, 16), :]
            vlo = vtlo[m, pl.ds(row, 16), :]
            lv = jnp.concatenate([jnp.concatenate([vhi, vhi], 1), jnp.concatenate([vlo, zero16], 1), ones], 0)
            out = dot_nt(lv, jnp.concatenate(ehl, 0))
            acc = out[0:16] + out[16:32]
            sums = out[32:48]
            inv = 1.0 / jnp.concatenate([sums[0:8, 0:128], sums[8:16, 128:256]], 0)
            linv_ref[m, pl.ds(row, 16), :] = inv
            mixt_ref[m, pl.ds(row, 16), :] = jnp.concatenate([acc[0:8, 0:128], acc[8:16, 128:256]], 0) * inv
        return carry

    if span == 1:
        one(0, 0)
    else:
        lax.fori_loop(0, span, one, 0)
    @pl.when(s == mols*groups // span - 1)
    def _():
        mix = jnp.concatenate([jnp.transpose(mixt_ref[m]) for m in range(mols)], 0)
        whi, wlo = split(wo_ref[...])
        mid = first_ref[...] + (mm3(mix, whi, wlo) + bo_ref[...])
        middle_ref[...] = mid
        mcen = mid - jnp.mean(mid, axis=-1, keepdims=True)
        mvar = jnp.mean(mcen*mcen, axis=-1, keepdims=True)
        normed_ref[...] = mcen * lax.rsqrt(mvar + EPSILON) * fgain_ref[...] + fshift_ref[...]

def attention_forward(lengths, types, feats, table, gain, shift, wq, bq, wk, wv, bv, wo, bo, fgain, fshift, bias):
    mols, slots = types.shape
    width = feats.shape[1]
    heads = bias.shape[1]
    groups = heads // 8
    rows = mols*slots
    full = lambda shape: pl.BlockSpec(shape, lambda s: (0,)*len(shape))
    vec = lambda v: v.reshape(1, -1)
    outs = [jax.ShapeDtypeStruct((mols, heads, slots, slots), F32),
            jax.ShapeDtypeStruct((mols, heads, slots, 2*slots), BF),
            jax.ShapeDtypeStruct((rows, width), F32)] + [jax.ShapeDtypeStruct((mols, width, slots), BF)]*6 + [jax.ShapeDtypeStruct((mols, width, slots), F32)]*2 + [jax.ShapeDtypeStruct((rows, width), F32)]*2
    blk = lambda w: pl.BlockSpec((1, 8*SPAN, slots, w), lambda s: (s // (groups // SPAN), s % (groups // SPAN), 0, 0))
    in_specs = [pl.BlockSpec(memory_space=pltpu.SMEM), full((mols,1,slots)), full((rows,width)), full(table.shape), full((1,width)), full((1,width)),
                full(wq.shape), full((1,width)), full(wk.shape), full(wv.shape), full((1,width)), full(wo.shape), full((1,width)), full((1,width)), full((1,width)), blk(slots)]
    return pl.pallas_call(functools.partial(fwd_kernel, span=SPAN), out_shape=outs, grid=(mols*groups // SPAN,), in_specs=in_specs,
        out_specs=[blk(slots), blk(2*slots), full((rows,width))] + [full((mols,width,slots))]*8 + [full((rows,width))]*2,
        scratch_shapes=[pltpu.VMEM((mols, groups, slots, 256), BF)],
        compiler_params=pltpu.CompilerParams(vmem_limit_bytes=60*1024*1024, dimension_semantics=("arbitrary",)),
        name="attention_forward",
    )(lengths, types.reshape(mols,1,slots), feats, table, vec(gain), vec(shift), wq, vec(bq), wk, wv, vec(bv), wo, vec(bo), vec(fgain), vec(fshift), bias)


LOGICAL = pl.DeviceIdType.LOGICAL


class Place:
    def __init__(self, dpbits):
        tensor, dp = lax.axis_index("tensor"), lax.axis_index("dp")
        me = dp * 4 + tensor
        self.bits, self.partners = {}, {}
        for axis, index, count, stride in (("tensor", tensor, 2, 1), ("dp", dp, dpbits, 4)):
            for bit in range(count):
                value = lax.rem(lax.div(index, 1 << bit), 2)
                self.bits[axis, bit] = value
                self.partners[axis, bit] = me + (1 - 2 * value) * (stride << bit)


class Exchange:
    def __init__(self, at, src, dst, sems, slot, stage, before=None, after=None):
        self.before, self.after = before, after
        self.copy = lambda: pltpu.make_async_remote_copy(
            src_ref=src(), dst_ref=dst(), send_sem=sems.at[0, slot], recv_sem=sems.at[1, slot],
            device_id=at.partners[stage], device_id_type=LOGICAL)

    def start(self):
        if self.before is not None:
            self.before()
        self.copy().start()

    def wait(self):
        self.copy().wait()
        if self.after is not None:
            self.after()


class Pause:
    def __init__(self, wait):
        self.wait = wait

    def start(self):
        pass


class Job:
    def __init__(self, at, buf, recv, sems, free, first_slot, rows, stages, done=None):
        self.done = done
        self.slots = 0
        self.recv_rows = 0
        self.steps = []
        plan = []
        numbers = []
        length = rows
        for stage in stages:
            halve = (length // 2) % 8 == 0
            part = length // 2 if halve else length
            plan.append((stage, halve, length, part, self.recv_rows))
            self.recv_rows += part
            length = part
        halved = [p[0] for p in plan if p[1]]

        def offset(count):
            off, size = 0, rows
            for axis, bit in halved[:count]:
                size //= 2
                off = off + at.bits[axis, bit] * size
            return off if isinstance(off, int) else pl.multiple_of(off, 8)

        depth = 0
        for stage, halve, length, part, place in plan:
            here = depth
            if halve:
                depth += 1

                def src(stage=stage, here=here, part=part):
                    return buf.at[pl.ds(pl.multiple_of(offset(here) + (1 - at.bits[stage]) * part, 8), part)]
            else:
                def src(here=here, part=part):
                    return buf.at[pl.ds(offset(here), part)]

            def dst(place=place, part=part):
                return recv.at[pl.ds(place, part)]

            def add(depth=depth, place=place, part=part, to=buf):
                mine = pl.ds(offset(depth), part)
                to[mine, :] = buf[mine, :] + recv[pl.ds(place, part), :]

            number = first_slot + self.slots

            def tell(number=number, stage=stage):
                pl.semaphore_signal(free.at[number], inc=1, device_id=at.partners[stage], device_id_type=LOGICAL)

            self.steps.append((Exchange(at, src, dst, sems, number, stage, after=tell if halve else None), add))
            numbers.append(number)
            self.slots += 1
        if plan[-1][1]:
            self.steps.append((Pause(lambda number=numbers[-1]: pl.semaphore_wait(free.at[number], 1)), None))
        for (stage, halve, length, part, place), number in zip(reversed(plan), reversed(numbers)):
            if not halve:
                continue

            def freed(number=number):
                pl.semaphore_wait(free.at[number], 1)

            def region(depth=depth, part=part):
                return buf.at[pl.ds(offset(depth), part)]

            if number == numbers[-1]:
                freed = None
            self.steps.append((Exchange(at, region, region, sems, first_slot + self.slots, stage, before=freed), None))
            self.slots += 1
            depth -= 1
        self.ticks = len(self.steps) + 1

    def tick(self, k):
        if k > 0:
            exchange, add = self.steps[k - 1]
            exchange.wait()
            if add is not None:
                add()
        if k < len(self.steps):
            self.steps[k][0].start()
        elif self.done is not None:
            self.done()


class Actions:
    def __init__(self, *functions):
        self.tick = lambda k: functions[k]()


def job_need(rows, stages):
    job = Job(None, None, None, None, None, 0, rows, stages)
    return job.recv_rows, job.slots


ORDERS = ("CXYZW", "CXZWY", "CYXZW", "CYZWX", "CZWXY", "CXZYW", "CZXYW", "CZYXW")
E_ORDERS = ("YZW", "ZWY", "ZYW")


def stages_of(order, dpbits):
    table = {"C": [("tensor", 0)], "X": [("tensor", 1)], "Y": [("dp", i) for i in range(dpbits - 2)],
             "Z": [("dp", dpbits - 2)], "W": [("dp", dpbits - 1)]}
    return [stage for token in order for stage in table[token]]


def stage_cost(stage, size):
    rate = 43.0e3
    if stage is None:
        return [], 1.0 + size
    axis, bit = stage
    if axis == "tensor":
        return ([("core", size / 700e3)], 0.9) if bit == 0 else ([("x", size / rate)], 2.0)
    if bit == 0:
        return [("y", size / rate)], 2.0
    if bit == 1:
        return [("outer", size / rate)], 2.0
    return [("outer", size / rate), ("inner", 2 * size / rate)], 2.5


def tick_order(segments, jobs):
    now, free, flying, points, current = 0.0, {}, [], [], []
    segments = list(segments)
    ended = set()

    def start(name, k):
        stage, size, _ = jobs[name][k]
        links, latency = stage_cost(stage, size)
        begin = max([now] + [free.get(link, 0.0) for link, _ in links])
        for link, length in links:
            free[link] = begin + length
        flying.append((begin + max([length for _, length in links], default=0.0) + latency, name, k))

    while segments or flying:
        ready = [f for f in flying if f[0] <= now]
        if ready:
            first = min(ready)
            flying.remove(first)
            _, name, k = first
            now += 0.05 + (jobs[name][k][1] / 1.5e6 if jobs[name][k][2] else 0.0)
            current.append((name, k + 1))
            if k + 1 < len(jobs[name]):
                start(name, k + 1)
            else:
                ended.add(name)
        elif segments and all(name in ended for name in segments[0][3]):
            points.append(current)
            current = []
            _, length, released, _ = segments.pop(0)
            now += length
            for name in released:
                start(name, 0)
        else:
            now = min(f[0] for f in flying)
    points.append(current)
    return points[1:]


def job_steps(rows, width, stages, hold=0.0):
    length, out, back = rows, [], []
    for stage in stages:
        halve = (length // 2) % 8 == 0
        length = length // 2 if halve else length
        out.append((stage, length * width * 4, True))
        if halve:
            back.append((stage, length * width * 4, False))
    return out + ([(None, hold, False)] if halve else []) + back[::-1]


def make_plan(config, dpbits, mols, groups, width, hidden, small):
    ne, ch, fs, no = config["ne"], config["ch"], config["fs"], config["no"]
    jobs, steps = {}, {}

    def add(name, kind, index, first, rows, stages, cols):
        jobs[name] = (kind, index, first, rows, stages)
        steps[name] = job_steps(rows, cols, stages, config["hold"].get(name, 0.0))

    for i in range(ne):
        n = (width + hidden) // ne
        add("e%d" % i, "e", 0, i * n, n, stages_of(E_ORDERS[config["eo"][i]], dpbits), width)
    for i in range(no):
        n = width // no
        add("o%d" % i, "o", 0, i * n, n, stages_of(ORDERS[config["oo"][i]], dpbits), width)
    for c in range(ch):
        for h in range(fs):
            n = 3 * width // fs
            add("f%d_%d" % (c, h), "f", c, h * n, n, stages_of(ORDERS[config["fo"][c * fs + h]], dpbits), width // ch)
    add("s", "s", 0, 0, small, stages_of(ORDERS[config["so"]], dpbits), width)
    add("b", "b", 0, 0, 8, stages_of("YZW", dpbits), hidden)
    q = ne // 4
    pos = config["pos"]
    segments = []

    def put(moment):
        for k in range(4):
            if pos[k] == moment:
                segments.append((("e", k), 0.65 if k < 2 else 1.3, ["e%d" % i for i in range(k * q, (k + 1) * q)], []))
        if pos[4] == moment:
            segments.append((("down",), 2.3, ["d"], []))

    swap = width * width * 2
    steps["d"] = [(("tensor", 0), swap, True), (("tensor", 1), swap, False)]
    steps["n"] = [(("tensor", 0), swap // 2, True), (("tensor", 1), swap // 2, False)]
    segments.append((("ffn",), 0.0, ["n", "b"], []))
    put(-2)
    segments.append((("pro1",), 1.2, ["o%d" % i for i in range(no)], ["n"]))
    put(-1)
    segments.append((("pro2",), 1.0, [], []))
    per = groups // ch
    for s in range(mols * groups):
        segments.append((("step", s), 0.8, [], []))
        if (s + 1) % (per * mols) == 0:
            c = s // (per * mols)
            segments.append((("chunk", c), 5.0 / ch, ["f%d_%d" % (c, h) for h in range(fs)], []))
        put(s)
    segments.append((("end",), 0.6, ["s"], []))
    return jobs, segments, tick_order(segments, steps)


def gelu_and_slope(x):
    cdf = 0.5 + 0.5 * lax.erf(x * (0.5 ** 0.5))
    return x * cdf, cdf + x * (jnp.exp(-0.5 * x * x) * (1.0 / math.sqrt(2.0 * math.pi)))


def mm3_nt(ahi, alo, bhi, blo):
    return dot_nt(ahi, bhi) + (dot_nt(ahi, blo) + dot_nt(alo, bhi))


def mm3_nn(ahi, alo, bhi, blo):
    return dot(ahi, bhi) + (dot(ahi, blo) + dot(alo, bhi))


def main_kernel(plan, *refs):
    refs = list(refs)
    take_n = lambda n: [refs.pop(0) for _ in range(n)]
    len_ref, types_ref, normed2_any = take_n(3)
    cot_refs = take_n(2)
    held_any = take_n(10)
    gain_ref, shift_ref, fgain_ref, bup_ref, bdown_ref = take_n(5)
    wup_any, wdown_any, wq_any, wk_any, wv_any, wo_any, pair_any, e_any = take_n(8)
    gpair, outv, gatv, eres, ores, fres, sres, bres = take_n(8)
    dl, qhi, qlo, khi, klo, vhi, vlo, dmhi, dmlo, dqt, dkt, dvt, maskc, dmid, energy = take_n(15)
    wq, wk, wv, wo, wuhi, wulo, wdhi, wdlo = take_n(8)
    gath, cots, duhi, dulo, pn, pd, rsn, rsd, nt, dn1 = take_n(10)
    ebuf, erecv, obuf, orecv, fbuf, frecv, sbuf, srecv, tbuf, tres, trecv, bbuf, brecv = take_n(13)
    middle_ref, first_ref, mixt_ref, linv_ref, pring, ering = take_n(6)
    rsems, free, lsems = take_n(3)
    assert not refs
    s = pl.program_id(0)
    mols, slots = types_ref.shape[0], types_ref.shape[2]
    groups = dl.shape[1]
    heads = groups * 8
    width = wo.shape[0]
    hidden = wuhi.shape[1]
    rows = mols * slots
    types = plan["types"]
    last = mols * groups - 1
    at = Place(plan["dpbits"])
    core, xbit = ("tensor", 0), ("tensor", 1)
    dpbits = [("dp", i) for i in range(plan["dpbits"])]
    wide = [core, xbit] + dpbits
    jobs, segments, points = plan["jobs"], plan["segments"], plan["points"]
    chunks = plan["chunks"]
    fcols = width // chunks

    tiles = [(r, c) for r in range(rows // 128) for c in range(hidden // 128)]

    across = hidden // 128

    def keep(base, b, x, top=0):
        for i, (r, c) in enumerate(tiles):
            if r < x.shape[0] // 128:
                gpair[0, base + b * len(tiles) + top * across + i] = x[r * 128:(r + 1) * 128, c * 128:(c + 1) * 128]

    def kept(base, b, top=0, n=rows // 128):
        parts = [gpair[0, base + b * len(tiles) + top * across + i] for i in range(n * across)]
        return jnp.concatenate([jnp.concatenate(parts[r * across:(r + 1) * across], 1) for r in range(n)], 0)

    ACT, DACT = 0, 4 * len(tiles)
    slot = [0]

    def swap(src, dst, stage):
        slot[0] += 1
        return Exchange(at, lambda: src, lambda: dst, rsems, slot[0] - 1, stage)

    hrows = rows // 2
    hpart = [pl.ds(i * hrows, hrows) for i in range(2)]
    n_core = swap(normed2_any, gath.at[1], core)
    n_x = [swap(normed2_any.at[h], gath.at[2, h], xbit) for h in hpart]
    c_core = swap(cot_refs[0], cots.at[1], core)
    c_diag = swap(cot_refs[1], cots.at[3], core)
    n_diag = [swap(gath.at[2, h], gath.at[3, h], core) for h in hpart]
    dn_core = swap(pn.at[1], rsn.at[0], core)
    dn_diag = [swap(pn.at[3, h], rsn.at[1, h], core) for h in hpart]
    dn_x = [swap(pn.at[2, h], rsn.at[2, h], xbit) for h in hpart]
    dd_core = swap(pd.at[1], rsd.at[0], core)
    dd_diag = swap(pd.at[3], rsd.at[1], core)
    dd_x = swap(pd.at[2], rsd.at[2], xbit)

    def make(buf, res, recv, nrows, stages):
        def done():
            res[...] = buf[...]
        job = Job(at, buf, recv, rsems, free, slot[0], nrows, stages, done)
        slot[0] += job.slots
        return job

    total_job = make(tbuf, tres, trecv, 8, wide)
    running = {}
    place = {"e": 0, "o": 0, "f": 0}
    for name, (kind, index, first_row, nrows, stages) in jobs.items():
        if kind == "s":
            running[name] = make(sbuf, sres, srecv, nrows, stages)
        elif kind == "b":
            running[name] = make(bbuf, bres, brecv, nrows, stages)
        else:
            need = job_need(nrows, stages)[0]
            if kind == "f":
                buf, res, recv = fbuf.at[index], fres.at[index], frecv
            else:
                buf, res, recv = {"e": (ebuf, eres, erecv), "o": (obuf, ores, orecv)}[kind]
            running[name] = make(buf.at[pl.ds(first_row, nrows)], res.at[pl.ds(first_row, nrows)], recv.at[pl.ds(place[kind], need)], nrows, stages)
            place[kind] += need
    assert slot[0] == plan["slots"], slot[0]
    half = width // 2

    def n_sum(i):
        dn_diag[i].wait()
        pn[2, hpart[i], :] = pn[2, hpart[i], :] + rsn[1, hpart[i], :]
        dn_x[i].start()

    def n_end():
        dn_core.wait()
        dn_x[0].wait()
        dn_x[1].wait()

    def d_begin():
        dd_diag.start()
        dd_core.start()

    def d_sum():
        dd_diag.wait()
        pd[2] = pd[2] + rsd[1]
        dd_x.start()

    def d_end():
        dd_core.wait()
        dd_x.wait()
        outv[...] = middle_ref[...] + bdown_ref[...] + (pd[0] + (rsd[0] + rsd[2]))

    running["n"] = Actions(dn_diag[1].start, functools.partial(n_sum, 1), n_end)
    running["d"] = Actions(d_begin, d_sum, d_end)

    cot_load = [pltpu.make_async_copy(cot_refs[b], cots.at[2 * b], lsems.at[b]) for b in range(2)]
    piece = width // rows
    up_load = [pltpu.make_async_copy(wup_any.at[pl.ds(i * rows, rows)], pn.at[i], lsems.at[4 + i]) for i in range(piece)]
    down_load = [pltpu.make_async_copy(wdown_any.at[pl.ds(i * rows, rows)], pn.at[2 + i], lsems.at[6 + i]) for i in range(piece)]
    load = [pltpu.make_async_copy(a, b, lsems.at[8 + i]) for i, (a, b) in enumerate(((wo_any, wo), (wq_any, wq), (wk_any, wk), (wv_any, wv)))]
    own_load = pltpu.make_async_copy(normed2_any, gath.at[0], lsems.at[12])
    held = (first_ref, middle_ref, qhi, qlo, khi, klo, vhi, vlo, mixt_ref, linv_ref)
    held_load = [pltpu.make_async_copy(a, b, lsems.at[13 + i]) for i, (a, b) in enumerate(zip(held_any, held))]
    depth = pring.shape[0]

    def ring(step):
        which = lax.rem(step, depth)
        mol, first_head = lax.rem(step, mols), lax.div(step, mols) * 8
        return [pltpu.make_async_copy(a.at[mol, pl.ds(first_head, 8)], r.at[which], lsems.at[23 + i * depth + which])
                for i, (a, r) in enumerate(((pair_any, pring), (e_any, ering)))]

    def seg_ffn():
        barrier = pltpu.get_barrier_semaphore()
        for stage in wide:
            pl.semaphore_signal(barrier, inc=1, device_id=at.partners[stage], device_id_type=LOGICAL)
        pl.semaphore_wait(barrier, len(wide))
        for copy in n_x:
            copy.start()
        c_core.start()
        c_diag.start()
        n_core.start()
        for copy in down_load + cot_load[:1] + up_load + cot_load[1:] + [own_load]:
            copy.start()
        square = jnp.zeros((1, 1), F32)
        for m in range(mols):
            f = jnp.full((1, 1), len_ref[m], jnp.int32).astype(F32)
            square = square + f * f
        tbuf[...] = jnp.broadcast_to(square, tbuf.shape)
        total_job.tick(0)
        bbuf[...] = jnp.zeros_like(bbuf)
        sbuf[...] = jnp.zeros_like(sbuf)
        for copy in down_load:
            copy.wait()
        for i in range(piece):
            part = pl.ds(i * rows, rows)
            wdhi[part, :], wdlo[part, :] = split(pn[2 + i])
        for copy in cot_load + up_load:
            copy.wait()
        for i in range(piece):
            part = pl.ds(i * rows, rows)
            wuhi[part, :], wulo[part, :] = split(pn[i])
        total_job.tick(1)
        for copy in held_load + load:
            copy.start()
        for step in range(depth - 1):
            for copy in ring(step):
                copy.start()

        def p1(b, carry):
            hi, lo = split(cots[b])
            keep(DACT, b, mm3_nt(hi, lo, wdhi[...], wdlo[...]))
            return carry

        lax.fori_loop(0, 2, lambda b, carry: p1(2 * b, carry), 0)
        c_core.wait()
        c_diag.wait()
        lax.fori_loop(0, 2, lambda b, carry: p1(2 * b + 1, carry), 0)
        own_load.wait()
        n_core.wait()
        total_job.tick(2)

        def p2(b, top=0, n=rows // 128):
            part = pl.ds(top * 128, n * 128)
            hi, lo = split(gath[b, part, :])
            upper = mm3_nn(hi, lo, wuhi[...], wulo[...]) + bup_ref[...]
            a, slope = gelu_and_slope(upper)
            keep(ACT, b, a, top)
            du = kept(DACT, b, top, n) * slope
            dhi, dlo = split(du)
            duhi[b, part, :] = dhi
            dulo[b, part, :] = dlo
            bbuf[...] = bbuf[...] + jnp.broadcast_to(jnp.sum(du, axis=0, keepdims=True), bbuf.shape)
            pn[b, part, :] = mm3_nt(dhi, dlo, wuhi[...], wulo[...])

        def p2_loop(b, carry):
            p2(b)
            return carry

        lax.fori_loop(0, 2, p2_loop, 0)
        dn_core.start()
        first_work()
        n = hrows // 128
        for i in range(2):
            n_x[i].wait()
            n_diag[i].start()
            p2(2, i * n, n)
            n_diag[i].wait()
            p2(3, i * n, n)
            total_job.tick(3 + i)
            if i == 0:
                dn_diag[0].start()
                n_sum(0)
        running["n"].tick(0)
        running["b"].tick(0)

    def first_work():
        for copy in held_load:
            copy.wait()
        first = first_ref[...]
        cen = first - jnp.mean(first, axis=-1, keepdims=True)
        rstd = lax.rsqrt(jnp.mean(cen * cen, axis=-1, keepdims=True) + EPSILON)
        normed = cen * rstd * gain_ref[...] + shift_ref[...]
        for m in range(mols):
            nt[:, m * slots:(m + 1) * slots] = jnp.transpose(normed[m * slots:(m + 1) * slots])
        dn1[...] = jnp.zeros_like(dn1)
        energy[...] = jnp.zeros_like(energy)
        for k in range(2):
            lax.fori_loop(0, 2, functools.partial(weight_part, k), 0)

    def down_part(b, carry):
        hi, lo = split(kept(ACT, b))
        pd[b] = mm3_nn(hi, lo, wdhi[...], wdlo[...])
        return carry

    def weight_part(k, b, carry):
        part = slice((k % 2) * half, (k % 2 + 1) * half)
        left = kept(ACT, b)[:, part] if k < 2 else gath[b, :, part]
        ahi, alo = split(jnp.transpose(left))
        if k < 2:
            chi, clo = split(cots[b])
        else:
            chi, clo = duhi[b], dulo[b]
        g = mm3_nn(ahi, alo, chi, clo)
        to = pl.ds(k * half, half)

        @pl.when(b == 0)
        def _():
            ebuf[to, :] = g

        @pl.when(b > 0)
        def _():
            ebuf[to, :] = ebuf[to, :] + g
        return carry

    def seg_e(k):
        lax.fori_loop(2 if k < 2 else 0, 4, functools.partial(weight_part, k), 0)
        q = plan["ne"] // 4
        for i in range(k * q, (k + 1) * q):
            running["e%d" % i].tick(0)

    def seg_down():
        lax.fori_loop(0, 4, down_part, 0)
        running["d"].tick(0)

    def small(i, value):
        sbuf[types + i:types + i + 1, :] = value

    def seg_pro1():
        mid = middle_ref[...]
        cen = mid - jnp.mean(mid, axis=-1, keepdims=True)
        rstd = lax.rsqrt(jnp.mean(cen * cen, axis=-1, keepdims=True) + EPSILON)
        xhat = cen * rstd
        c = pn[0] + (rsn[0] + rsn[2])
        small(0, jnp.sum(c * xhat, axis=0, keepdims=True))
        small(1, jnp.sum(c, axis=0, keepdims=True))
        cot = cots[0]
        small(2, jnp.sum(cot, axis=0, keepdims=True))
        ce = c * fgain_ref[...]
        dmiddle = cot + rstd * (ce - jnp.mean(ce, axis=-1, keepdims=True) - xhat * jnp.mean(ce * xhat, axis=-1, keepdims=True))
        dmid[...] = dmiddle
        small(3, jnp.sum(dmiddle, axis=0, keepdims=True))
        for copy in load:
            copy.wait()
        dhi, dlo = split(dmiddle)
        mhi, mlo = split(jnp.concatenate([mixt_ref[m] for m in range(mols)], 1))
        obuf[...] = mm3_nn(mhi, mlo, dhi, dlo)
        for i in range(plan["no"]):
            running["o%d" % i].tick(0)

    def seg_pro2():
        for k in range(5, total_job.ticks):
            total_job.tick(k)
        wohi, wolo = split(wo[...])
        dhi, dlo = split(dmid[...])
        dm = mm3_nt(dhi, dlo, wohi, wolo)
        lane = lax.broadcasted_iota(jnp.int32, (slots, 128), 1)
        rowi = lax.broadcasted_iota(jnp.int32, (slots, slots), 0)
        coli = lax.broadcasted_iota(jnp.int32, (slots, slots), 1)
        twice = 2.0 / (heads * tres[0:1, 0:slots])
        for m in range(mols):
            length = len_ref[m]
            maskc[m] = jnp.where(jnp.logical_and(rowi < length, coli < length), twice, 0.0)
            dmt = jnp.transpose(dm[m * slots:(m + 1) * slots]) * linv_ref[m]
            dmhi[m], dmlo[m] = split(dmt)
            prod = dmt * mixt_ref[m]
            delta = jnp.sum(prod.reshape(heads, 8, slots), axis=1)
            for g in range(groups):
                d8 = -delta[g * 8:(g + 1) * 8]
                x = jnp.concatenate([dmt[g * 64:(g + 1) * 64], d8, d8, jnp.zeros((48, slots), F32)], 0)
                y = jnp.transpose(x)
                yhi = y.astype(BF).astype(F32)
                ylo = y - yhi
                dl[m, g, :, 0:128] = jnp.where(lane < 64, yhi, pltpu.roll(ylo, 64, 1)).astype(BF)
                dl[m, g, :, 128:256] = jnp.where(lane < 72, yhi, ylo).astype(BF)

    def seg_chunk(c):
        part = slice(c * fcols, (c + 1) * fcols)
        nhi, nlo = split(nt[...])
        for i, t_ref in enumerate((dqt, dkt, dvt)):
            thi, tlo = split(jnp.concatenate([t_ref[mm, part, :] for mm in range(mols)], 1))
            fbuf[c, i * width:(i + 1) * width, :] = mm3_nt(nhi, nlo, thi, tlo)
        for h in range(plan["fs"]):
            running["f%d_%d" % (c, h)].tick(0)
        acc = dn1[...]
        for i, (t_ref, w) in enumerate(((dqt, wq), (dkt, wk), (dvt, wv))):
            nat = jnp.concatenate([jnp.transpose(t_ref[mm, part, :]) for mm in range(mols)], 0)
            if i != 1:
                r = types + (4 if i == 0 else 5)
                sbuf[r:r + 1, part] = jnp.sum(nat, axis=0, keepdims=True)
            ahi, alo = split(nat)
            whi, wlo = split(w[:, part])
            acc = acc + mm3_nt(ahi, alo, whi, wlo)
        dn1[...] = acc

    def seg_end():
        first = first_ref[...]
        cen = first - jnp.mean(first, axis=-1, keepdims=True)
        rstd = lax.rsqrt(jnp.mean(cen * cen, axis=-1, keepdims=True) + EPSILON)
        xhat = cen * rstd
        dn = dn1[...]
        small(6, jnp.sum(dn * xhat, axis=0, keepdims=True))
        small(7, jnp.sum(dn, axis=0, keepdims=True))
        ge = dn * gain_ref[...]
        gat = dmid[...] + rstd * (ge - jnp.mean(ge, axis=-1, keepdims=True) - xhat * jnp.mean(ge * xhat, axis=-1, keepdims=True))
        gatv[...] = gat
        acc = None
        for mm in range(mols):
            one = (lax.broadcasted_iota(jnp.int32, (types, slots), 0) == types_ref[mm]).astype(F32).astype(BF)
            for bits in split3(gat[mm * slots:(mm + 1) * slots]):
                part = dot(one, bits)
                acc = part if acc is None else acc + part
        sbuf[0:types, :] = acc
        total = jnp.sum(jnp.sum(energy[...], axis=0, keepdims=True), axis=1, keepdims=True) * 0.5
        small(8, jnp.broadcast_to(total, (1, width)))
        running["s"].tick(0)

    work = {"ffn": seg_ffn, "e": seg_e, "down": seg_down, "pro1": seg_pro1, "pro2": seg_pro2, "chunk": seg_chunk, "end": seg_end}
    before, after = [], {}
    step_now = None
    for (name, _, _, _), ticks in zip(segments, points):
        if name[0] == "step":
            step_now = name[1]
        else:
            to = before if step_now is None else after.setdefault(step_now, [])
            to.append(functools.partial(work[name[0]], *name[1:]))
        to = before if step_now is None else after.setdefault(step_now, [])
        to += [functools.partial(running[job].tick, k) for job, k in ticks]

    @pl.when(s == 0)
    def _():
        for fn in before:
            fn()

    g = s // mols
    m = s % mols
    lhs = dl[m, g]
    which = lax.rem(s, depth)
    for copy in ring(s):
        copy.wait()

    @pl.when(s + depth - 1 <= last)
    def _():
        for copy in ring(s + depth - 1):
            copy.start()

    sub = lax.broadcasted_iota(jnp.int32, (16, 128), 0)
    z = jnp.zeros((16, 256), BF)
    zero16 = jnp.zeros((16, 128), BF)
    mc = maskc[m]
    en = energy[...]
    for p in range(4):
        row = pl.multiple_of(g * 64 + 16 * p, 16)
        rows16 = pl.ds(row, 16)

        def blk(x):
            x = x.astype(F32)
            a = jnp.where(sub < 8, x, 0.0).astype(BF)
            b = jnp.where(sub >= 8, x, 0.0).astype(BF)
            return jnp.concatenate([a, b], axis=1)
        bhi, blo = blk(vhi[m, rows16, :]), blk(vlo[m, rows16, :])
        sel = jnp.concatenate([jnp.where(sub % 8 == 2 * p, 1.0, 0.0), jnp.where(sub % 8 == 2 * p + 1, 1.0, 0.0)], axis=1).astype(BF)
        rws = [bhi if i == p else z for i in range(4)]
        rws += rws
        rws += [blo if i == p else z for i in range(4)]
        rws += [sel, z, z, z]
        dp = dot(lhs, jnp.concatenate(rws, axis=0))
        gs = []
        es = []
        for hf in range(2):
            both = ering[which, 2 * p + hf]
            es.append(both)
            e = both[:, 0:128].astype(F32) + both[:, 128:256].astype(F32)
            logits = pring[which, 2 * p + hf]
            t = logits * mc
            en = en + t * logits
            gp = e * dp[:, hf * 128:(hf + 1) * 128] + t
            gpair[m, g * 8 + 2 * p + hf] = gp
            gs.append(split(gp))

        def rows_lhs(hi, lo):
            return jnp.concatenate([jnp.concatenate([hi, hi], 1), jnp.concatenate([lo, zero16], 1)], 0)

        def take(out):
            acc = out[0:16] + out[16:32]
            return jnp.concatenate([acc[0:8, 0:128], acc[8:16, 128:256]], 0)
        ecol = jnp.concatenate([jnp.concatenate([es[0][:, 0:128], es[1][:, 0:128]], 1), jnp.concatenate([es[0][:, 128:256], es[1][:, 128:256]], 1)], 0)
        dvt[m, rows16, :] = take(dot(rows_lhs(dmhi[m, rows16, :], dmlo[m, rows16, :]), ecol))
        gcol = jnp.concatenate([jnp.concatenate([gs[0][0], gs[1][0]], 1), jnp.concatenate([gs[0][1], gs[1][1]], 1)], 0)
        dkt[m, rows16, :] = take(dot(rows_lhs(qhi[m, rows16, :], qlo[m, rows16, :]), gcol))
        grow = jnp.concatenate([jnp.concatenate(gs[0], 1), jnp.concatenate(gs[1], 1)], 0)
        dqt[m, rows16, :] = take(dot_nt(rows_lhs(khi[m, rows16, :], klo[m, rows16, :]), grow)) * (8 ** -0.5)
    energy[...] = en

    for moment in sorted(after):
        def body(moment=moment):
            for fn in after[moment]:
                fn()
        pl.when(s == moment)(body)


CONFIG = dict(ne=8, ch=4, fs=3, no=2, eo=[1, 0, 1, 0, 0, 0, 0, 0], fo=[5, 0, 5, 2, 2, 0, 2, 1, 0, 0, 5, 0], oo=[0, 2], so=2, pos=[-2, -2, -2, -2, -2], hold={'e2': 32, 'e0': 32, 'e3': 32, 'e7': 24, 'o1': 8, 'e4': 4, 'o0': 4, 'e6': 2, 'f2_1': 2, 'f0_0': 8, 'f3_2': 2, 'f1_2': 2, 'f3_1': 2, 'f2_0': 2})


def main_call(mesh, lengths, types, normed2, cots, held, gain, shift, fgain, bup, bdown,
              wup, wdown, wq, wk, wv, wo, pair, e, ntypes):
    mols, slots = types.shape
    rows, width = normed2.shape
    heads = pair.shape[1]
    groups = heads // 8
    hidden = wup.shape[1]
    dp = mesh.shape["dp"]
    dpbits = dp.bit_length() - 1
    assert (1 << dpbits) == dp and mesh.shape["tensor"] == 4
    small = -(-(ntypes + 9) // 64) * 64
    config = CONFIG if dpbits <= 3 else dict(ne=4, ch=1, fs=1, no=1, eo=[0] * 4, fo=[0], oo=[0], so=0, pos=[-2, -2, -2, -2, -2], hold={})
    jobs, segments, points = make_plan(config, dpbits, mols, groups, width, hidden, small)
    chunks = config["ch"]
    fcols = width // chunks
    needs = {"e": 0, "o": 0, "f": 0, "s": 0, "b": 0}
    stages = stages_of("CXYZW", dpbits)
    t_need = job_need(8, stages)
    nslots = 15 + t_need[1]
    for kind, index, first_row, nrows, order in jobs.values():
        need = job_need(nrows, order)
        needs[kind] += need[0]
        nslots += need[1]
    plan = dict(dpbits=dpbits, chunks=chunks, types=ntypes, slots=nslots, jobs=jobs, segments=segments, points=points,
                ne=config["ne"], no=config["no"], fs=config["fs"])
    V = pltpu.VMEM
    one = lambda shape: pl.BlockSpec(shape, lambda s: (0,) * len(shape), pipeline_mode=pl.Buffered(1))
    any_ = pl.BlockSpec(memory_space=pl.ANY)
    smem = pl.BlockSpec(memory_space=pltpu.SMEM)
    vmem = pl.BlockSpec(memory_space=pltpu.VMEM)
    vec = lambda v: v.reshape(1, -1)
    tt = (mols, width, slots)
    rw = (rows, width)
    in_specs = [smem, one((mols, 1, slots))] + [any_] * 13 + \
        [one((1, width))] * 3 + [one((1, hidden)), one((1, width))] + [any_] * 8
    ww = (width, width)
    ff = (width + hidden, width)
    outs = [V(pair.shape, F32), V(rw, F32), V(rw, F32), V(ff, F32), V(ww, F32), V((chunks, 3 * width, fcols), F32), V((small, width), F32), V((8, hidden), F32)]
    four = (4, rows, width)
    scratch = [V((mols, groups, slots, 256), BF)] + [V(tt, BF)] * 8 + [V(tt, F32)] * 3 + [V((mols, slots, slots), F32), V(rw, F32), V((slots, slots), F32)]
    scratch += [V(ww, F32)] * 4 + [V((width, hidden), BF)] * 2 + [V((hidden, width), BF)] * 2
    scratch += [V(four, F32)] * 2 + [V(four, BF)] * 2 + [V(four, F32)] * 2 + [V((3, rows, width), F32)] * 2 + [V((width, rows), F32), V(rw, F32)]
    scratch += [V(ff, F32), V((needs["e"], width), F32), V(ww, F32), V((needs["o"], width), F32)]
    scratch += [V((chunks, 3 * width, fcols), F32), V((needs["f"], fcols), F32), V((small, width), F32), V((needs["s"], width), F32)]
    scratch += [V((8, 128), F32)] * 2 + [V((t_need[0], 128), F32), V((8, hidden), F32), V((needs["b"], hidden), F32)]
    scratch += [V(rw, F32)] * 2 + [V(tt, F32)] * 2 + [V((DEPTH, 8, slots, slots), F32), V((DEPTH, 8, slots, 2 * slots), BF)]
    scratch += [pltpu.SemaphoreType.DMA((2, nslots)), pltpu.SemaphoreType.REGULAR((nslots,)), pltpu.SemaphoreType.DMA((23 + 2 * DEPTH,))]
    return pl.pallas_call(functools.partial(main_kernel, plan), out_shape=outs, grid=(mols * groups,), in_specs=in_specs, out_specs=[vmem] * 8,
        scratch_shapes=scratch,
        compiler_params=pltpu.CompilerParams(vmem_limit_bytes=VLIMIT, dimension_semantics=("arbitrary",), collective_id=0, has_side_effects=True),
        name="feed_forward_and_backward",
    )(lengths, types.reshape(mols, 1, slots), normed2, *cots, *held, vec(gain), vec(shift), vec(fgain), vec(bup), vec(bdown),
      wup, wdown, wq, wk, wv, wo, pair, e)


DEPTH = 4
VLIMIT = 47 * 1024 * 1024
SMALL_ROWS = (0, 1, 2, 3, 4, 5, 6, 7)


def finish_kernel(types, gpair, outv, gatv, eres, ores, fres, sres, bres, *refs):
    refs = list(refs)
    gp_out, atom_out, gatoms_out, gdown_out, gup_out, gwo_out, gwq_out, gwk_out, gwv_out, table_out = [refs.pop(0) for _ in range(10)]
    rows_out = [refs.pop(0) for _ in range(len(SMALL_ROWS))]
    gbup_out, pen_out, sems = refs
    width = outv.shape[1]
    hidden = eres.shape[0] - width
    copies = []

    def go(src, dst):
        copy = pltpu.make_async_copy(src, dst, sems.at[len(copies)])
        copy.start()
        copies.append(copy)

    for m in range(gpair.shape[0]):
        for h in range(0, gpair.shape[1], 16):
            go(gpair.at[m, pl.ds(h, 16)], gp_out.at[m, pl.ds(h, 16)])
    go(eres.at[pl.ds(0, hidden)], gdown_out)
    go(eres.at[pl.ds(hidden, width)], gup_out)
    go(ores, gwo_out)
    chunks, _, fcols = fres.shape
    for c in range(chunks):
        for j, out in enumerate((gwq_out, gwk_out, gwv_out)):
            go(fres.at[c, pl.ds(j * width, width)], out.at[:, pl.ds(c * fcols, fcols)])
    go(outv, atom_out)
    go(gatv, gatoms_out)
    go(sres.at[pl.ds(0, types)], table_out)
    for i, out in zip(SMALL_ROWS, rows_out):
        out[...] = sres[types + i, :]
    gbup_out[...] = bres[0, :]
    pen_out[0, 0] = jnp.sum(sres[types + 8:types + 9, 0:1])
    for copy in copies:
        copy.wait()


def finish(types, parts, width, hidden):
    gpair, outv, gatv, eres, ores, fres, sres, bres = parts
    S = jax.ShapeDtypeStruct
    any_ = pl.BlockSpec(memory_space=pl.ANY)
    vmem = pl.BlockSpec(memory_space=pltpu.VMEM)
    shapes = [gpair.shape, outv.shape, gatv.shape, (hidden, width), (width, hidden)] + [(width, width)] * 4 + [(types, width)]
    outs = [S(shape, F32) for shape in shapes] + [S((width,), F32)] * len(SMALL_ROWS) + [S((hidden,), F32), S((1, 1), F32)]
    ncopies = gpair.shape[0] * gpair.shape[1] // 16 + 6 + 3 * fres.shape[0]
    return pl.pallas_call(functools.partial(finish_kernel, types), out_shape=outs, in_specs=[vmem] * 8,
        out_specs=[any_] * 10 + [vmem] * (len(SMALL_ROWS) + 1) + [pl.BlockSpec(memory_space=pltpu.SMEM)],
        scratch_shapes=[pltpu.SemaphoreType.DMA((ncopies,))], compiler_params=pltpu.CompilerParams(vmem_limit_bytes=4 * 1024 * 1024),
        name="finish")(*parts)


def local(mesh, atom_types, lengths, atom_feats, pair_bias, out_cotangent, type_table, norm_gain, norm_shift, w_query, b_query,
          w_key, w_value, b_value, w_out, b_out, ffn_gain, ffn_shift, w_up, b_up, w_down, b_down):
    tensor = mesh.shape["tensor"]
    cots = [out_cotangent, lax.ppermute(out_cotangent, "tensor", [(i, i ^ 2) for i in range(tensor)])]
    pair_out, e, first, qhi, qlo, khi, klo, vhi, vlo, mixt, linv, middle, normed2 = attention_forward(
        lengths, atom_types, atom_feats, type_table, norm_gain, norm_shift, w_query, b_query, w_key, w_value, b_value, w_out, b_out,
        ffn_gain, ffn_shift, pair_bias)
    types = type_table.shape[0]
    parts = main_call(
        mesh, lengths, atom_types, normed2, cots, (first, middle, qhi, qlo, khi, klo, vhi, vlo, mixt, linv), norm_gain, norm_shift, ffn_gain, b_up, b_down,
        w_up, w_down, w_query, w_key, w_value, w_out, pair_out, e, types)
    (grad_pair, atom_out, grad_atoms, gwdown, gwup, gwo, gwq, gwk, gwv, table, g_fgain, g_fshift, g_bdown, g_bout, g_bq, g_bv, g_gain, g_shift,
     gbup, penalty) = finish(types, parts, w_up.shape[0], w_up.shape[1])
    return (atom_out, pair_out, penalty.reshape(()), grad_atoms, grad_pair, table, g_gain, g_shift, gwq, g_bq, gwk, gwv, g_bv,
            gwo, g_bout, g_fgain, g_fshift, gwup, gbup, gwdown, g_bdown)


def solution(mesh):
    in_specs = (
        P(("dp", "tensor"), None),
        P(("dp", "tensor")),
        P(("dp", "tensor"), None),
        P(("dp", "tensor"), None, None, None),
        P(("dp", "tensor"), None),
        P(),
        P(),
        P(),
        P(),
        P(),
        P(),
        P(),
        P(),
        P(),
        P(),
        P(),
        P(),
        P(None, "tensor"),
        P("tensor"),
        P("tensor", None),
        P(),
    )
    out_specs = (
        P(("dp", "tensor"), None),
        P(("dp", "tensor"), None, None, None),
        P(),
        P(("dp", "tensor"), None),
        P(("dp", "tensor"), None, None, None),
        P(),
        P(),
        P(),
        P(),
        P(),
        P(),
        P(),
        P(),
        P(),
        P(),
        P(),
        P(),
        P(None, "tensor"),
        P("tensor"),
        P("tensor", None),
        P(),
    )
    return jax.shard_map(functools.partial(local, mesh), mesh=mesh, in_specs=in_specs, out_specs=out_specs, check_vma=False)
```

```python
import functools, math
import jax, jax.numpy as jnp
from jax import lax
from jax.experimental import pallas as pl
from jax.experimental.pallas import tpu as pltpu
from jax.sharding import PartitionSpec as P
F32=jnp.float32; BF=jnp.bfloat16
EPSILON=1e-5
SPAN=2

def split(x):
    hi = x.astype(BF)
    lo = (x - hi.astype(F32)).astype(BF)
    return hi, lo

def split3(x):
    hi = x.astype(BF)
    r = x - hi.astype(F32)
    mid = r.astype(BF)
    lo = (r - mid.astype(F32)).astype(BF)
    return hi, mid, lo

def dot(a, b):
    return jnp.dot(a, b, preferred_element_type=F32)

def dot_nt(a, b):
    return lax.dot_general(a, b, (((1,), (1,)), ((), ())), preferred_element_type=F32)

def mm3(a, bhi, blo):
    ahi, alo = split(a)
    return dot(ahi, bhi) + (dot(ahi, blo) + dot(alo, bhi))

def fwd_kernel(len_ref, types_ref, feats_ref, table_ref, gain_ref, shift_ref, wq_ref, bq_ref, wk_ref, wv_ref, bv_ref,
               wo_ref, bo_ref, fgain_ref, fshift_ref, bias_ref,
               pair_ref, e_ref, first_ref, qthi, qtlo, kthi, ktlo, vthi, vtlo, mixt_ref, linv_ref, middle_ref, normed_ref,
               ql, *, span):
    s = pl.program_id(0)
    mols, slots = types_ref.shape[0], types_ref.shape[2]
    groups = ql.shape[1]
    @pl.when(s == 0)
    def _():
        tab = split3(table_ref[...])
        types = table_ref.shape[0]
        for m in range(mols):
            ids = types_ref[m]
            oneT = (lax.broadcasted_iota(jnp.int32, (slots, slots), 0) == ids).astype(F32)
            one = jnp.transpose(oneT)[:, :types].astype(BF)
            rows = pl.ds(m*slots, slots)
            first = feats_ref[rows, :] + (dot(one, tab[0]) + (dot(one, tab[1]) + dot(one, tab[2])))
            first_ref[rows, :] = first
        first = first_ref[...]
        cen = first - jnp.mean(first, axis=-1, keepdims=True)
        var = jnp.mean(cen*cen, axis=-1, keepdims=True)
        normed = cen * lax.rsqrt(var + EPSILON) * gain_ref[...] + shift_ref[...]
        nhi, nlo = split(normed)
        def proj(w_ref):
            whi, wlo = split(w_ref[...])
            return dot(nhi, whi) + (dot(nhi, wlo) + dot(nlo, whi))
        q = (proj(wq_ref) + bq_ref[...]) * (8 ** -0.5)
        k = proj(wk_ref)
        v = proj(wv_ref) + bv_ref[...]
        lane = lax.broadcasted_iota(jnp.int32, (slots, 128), 1)
        for m in range(mols):
            sl = slice(m*slots, (m+1)*slots)
            qm = q[sl]
            qthi[m], qtlo[m] = split(jnp.transpose(qm))
            kt = jnp.transpose(k[sl])
            kthi[m], ktlo[m] = split(kt)
            vt = jnp.transpose(v[sl])
            vthi[m], vtlo[m] = split(vt)
            for t in range(groups // 2):
                tile = qm[:, t*128:(t+1)*128]
                rolled = pltpu.roll(tile, 64, 1)
                for half in range(2):
                    dup = jnp.where(lane < 64, tile, rolled) if half == 0 else jnp.where(lane < 64, rolled, tile)
                    hi, lo = split(dup)
                    hi32, lo32 = hi.astype(F32), lo.astype(F32)
                    ql[m, 2*t+half, :, 0:128] = jnp.where(lane < 64, hi32, lo32).astype(BF)
                    ql[m, 2*t+half, :, 128:256] = jnp.where(lane < 64, hi32, 0.0).astype(BF)
    per = groups // span
    m = s // per
    length = len_ref[m]
    col_live = lax.broadcasted_iota(jnp.int32, (slots, slots), 1) < length
    sub = lax.broadcasted_iota(jnp.int32, (16, 128), 0)
    zero16 = jnp.zeros((16, 128), BF)
    ones = jnp.ones((16, 256), BF)
    def one(i, carry):
        g = (s % per) * span + i
        h0 = i * 8
        lhs = ql[m, g]
        for p in range(4):
            row = pl.multiple_of(g*64 + 16*p, 16)
            khi = kthi[m, pl.ds(row, 16), :].astype(F32)
            klo = ktlo[m, pl.ds(row, 16), :].astype(F32)
            def blk(x):
                a = jnp.where(sub < 8, x, 0.0).astype(BF)
                b = jnp.where(sub >= 8, x, 0.0).astype(BF)
                return jnp.concatenate([a, b], axis=1)
            bhi, blo = blk(khi), blk(klo)
            z = jnp.concatenate([zero16, zero16], axis=1)
            rows = [bhi if i == p else z for i in range(4)]
            rows += rows
            rows += [blo if i == p else z for i in range(4)]
            rows += [z]*4
            rhs = jnp.concatenate(rows, axis=0)
            lg = dot(lhs, rhs)
            ehl = []
            for half in range(2):
                logits = lg[:, half*128:(half+1)*128] + bias_ref[0, h0 + 2*p+half].astype(F32)
                pair_ref[0, h0 + 2*p+half] = logits
                masked = jnp.where(col_live, logits, -1e30)
                top = jnp.max(masked, axis=1, keepdims=True)
                e = jnp.exp(masked - top)
                hi, lo = split(e)
                both = jnp.concatenate([hi, lo], axis=1)
                e_ref[0, h0 + 2*p+half] = both
                ehl.append(both)
            vhi = vthi[m, pl.ds(row, 16), :]
            vlo = vtlo[m, pl.ds(row, 16), :]
            lv = jnp.concatenate([jnp.concatenate([vhi, vhi], 1), jnp.concatenate([vlo, zero16], 1), ones], 0)
            out = dot_nt(lv, jnp.concatenate(ehl, 0))
            acc = out[0:16] + out[16:32]
            sums = out[32:48]
            inv = 1.0 / jnp.concatenate([sums[0:8, 0:128], sums[8:16, 128:256]], 0)
            linv_ref[m, pl.ds(row, 16), :] = inv
            mixt_ref[m, pl.ds(row, 16), :] = jnp.concatenate([acc[0:8, 0:128], acc[8:16, 128:256]], 0) * inv
        return carry

    if span == 1:
        one(0, 0)
    else:
        lax.fori_loop(0, span, one, 0)
    @pl.when(s == mols*groups // span - 1)
    def _():
        mix = jnp.concatenate([jnp.transpose(mixt_ref[m]) for m in range(mols)], 0)
        whi, wlo = split(wo_ref[...])
        mid = first_ref[...] + (mm3(mix, whi, wlo) + bo_ref[...])
        middle_ref[...] = mid
        mcen = mid - jnp.mean(mid, axis=-1, keepdims=True)
        mvar = jnp.mean(mcen*mcen, axis=-1, keepdims=True)
        normed_ref[...] = mcen * lax.rsqrt(mvar + EPSILON) * fgain_ref[...] + fshift_ref[...]

def attention_forward(lengths, types, feats, table, gain, shift, wq, bq, wk, wv, bv, wo, bo, fgain, fshift, bias):
    mols, slots = types.shape
    width = feats.shape[1]
    heads = bias.shape[1]
    groups = heads // 8
    rows = mols*slots
    full = lambda shape: pl.BlockSpec(shape, lambda s: (0,)*len(shape))
    vec = lambda v: v.reshape(1, -1)
    outs = [jax.ShapeDtypeStruct((mols, heads, slots, slots), F32),
            jax.ShapeDtypeStruct((mols, heads, slots, 2*slots), BF),
            jax.ShapeDtypeStruct((rows, width), F32)] + [jax.ShapeDtypeStruct((mols, width, slots), BF)]*6 + [jax.ShapeDtypeStruct((mols, width, slots), F32)]*2 + [jax.ShapeDtypeStruct((rows, width), F32)]*2
    blk = lambda w: pl.BlockSpec((1, 8*SPAN, slots, w), lambda s: (s // (groups // SPAN), s % (groups // SPAN), 0, 0))
    in_specs = [pl.BlockSpec(memory_space=pltpu.SMEM), full((mols,1,slots)), full((rows,width)), full(table.shape), full((1,width)), full((1,width)),
                full(wq.shape), full((1,width)), full(wk.shape), full(wv.shape), full((1,width)), full(wo.shape), full((1,width)), full((1,width)), full((1,width)), blk(slots)]
    return pl.pallas_call(functools.partial(fwd_kernel, span=SPAN), out_shape=outs, grid=(mols*groups // SPAN,), in_specs=in_specs,
        out_specs=[blk(slots), blk(2*slots), full((rows,width))] + [full((mols,width,slots))]*8 + [full((rows,width))]*2,
        scratch_shapes=[pltpu.VMEM((mols, groups, slots, 256), BF)],
        compiler_params=pltpu.CompilerParams(vmem_limit_bytes=67043328, dimension_semantics=("arbitrary",)),
        name="attention_forward",
    )(lengths, types.reshape(mols,1,slots), feats, table, vec(gain), vec(shift), wq, vec(bq), wk, wv, vec(bv), wo, vec(bo), vec(fgain), vec(fshift), bias)


LOGICAL = pl.DeviceIdType.LOGICAL


class Place:
    def __init__(self, dpbits):
        tensor, dp = lax.axis_index("tensor"), lax.axis_index("dp")
        me = dp * 4 + tensor
        self.bits, self.partners = {}, {}
        for axis, index, count, stride in (("tensor", tensor, 2, 1), ("dp", dp, dpbits, 4)):
            for bit in range(count):
                value = lax.rem(lax.div(index, 1 << bit), 2)
                self.bits[axis, bit] = value
                self.partners[axis, bit] = me + (1 - 2 * value) * (stride << bit)


class Exchange:
    def __init__(self, at, src, dst, sems, slot, stage, before=None, after=None):
        self.before, self.after = before, after
        self.copy = lambda: pltpu.make_async_remote_copy(
            src_ref=src(), dst_ref=dst(), send_sem=sems.at[0, slot], recv_sem=sems.at[1, slot],
            device_id=at.partners[stage], device_id_type=LOGICAL)

    def start(self):
        if self.before is not None:
            self.before()
        self.copy().start()

    def wait(self):
        self.copy().wait()
        if self.after is not None:
            self.after()


class Pause:
    def __init__(self, wait):
        self.wait = wait

    def start(self):
        pass


class Job:
    def __init__(self, at, buf, recv, sems, free, first_slot, rows, stages, done=None):
        self.done = done
        self.slots = 0
        self.recv_rows = 0
        self.steps = []
        plan = []
        numbers = []
        length = rows
        for stage in stages:
            halve = (length // 2) % 8 == 0
            part = length // 2 if halve else length
            plan.append((stage, halve, length, part, self.recv_rows))
            self.recv_rows += part
            length = part
        halved = [p[0] for p in plan if p[1]]

        def offset(count):
            off, size = 0, rows
            for axis, bit in halved[:count]:
                size //= 2
                off = off + at.bits[axis, bit] * size
            return off if isinstance(off, int) else pl.multiple_of(off, 8)

        depth = 0
        for stage, halve, length, part, place in plan:
            here = depth
            if halve:
                depth += 1

                def src(stage=stage, here=here, part=part):
                    return buf.at[pl.ds(pl.multiple_of(offset(here) + (1 - at.bits[stage]) * part, 8), part)]
            else:
                def src(here=here, part=part):
                    return buf.at[pl.ds(offset(here), part)]

            def dst(place=place, part=part):
                return recv.at[pl.ds(place, part)]

            def add(depth=depth, place=place, part=part, to=buf):
                mine = pl.ds(offset(depth), part)
                to[mine, :] = buf[mine, :] + recv[pl.ds(place, part), :]

            number = first_slot + self.slots

            def tell(number=number, stage=stage):
                pl.semaphore_signal(free.at[number], inc=1, device_id=at.partners[stage], device_id_type=LOGICAL)

            self.steps.append((Exchange(at, src, dst, sems, number, stage, after=tell if halve else None), add))
            numbers.append(number)
            self.slots += 1
        if plan[-1][1]:
            self.steps.append((Pause(lambda number=numbers[-1]: pl.semaphore_wait(free.at[number], 1)), None))
        for (stage, halve, length, part, place), number in zip(reversed(plan), reversed(numbers)):
            if not halve:
                continue

            def freed(number=number):
                pl.semaphore_wait(free.at[number], 1)

            def region(depth=depth, part=part):
                return buf.at[pl.ds(offset(depth), part)]

            if number == numbers[-1]:
                freed = None
            self.steps.append((Exchange(at, region, region, sems, first_slot + self.slots, stage, before=freed), None))
            self.slots += 1
            depth -= 1
        self.ticks = len(self.steps) + 1

    def tick(self, k):
        if k > 0:
            exchange, add = self.steps[k - 1]
            exchange.wait()
            if add is not None:
                add()
        if k < len(self.steps):
            self.steps[k][0].start()
        elif self.done is not None:
            self.done()


class Actions:
    def __init__(self, *functions):
        self.tick = lambda k: functions[k]()


def job_need(rows, stages):
    job = Job(None, None, None, None, None, 0, rows, stages)
    return job.recv_rows, job.slots


ORDERS = ("CXYZW", "CXZWY", "CYXZW", "CYZWX", "CZWXY", "CXZYW", "CZXYW", "CZYXW")
E_ORDERS = ("YZW", "ZWY", "ZYW")


def stages_of(order, dpbits):
    table = {"C": [("tensor", 0)], "X": [("tensor", 1)], "Y": [("dp", i) for i in range(dpbits - 2)],
             "Z": [("dp", dpbits - 2)], "W": [("dp", dpbits - 1)]}
    return [stage for token in order for stage in table[token]]


def stage_cost(stage, size):
    rate = 43.0e3
    if stage is None:
        return [], 1.0 + size
    axis, bit = stage
    if axis == "tensor":
        return ([("core", size / 700e3)], 0.9) if bit == 0 else ([("x", size / rate)], 2.0)
    if bit == 0:
        return [("y", size / rate)], 2.0
    if bit == 1:
        return [("outer", size / rate)], 2.0
    return [("outer", size / rate), ("inner", 2 * size / rate)], 2.5


def tick_order(segments, jobs):
    now, free, flying, points, current = 0.0, {}, [], [], []
    segments = list(segments)
    ended = set()

    def start(name, k):
        stage, size, _ = jobs[name][k]
        links, latency = stage_cost(stage, size)
        begin = max([now] + [free.get(link, 0.0) for link, _ in links])
        for link, length in links:
            free[link] = begin + length
        flying.append((begin + max([length for _, length in links], default=0.0) + latency, name, k))

    while segments or flying:
        ready = [f for f in flying if f[0] <= now]
        if ready:
            first = min(ready)
            flying.remove(first)
            _, name, k = first
            now += 0.05 + (jobs[name][k][1] / 1.5e6 if jobs[name][k][2] else 0.0)
            current.append((name, k + 1))
            if k + 1 < len(jobs[name]):
                start(name, k + 1)
            else:
                ended.add(name)
        elif segments and all(name in ended for name in segments[0][3]):
            points.append(current)
            current = []
            _, length, released, _ = segments.pop(0)
            now += length
            for name in released:
                start(name, 0)
        else:
            now = min(f[0] for f in flying)
    points.append(current)
    return points[1:]


def job_steps(rows, width, stages, hold=0.0):
    length, out, back = rows, [], []
    for stage in stages:
        halve = (length // 2) % 8 == 0
        length = length // 2 if halve else length
        out.append((stage, length * width * 4, True))
        if halve:
            back.append((stage, length * width * 4, False))
    return out + ([(None, hold, False)] if halve else []) + back[::-1]


def make_plan(config, dpbits, mols, groups, width, hidden, small):
    ne, ch, fs, no = config["ne"], config["ch"], config["fs"], config["no"]
    jobs, steps = {}, {}

    def add(name, kind, index, first, rows, stages, cols):
        jobs[name] = (kind, index, first, rows, stages)
        steps[name] = job_steps(rows, cols, stages, config["hold"].get(name, 0.0))

    for i in range(ne):
        n = (width + hidden) // ne
        add("e%d" % i, "e", 0, i * n, n, stages_of(E_ORDERS[config["eo"][i]], dpbits), width)
    for i in range(no):
        n = width // no
        add("o%d" % i, "o", 0, i * n, n, stages_of(ORDERS[config["oo"][i]], dpbits), width)
    for c in range(ch):
        for h in range(fs):
            n = 3 * width // fs
            add("f%d_%d" % (c, h), "f", c, h * n, n, stages_of(ORDERS[config["fo"][c * fs + h]], dpbits), width // ch)
    add("s", "s", 0, 0, small, stages_of(ORDERS[config["so"]], dpbits), width)
    add("b", "b", 0, 0, 8, stages_of("YZW", dpbits), hidden)
    q = ne // 4
    pos = config["pos"]
    segments = []

    def put(moment):
        for k in range(4):
            if pos[k] == moment:
                segments.append((("e", k), 0.65 if k < 2 else 1.3, ["e%d" % i for i in range(k * q, (k + 1) * q)], []))
        if pos[4] == moment:
            segments.append((("down",), 2.3, ["d"], []))

    swap = width * width * 2
    steps["d"] = [(("tensor", 0), swap, True), (("tensor", 1), swap, False)]
    steps["n"] = [(("tensor", 0), swap // 2, True), (("tensor", 1), swap // 2, False)]
    segments.append((("ffn",), 0.0, ["n", "b"], []))
    put(-2)
    segments.append((("pro1",), 1.2, ["o%d" % i for i in range(no)], ["n"]))
    put(-1)
    segments.append((("pro2",), 1.0, [], []))
    per = groups // ch
    for s in range(mols * groups):
        segments.append((("step", s), 0.8, [], []))
        if (s + 1) % (per * mols) == 0:
            c = s // (per * mols)
            segments.append((("chunk", c), 5.0 / ch, ["f%d_%d" % (c, h) for h in range(fs)], []))
        put(s)
    segments.append((("end",), 0.6, ["s"], []))
    return jobs, segments, tick_order(segments, steps)


def gelu_and_slope(x):
    cdf = 0.5 + 0.5 * lax.erf(x * (0.5 ** 0.5))
    return x * cdf, cdf + x * (jnp.exp(-0.5 * x * x) * (1.0 / math.sqrt(2.0 * math.pi)))


def mm3_nt(ahi, alo, bhi, blo):
    return dot_nt(ahi, bhi) + (dot_nt(ahi, blo) + dot_nt(alo, bhi))


def mm3_nn(ahi, alo, bhi, blo):
    return dot(ahi, bhi) + (dot(ahi, blo) + dot(alo, bhi))


def main_kernel(plan, *refs):
    refs = list(refs)
    take_n = lambda n: [refs.pop(0) for _ in range(n)]
    len_ref, types_ref, normed2_any = take_n(3)
    cot_refs = take_n(2)
    held_any = take_n(10)
    gain_ref, shift_ref, fgain_ref, bup_ref, bdown_ref = take_n(5)
    wup_any, wdown_any, wq_any, wk_any, wv_any, wo_any, pair_any, e_any = take_n(8)
    gpair, outv, gatv, eres, ores, fres, sres, bres = take_n(8)
    dl, qhi, qlo, khi, klo, vhi, vlo, dmhi, dmlo, dqt, dkt, dvt, maskc, dmid, energy = take_n(15)
    wq, wk, wv, wo, wuhi, wulo, wdhi, wdlo = take_n(8)
    gath, cots, duhi, dulo, pn, pd, rsn, rsd, nt, dn1 = take_n(10)
    ebuf, erecv, obuf, orecv, fbuf, frecv, sbuf, srecv, tbuf, tres, trecv, bbuf, brecv = take_n(13)
    middle_ref, first_ref, mixt_ref, linv_ref, pring, ering = take_n(6)
    rsems, free, lsems = take_n(3)
    assert not refs
    s = pl.program_id(0)
    mols, slots = types_ref.shape[0], types_ref.shape[2]
    groups = dl.shape[1]
    heads = groups * 8
    width = wo.shape[0]
    hidden = wuhi.shape[1]
    rows = mols * slots
    types = plan["types"]
    last = mols * groups - 1
    at = Place(plan["dpbits"])
    core, xbit = ("tensor", 0), ("tensor", 1)
    dpbits = [("dp", i) for i in range(plan["dpbits"])]
    wide = [core, xbit] + dpbits
    jobs, segments, points = plan["jobs"], plan["segments"], plan["points"]
    chunks = plan["chunks"]
    fcols = width // chunks

    tiles = [(r, c) for r in range(rows // 128) for c in range(hidden // 128)]

    across = hidden // 128

    def keep(base, b, x, top=0):
        for i, (r, c) in enumerate(tiles):
            if r < x.shape[0] // 128:
                gpair[0, base + b * len(tiles) + top * across + i] = x[r * 128:(r + 1) * 128, c * 128:(c + 1) * 128]

    def kept(base, b, top=0, n=rows // 128):
        parts = [gpair[0, base + b * len(tiles) + top * across + i] for i in range(n * across)]
        return jnp.concatenate([jnp.concatenate(parts[r * across:(r + 1) * across], 1) for r in range(n)], 0)

    ACT, DACT = 0, 4 * len(tiles)
    slot = [0]

    def swap(src, dst, stage):
        slot[0] += 1
        return Exchange(at, lambda: src, lambda: dst, rsems, slot[0] - 1, stage)

    hrows = rows // 2
    hpart = [pl.ds(i * hrows, hrows) for i in range(2)]
    n_core = swap(normed2_any, gath.at[1], core)
    n_x = [swap(normed2_any.at[h], gath.at[2, h], xbit) for h in hpart]
    c_core = swap(cot_refs[0], cots.at[1], core)
    c_diag = swap(cot_refs[1], cots.at[3], core)
    n_diag = [swap(gath.at[2, h], gath.at[3, h], core) for h in hpart]
    dn_core = swap(pn.at[1], rsn.at[0], core)
    dn_diag = [swap(pn.at[3, h], rsn.at[1, h], core) for h in hpart]
    dn_x = [swap(pn.at[2, h], rsn.at[2, h], xbit) for h in hpart]
    dd_core = swap(pd.at[1], rsd.at[0], core)
    dd_diag = swap(pd.at[3], rsd.at[1], core)
    dd_x = swap(pd.at[2], rsd.at[2], xbit)

    def make(buf, res, recv, nrows, stages):
        def done():
            res[...] = buf[...]
        job = Job(at, buf, recv, rsems, free, slot[0], nrows, stages, done)
        slot[0] += job.slots
        return job

    total_job = make(tbuf, tres, trecv, 8, wide)
    running = {}
    place = {"e": 0, "o": 0, "f": 0}
    for name, (kind, index, first_row, nrows, stages) in jobs.items():
        if kind == "s":
            running[name] = make(sbuf, sres, srecv, nrows, stages)
        elif kind == "b":
            running[name] = make(bbuf, bres, brecv, nrows, stages)
        else:
            need = job_need(nrows, stages)[0]
            if kind == "f":
                buf, res, recv = fbuf.at[index], fres.at[index], frecv
            else:
                buf, res, recv = {"e": (ebuf, eres, erecv), "o": (obuf, ores, orecv)}[kind]
            running[name] = make(buf.at[pl.ds(first_row, nrows)], res.at[pl.ds(first_row, nrows)], recv.at[pl.ds(place[kind], need)], nrows, stages)
            place[kind] += need
    assert slot[0] == plan["slots"], slot[0]
    half = width // 2

    def n_sum(i):
        dn_diag[i].wait()
        pn[2, hpart[i], :] = pn[2, hpart[i], :] + rsn[1, hpart[i], :]
        dn_x[i].start()

    def n_end():
        dn_core.wait()
        dn_x[0].wait()
        dn_x[1].wait()

    def d_begin():
        dd_diag.start()
        dd_core.start()

    def d_sum():
        dd_diag.wait()
        pd[2] = pd[2] + rsd[1]
        dd_x.start()

    def d_end():
        dd_core.wait()
        dd_x.wait()
        outv[...] = middle_ref[...] + bdown_ref[...] + (pd[0] + (rsd[0] + rsd[2]))

    running["n"] = Actions(dn_diag[1].start, functools.partial(n_sum, 1), n_end)
    running["d"] = Actions(d_begin, d_sum, d_end)

    cot_load = [pltpu.make_async_copy(cot_refs[b], cots.at[2 * b], lsems.at[b]) for b in range(2)]
    piece = width // rows
    up_load = [pltpu.make_async_copy(wup_any.at[pl.ds(i * rows, rows)], pn.at[i], lsems.at[4 + i]) for i in range(piece)]
    down_load = [pltpu.make_async_copy(wdown_any.at[pl.ds(i * rows, rows)], pn.at[2 + i], lsems.at[6 + i]) for i in range(piece)]
    load = [pltpu.make_async_copy(a, b, lsems.at[8 + i]) for i, (a, b) in enumerate(((wo_any, wo), (wq_any, wq), (wk_any, wk), (wv_any, wv)))]
    own_load = pltpu.make_async_copy(normed2_any, gath.at[0], lsems.at[12])
    held = (first_ref, middle_ref, qhi, qlo, khi, klo, vhi, vlo, mixt_ref, linv_ref)
    held_load = [pltpu.make_async_copy(a, b, lsems.at[13 + i]) for i, (a, b) in enumerate(zip(held_any, held))]
    depth = pring.shape[0]

    def ring(step):
        which = lax.rem(step, depth)
        mol, first_head = lax.rem(step, mols), lax.div(step, mols) * 8
        return [pltpu.make_async_copy(a.at[mol, pl.ds(first_head, 8)], r.at[which], lsems.at[23 + i * depth + which])
                for i, (a, r) in enumerate(((pair_any, pring), (e_any, ering)))]

    def seg_ffn():
        barrier = pltpu.get_barrier_semaphore()
        for stage in wide:
            pl.semaphore_signal(barrier, inc=1, device_id=at.partners[stage], device_id_type=LOGICAL)
        pl.semaphore_wait(barrier, len(wide))
        for copy in n_x:
            copy.start()
        c_core.start()
        c_diag.start()
        n_core.start()
        for copy in down_load + cot_load[:1] + up_load + cot_load[1:] + [own_load]:
            copy.start()
        square = jnp.zeros((1, 1), F32)
        for m in range(mols):
            f = jnp.full((1, 1), len_ref[m], jnp.int32).astype(F32)
            square = square + f * f
        tbuf[...] = jnp.broadcast_to(square, tbuf.shape)
        total_job.tick(0)
        bbuf[...] = jnp.zeros_like(bbuf)
        sbuf[...] = jnp.zeros_like(sbuf)
        for copy in down_load:
            copy.wait()
        for i in range(piece):
            part = pl.ds(i * rows, rows)
            wdhi[part, :], wdlo[part, :] = split(pn[2 + i])
        for copy in cot_load + up_load:
            copy.wait()
        for i in range(piece):
            part = pl.ds(i * rows, rows)
            wuhi[part, :], wulo[part, :] = split(pn[i])
        total_job.tick(1)
        for copy in held_load + load:
            copy.start()
        for step in range(depth - 1):
            for copy in ring(step):
                copy.start()

        def p1(b, carry):
            hi, lo = split(cots[b])
            keep(DACT, b, mm3_nt(hi, lo, wdhi[...], wdlo[...]))
            return carry

        lax.fori_loop(0, 2, lambda b, carry: p1(2 * b, carry), 0)
        c_core.wait()
        c_diag.wait()
        lax.fori_loop(0, 2, lambda b, carry: p1(2 * b + 1, carry), 0)
        own_load.wait()
        n_core.wait()
        total_job.tick(2)

        def p2(b, top=0, n=rows // 128):
            part = pl.ds(top * 128, n * 128)
            hi, lo = split(gath[b, part, :])
            upper = mm3_nn(hi, lo, wuhi[...], wulo[...]) + bup_ref[...]
            a, slope = gelu_and_slope(upper)
            keep(ACT, b, a, top)
            du = kept(DACT, b, top, n) * slope
            dhi, dlo = split(du)
            duhi[b, part, :] = dhi
            dulo[b, part, :] = dlo
            bbuf[...] = bbuf[...] + jnp.broadcast_to(jnp.sum(du, axis=0, keepdims=True), bbuf.shape)
            pn[b, part, :] = mm3_nt(dhi, dlo, wuhi[...], wulo[...])

        def p2_loop(b, carry):
            p2(b)
            return carry

        lax.fori_loop(0, 2, p2_loop, 0)
        dn_core.start()
        first_work()
        n = hrows // 128
        for i in range(2):
            n_x[i].wait()
            n_diag[i].start()
            p2(2, i * n, n)
            n_diag[i].wait()
            p2(3, i * n, n)
            total_job.tick(3 + i)
            if i == 0:
                dn_diag[0].start()
                n_sum(0)
        running["n"].tick(0)
        running["b"].tick(0)

    def first_work():
        for copy in held_load:
            copy.wait()
        first = first_ref[...]
        cen = first - jnp.mean(first, axis=-1, keepdims=True)
        rstd = lax.rsqrt(jnp.mean(cen * cen, axis=-1, keepdims=True) + EPSILON)
        normed = cen * rstd * gain_ref[...] + shift_ref[...]
        for m in range(mols):
            nt[:, m * slots:(m + 1) * slots] = jnp.transpose(normed[m * slots:(m + 1) * slots])
        dn1[...] = jnp.zeros_like(dn1)
        energy[...] = jnp.zeros_like(energy)
        for k in range(2):
            lax.fori_loop(0, 2, functools.partial(weight_part, k), 0)

    def down_part(b, carry):
        hi, lo = split(kept(ACT, b))
        pd[b] = mm3_nn(hi, lo, wdhi[...], wdlo[...])
        return carry

    def weight_part(k, b, carry):
        part = slice((k % 2) * half, (k % 2 + 1) * half)
        left = kept(ACT, b)[:, part] if k < 2 else gath[b, :, part]
        ahi, alo = split(jnp.transpose(left))
        if k < 2:
            chi, clo = split(cots[b])
        else:
            chi, clo = duhi[b], dulo[b]
        g = mm3_nn(ahi, alo, chi, clo)
        to = pl.ds(k * half, half)

        @pl.when(b == 0)
        def _():
            ebuf[to, :] = g

        @pl.when(b > 0)
        def _():
            ebuf[to, :] = ebuf[to, :] + g
        return carry

    def seg_e(k):
        lax.fori_loop(2 if k < 2 else 0, 4, functools.partial(weight_part, k), 0)
        q = plan["ne"] // 4
        for i in range(k * q, (k + 1) * q):
            running["e%d" % i].tick(0)

    def seg_down():
        lax.fori_loop(0, 4, down_part, 0)
        running["d"].tick(0)

    def small(i, value):
        sbuf[types + i:types + i + 1, :] = value

    def seg_pro1():
        mid = middle_ref[...]
        cen = mid - jnp.mean(mid, axis=-1, keepdims=True)
        rstd = lax.rsqrt(jnp.mean(cen * cen, axis=-1, keepdims=True) + EPSILON)
        xhat = cen * rstd
        c = pn[0] + (rsn[0] + rsn[2])
        small(0, jnp.sum(c * xhat, axis=0, keepdims=True))
        small(1, jnp.sum(c, axis=0, keepdims=True))
        cot = cots[0]
        small(2, jnp.sum(cot, axis=0, keepdims=True))
        ce = c * fgain_ref[...]
        dmiddle = cot + rstd * (ce - jnp.mean(ce, axis=-1, keepdims=True) - xhat * jnp.mean(ce * xhat, axis=-1, keepdims=True))
        dmid[...] = dmiddle
        small(3, jnp.sum(dmiddle, axis=0, keepdims=True))
        for copy in load:
            copy.wait()
        dhi, dlo = split(dmiddle)
        mhi, mlo = split(jnp.concatenate([mixt_ref[m] for m in range(mols)], 1))
        obuf[...] = mm3_nn(mhi, mlo, dhi, dlo)
        for i in range(plan["no"]):
            running["o%d" % i].tick(0)

    def seg_pro2():
        for k in range(5, total_job.ticks):
            total_job.tick(k)
        wohi, wolo = split(wo[...])
        dhi, dlo = split(dmid[...])
        dm = mm3_nt(dhi, dlo, wohi, wolo)
        lane = lax.broadcasted_iota(jnp.int32, (slots, 128), 1)
        rowi = lax.broadcasted_iota(jnp.int32, (slots, slots), 0)
        coli = lax.broadcasted_iota(jnp.int32, (slots, slots), 1)
        twice = 2.0 / (heads * tres[0:1, 0:slots])
        for m in range(mols):
            length = len_ref[m]
            maskc[m] = jnp.where(jnp.logical_and(rowi < length, coli < length), twice, 0.0)
            dmt = jnp.transpose(dm[m * slots:(m + 1) * slots]) * linv_ref[m]
            dmhi[m], dmlo[m] = split(dmt)
            prod = dmt * mixt_ref[m]
            delta = jnp.sum(prod.reshape(heads, 8, slots), axis=1)
            for g in range(groups):
                d8 = -delta[g * 8:(g + 1) * 8]
                x = jnp.concatenate([dmt[g * 64:(g + 1) * 64], d8, d8, jnp.zeros((48, slots), F32)], 0)
                y = jnp.transpose(x)
                yhi = y.astype(BF).astype(F32)
                ylo = y - yhi
                dl[m, g, :, 0:128] = jnp.where(lane < 64, yhi, pltpu.roll(ylo, 64, 1)).astype(BF)
                dl[m, g, :, 128:256] = jnp.where(lane < 72, yhi, ylo).astype(BF)

    def seg_chunk(c):
        part = slice(c * fcols, (c + 1) * fcols)
        nhi, nlo = split(nt[...])
        for i, t_ref in enumerate((dqt, dkt, dvt)):
            thi, tlo = split(jnp.concatenate([t_ref[mm, part, :] for mm in range(mols)], 1))
            fbuf[c, i * width:(i + 1) * width, :] = mm3_nt(nhi, nlo, thi, tlo)
        for h in range(plan["fs"]):
            running["f%d_%d" % (c, h)].tick(0)
        acc = dn1[...]
        for i, (t_ref, w) in enumerate(((dqt, wq), (dkt, wk), (dvt, wv))):
            nat = jnp.concatenate([jnp.transpose(t_ref[mm, part, :]) for mm in range(mols)], 0)
            if i != 1:
                r = types + (4 if i == 0 else 5)
                sbuf[r:r + 1, part] = jnp.sum(nat, axis=0, keepdims=True)
            ahi, alo = split(nat)
            whi, wlo = split(w[:, part])
            acc = acc + mm3_nt(ahi, alo, whi, wlo)
        dn1[...] = acc

    def seg_end():
        first = first_ref[...]
        cen = first - jnp.mean(first, axis=-1, keepdims=True)
        rstd = lax.rsqrt(jnp.mean(cen * cen, axis=-1, keepdims=True) + EPSILON)
        xhat = cen * rstd
        dn = dn1[...]
        small(6, jnp.sum(dn * xhat, axis=0, keepdims=True))
        small(7, jnp.sum(dn, axis=0, keepdims=True))
        ge = dn * gain_ref[...]
        gat = dmid[...] + rstd * (ge - jnp.mean(ge, axis=-1, keepdims=True) - xhat * jnp.mean(ge * xhat, axis=-1, keepdims=True))
        gatv[...] = gat
        acc = None
        for mm in range(mols):
            one = (lax.broadcasted_iota(jnp.int32, (types, slots), 0) == types_ref[mm]).astype(F32).astype(BF)
            for bits in split3(gat[mm * slots:(mm + 1) * slots]):
                part = dot(one, bits)
                acc = part if acc is None else acc + part
        sbuf[0:types, :] = acc
        total = jnp.sum(jnp.sum(energy[...], axis=0, keepdims=True), axis=1, keepdims=True) * 0.5
        small(8, jnp.broadcast_to(total, (1, width)))
        running["s"].tick(0)

    work = {"ffn": seg_ffn, "e": seg_e, "down": seg_down, "pro1": seg_pro1, "pro2": seg_pro2, "chunk": seg_chunk, "end": seg_end}
    before, after = [], {}
    step_now = None
    for (name, _, _, _), ticks in zip(segments, points):
        if name[0] == "step":
            step_now = name[1]
        else:
            to = before if step_now is None else after.setdefault(step_now, [])
            to.append(functools.partial(work[name[0]], *name[1:]))
        to = before if step_now is None else after.setdefault(step_now, [])
        to += [functools.partial(running[job].tick, k) for job, k in ticks]

    @pl.when(s == 0)
    def _():
        for fn in before:
            fn()

    g = s // mols
    m = s % mols
    lhs = dl[m, g]
    which = lax.rem(s, depth)
    for copy in ring(s):
        copy.wait()

    @pl.when(s + depth - 1 <= last)
    def _():
        for copy in ring(s + depth - 1):
            copy.start()

    sub = lax.broadcasted_iota(jnp.int32, (16, 128), 0)
    z = jnp.zeros((16, 256), BF)
    zero16 = jnp.zeros((16, 128), BF)
    mc = maskc[m]
    en = energy[...]
    for p in range(4):
        row = pl.multiple_of(g * 64 + 16 * p, 16)
        rows16 = pl.ds(row, 16)

        def blk(x):
            x = x.astype(F32)
            a = jnp.where(sub < 8, x, 0.0).astype(BF)
            b = jnp.where(sub >= 8, x, 0.0).astype(BF)
            return jnp.concatenate([a, b], axis=1)
        bhi, blo = blk(vhi[m, rows16, :]), blk(vlo[m, rows16, :])
        sel = jnp.concatenate([jnp.where(sub % 8 == 2 * p, 1.0, 0.0), jnp.where(sub % 8 == 2 * p + 1, 1.0, 0.0)], axis=1).astype(BF)
        rws = [bhi if i == p else z for i in range(4)]
        rws += rws
        rws += [blo if i == p else z for i in range(4)]
        rws += [sel, z, z, z]
        dp = dot(lhs, jnp.concatenate(rws, axis=0))
        gs = []
        es = []
        for hf in range(2):
            both = ering[which, 2 * p + hf]
            es.append(both)
            e = both[:, 0:128].astype(F32) + both[:, 128:256].astype(F32)
            logits = pring[which, 2 * p + hf]
            t = logits * mc
            en = en + t * logits
            gp = e * dp[:, hf * 128:(hf + 1) * 128] + t
            gpair[m, g * 8 + 2 * p + hf] = gp
            gs.append(split(gp))

        def rows_lhs(hi, lo):
            return jnp.concatenate([jnp.concatenate([hi, hi], 1), jnp.concatenate([lo, zero16], 1)], 0)

        def take(out):
            acc = out[0:16] + out[16:32]
            return jnp.concatenate([acc[0:8, 0:128], acc[8:16, 128:256]], 0)
        ecol = jnp.concatenate([jnp.concatenate([es[0][:, 0:128], es[1][:, 0:128]], 1), jnp.concatenate([es[0][:, 128:256], es[1][:, 128:256]], 1)], 0)
        dvt[m, rows16, :] = take(dot(rows_lhs(dmhi[m, rows16, :], dmlo[m, rows16, :]), ecol))
        gcol = jnp.concatenate([jnp.concatenate([gs[0][0], gs[1][0]], 1), jnp.concatenate([gs[0][1], gs[1][1]], 1)], 0)
        dkt[m, rows16, :] = take(dot(rows_lhs(qhi[m, rows16, :], qlo[m, rows16, :]), gcol))
        grow = jnp.concatenate([jnp.concatenate(gs[0], 1), jnp.concatenate(gs[1], 1)], 0)
        dqt[m, rows16, :] = take(dot_nt(rows_lhs(khi[m, rows16, :], klo[m, rows16, :]), grow)) * (8 ** -0.5)
    energy[...] = en

    for moment in sorted(after):
        def body(moment=moment):
            for fn in after[moment]:
                fn()
        pl.when(s == moment)(body)


CONFIG = dict(ne=8, ch=4, fs=3, no=2, eo=[1, 0, 1, 0, 0, 0, 0, 0], fo=[5, 0, 5, 2, 2, 0, 2, 1, 0, 0, 5, 0], oo=[0, 2], so=2, pos=[-2, -2, -2, -2, -2], hold={'e2': 32, 'e0': 32, 'e3': 32, 'e7': 24, 'o1': 8, 'e4': 4, 'o0': 4, 'e6': 2, 'f2_1': 2, 'f0_0': 8, 'f3_2': 2, 'f1_2': 2, 'f3_1': 2, 'f2_0': 2})


def main_call(mesh, lengths, types, normed2, cots, held, gain, shift, fgain, bup, bdown,
              wup, wdown, wq, wk, wv, wo, pair, e, ntypes):
    mols, slots = types.shape
    rows, width = normed2.shape
    heads = pair.shape[1]
    groups = heads // 8
    hidden = wup.shape[1]
    dp = mesh.shape["dp"]
    dpbits = dp.bit_length() - 1
    assert (1 << dpbits) == dp and mesh.shape["tensor"] == 4
    small = -(-(ntypes + 9) // 64) * 64
    config = CONFIG if dpbits <= 3 else dict(ne=4, ch=1, fs=1, no=1, eo=[0] * 4, fo=[0], oo=[0], so=0, pos=[-2, -2, -2, -2, -2], hold={})
    jobs, segments, points = make_plan(config, dpbits, mols, groups, width, hidden, small)
    chunks = config["ch"]
    fcols = width // chunks
    needs = {"e": 0, "o": 0, "f": 0, "s": 0, "b": 0}
    stages = stages_of("CXYZW", dpbits)
    t_need = job_need(8, stages)
    nslots = 15 + t_need[1]
    for kind, index, first_row, nrows, order in jobs.values():
        need = job_need(nrows, order)
        needs[kind] += need[0]
        nslots += need[1]
    plan = dict(dpbits=dpbits, chunks=chunks, types=ntypes, slots=nslots, jobs=jobs, segments=segments, points=points,
                ne=config["ne"], no=config["no"], fs=config["fs"])
    V = pltpu.VMEM
    one = lambda shape: pl.BlockSpec(shape, lambda s: (0,) * len(shape), pipeline_mode=pl.Buffered(1))
    any_ = pl.BlockSpec(memory_space=pl.ANY)
    smem = pl.BlockSpec(memory_space=pltpu.SMEM)
    vmem = pl.BlockSpec(memory_space=pltpu.VMEM)
    vec = lambda v: v.reshape(1, -1)
    tt = (mols, width, slots)
    rw = (rows, width)
    in_specs = [smem, one((mols, 1, slots))] + [any_] * 13 + \
        [one((1, width))] * 3 + [one((1, hidden)), one((1, width))] + [any_] * 8
    ww = (width, width)
    ff = (width + hidden, width)
    outs = [V(pair.shape, F32), V(rw, F32), V(rw, F32), V(ff, F32), V(ww, F32), V((chunks, 3 * width, fcols), F32), V((small, width), F32), V((8, hidden), F32)]
    four = (4, rows, width)
    scratch = [V((mols, groups, slots, 256), BF)] + [V(tt, BF)] * 8 + [V(tt, F32)] * 3 + [V((mols, slots, slots), F32), V(rw, F32), V((slots, slots), F32)]
    scratch += [V(ww, F32)] * 4 + [V((width, hidden), BF)] * 2 + [V((hidden, width), BF)] * 2
    scratch += [V(four, F32)] * 2 + [V(four, BF)] * 2 + [V(four, F32)] * 2 + [V((3, rows, width), F32)] * 2 + [V((width, rows), F32), V(rw, F32)]
    scratch += [V(ff, F32), V((needs["e"], width), F32), V(ww, F32), V((needs["o"], width), F32)]
    scratch += [V((chunks, 3 * width, fcols), F32), V((needs["f"], fcols), F32), V((small, width), F32), V((needs["s"], width), F32)]
    scratch += [V((8, 128), F32)] * 2 + [V((t_need[0], 128), F32), V((8, hidden), F32), V((needs["b"], hidden), F32)]
    scratch += [V(rw, F32)] * 2 + [V(tt, F32)] * 2 + [V((DEPTH, 8, slots, slots), F32), V((DEPTH, 8, slots, 2 * slots), BF)]
    scratch += [pltpu.SemaphoreType.DMA((2, nslots)), pltpu.SemaphoreType.REGULAR((nslots,)), pltpu.SemaphoreType.DMA((23 + 2 * DEPTH,))]
    return pl.pallas_call(functools.partial(main_kernel, plan), out_shape=outs, grid=(mols * groups,), in_specs=in_specs, out_specs=[vmem] * 8,
        scratch_shapes=scratch,
        compiler_params=pltpu.CompilerParams(vmem_limit_bytes=VLIMIT, dimension_semantics=("arbitrary",), collective_id=0, has_side_effects=True),
        name="feed_forward_and_backward",
    )(lengths, types.reshape(mols, 1, slots), normed2, *cots, *held, vec(gain), vec(shift), vec(fgain), vec(bup), vec(bdown),
      wup, wdown, wq, wk, wv, wo, pair, e)


DEPTH = 4
VLIMIT = 47 * 1024 * 1024
SMALL_ROWS = (0, 1, 2, 3, 4, 5, 6, 7)


def finish_kernel(types, gpair, outv, gatv, eres, ores, fres, sres, bres, *refs):
    refs = list(refs)
    gp_out, atom_out, gatoms_out, gdown_out, gup_out, gwo_out, gwq_out, gwk_out, gwv_out, table_out = [refs.pop(0) for _ in range(10)]
    rows_out = [refs.pop(0) for _ in range(len(SMALL_ROWS))]
    gbup_out, pen_out, sems = refs
    width = outv.shape[1]
    hidden = eres.shape[0] - width
    copies = []

    def go(src, dst):
        copy = pltpu.make_async_copy(src, dst, sems.at[len(copies)])
        copy.start()
        copies.append(copy)

    for m in range(gpair.shape[0]):
        for h in range(0, gpair.shape[1], 16):
            go(gpair.at[m, pl.ds(h, 16)], gp_out.at[m, pl.ds(h, 16)])
    go(eres.at[pl.ds(0, hidden)], gdown_out)
    go(eres.at[pl.ds(hidden, width)], gup_out)
    go(ores, gwo_out)
    chunks, _, fcols = fres.shape
    for c in range(chunks):
        for j, out in enumerate((gwq_out, gwk_out, gwv_out)):
            go(fres.at[c, pl.ds(j * width, width)], out.at[:, pl.ds(c * fcols, fcols)])
    go(outv, atom_out)
    go(gatv, gatoms_out)
    go(sres.at[pl.ds(0, types)], table_out)
    for i, out in zip(SMALL_ROWS, rows_out):
        out[...] = sres[types + i, :]
    gbup_out[...] = bres[0, :]
    pen_out[0, 0] = jnp.sum(sres[types + 8:types + 9, 0:1])
    for copy in copies:
        copy.wait()


def finish(types, parts, width, hidden):
    gpair, outv, gatv, eres, ores, fres, sres, bres = parts
    S = jax.ShapeDtypeStruct
    any_ = pl.BlockSpec(memory_space=pl.ANY)
    vmem = pl.BlockSpec(memory_space=pltpu.VMEM)
    shapes = [gpair.shape, outv.shape, gatv.shape, (hidden, width), (width, hidden)] + [(width, width)] * 4 + [(types, width)]
    outs = [S(shape, F32) for shape in shapes] + [S((width,), F32)] * len(SMALL_ROWS) + [S((hidden,), F32), S((1, 1), F32)]
    ncopies = gpair.shape[0] * gpair.shape[1] // 16 + 6 + 3 * fres.shape[0]
    return pl.pallas_call(functools.partial(finish_kernel, types), out_shape=outs, in_specs=[vmem] * 8,
        out_specs=[any_] * 10 + [vmem] * (len(SMALL_ROWS) + 1) + [pl.BlockSpec(memory_space=pltpu.SMEM)],
        scratch_shapes=[pltpu.SemaphoreType.DMA((ncopies,))], compiler_params=pltpu.CompilerParams(vmem_limit_bytes=4 * 1024 * 1024),
        name="finish")(*parts)


def local(mesh, atom_types, lengths, atom_feats, pair_bias, out_cotangent, type_table, norm_gain, norm_shift, w_query, b_query,
          w_key, w_value, b_value, w_out, b_out, ffn_gain, ffn_shift, w_up, b_up, w_down, b_down):
    tensor = mesh.shape["tensor"]
    cots = [out_cotangent, lax.ppermute(out_cotangent, "tensor", [(i, i ^ 2) for i in range(tensor)])]
    pair_out, e, first, qhi, qlo, khi, klo, vhi, vlo, mixt, linv, middle, normed2 = attention_forward(
        lengths, atom_types, atom_feats, type_table, norm_gain, norm_shift, w_query, b_query, w_key, w_value, b_value, w_out, b_out,
        ffn_gain, ffn_shift, pair_bias)
    types = type_table.shape[0]
    parts = main_call(
        mesh, lengths, atom_types, normed2, cots, (first, middle, qhi, qlo, khi, klo, vhi, vlo, mixt, linv), norm_gain, norm_shift, ffn_gain, b_up, b_down,
        w_up, w_down, w_query, w_key, w_value, w_out, pair_out, e, types)
    (grad_pair, atom_out, grad_atoms, gwdown, gwup, gwo, gwq, gwk, gwv, table, g_fgain, g_fshift, g_bdown, g_bout, g_bq, g_bv, g_gain, g_shift,
     gbup, penalty) = finish(types, parts, w_up.shape[0], w_up.shape[1])
    return (atom_out, pair_out, penalty.reshape(()), grad_atoms, grad_pair, table, g_gain, g_shift, gwq, g_bq, gwk, gwv, g_bv,
            gwo, g_bout, g_fgain, g_fshift, gwup, gbup, gwdown, g_bdown)


def solution(mesh):
    in_specs = (
        P(("dp", "tensor"), None),
        P(("dp", "tensor")),
        P(("dp", "tensor"), None),
        P(("dp", "tensor"), None, None, None),
        P(("dp", "tensor"), None),
        P(),
        P(),
        P(),
        P(),
        P(),
        P(),
        P(),
        P(),
        P(),
        P(),
        P(),
        P(),
        P(None, "tensor"),
        P("tensor"),
        P("tensor", None),
        P(),
    )
    out_specs = (
        P(("dp", "tensor"), None),
        P(("dp", "tensor"), None, None, None),
        P(),
        P(("dp", "tensor"), None),
        P(("dp", "tensor"), None, None, None),
        P(),
        P(),
        P(),
        P(),
        P(),
        P(),
        P(),
        P(),
        P(),
        P(),
        P(),
        P(),
        P(None, "tensor"),
        P("tensor"),
        P("tensor", None),
        P(),
    )
    return jax.shard_map(functools.partial(local, mesh), mesh=mesh, in_specs=in_specs, out_specs=out_specs, check_vma=False)
```

```python
import functools, math
import jax, jax.numpy as jnp
from jax import lax
from jax.experimental import pallas as pl
from jax.experimental.pallas import tpu as pltpu
from jax.sharding import PartitionSpec as P
F32=jnp.float32; BF=jnp.bfloat16
EPSILON=1e-5
SPAN=2

def split(x):
    hi = x.astype(BF)
    lo = (x - hi.astype(F32)).astype(BF)
    return hi, lo

def split3(x):
    hi = x.astype(BF)
    r = x - hi.astype(F32)
    mid = r.astype(BF)
    lo = (r - mid.astype(F32)).astype(BF)
    return hi, mid, lo

def dot(a, b):
    return jnp.dot(a, b, preferred_element_type=F32)

def dot_nt(a, b):
    return lax.dot_general(a, b, (((1,), (1,)), ((), ())), preferred_element_type=F32)

def mm3(a, bhi, blo):
    ahi, alo = split(a)
    return dot(ahi, bhi) + (dot(ahi, blo) + dot(alo, bhi))

def fwd_kernel(len_ref, types_ref, feats_ref, table_ref, gain_ref, shift_ref, wq_ref, bq_ref, wk_ref, wv_ref, bv_ref,
               wo_ref, bo_ref, fgain_ref, fshift_ref, bias_ref,
               pair_ref, e_ref, first_ref, qthi, qtlo, kthi, ktlo, vthi, vtlo, mixt_ref, linv_ref, middle_ref, normed_ref,
               ql, *, span):
    s = pl.program_id(0)
    mols, slots = types_ref.shape[0], types_ref.shape[2]
    groups = ql.shape[1]
    @pl.when(s == 0)
    def _():
        tab = split3(table_ref[...])
        types = table_ref.shape[0]
        for m in range(mols):
            ids = types_ref[m]
            oneT = (lax.broadcasted_iota(jnp.int32, (slots, slots), 0) == ids).astype(F32)
            one = jnp.transpose(oneT)[:, :types].astype(BF)
            rows = pl.ds(m*slots, slots)
            first = feats_ref[rows, :] + (dot(one, tab[0]) + (dot(one, tab[1]) + dot(one, tab[2])))
            first_ref[rows, :] = first
        first = first_ref[...]
        cen = first - jnp.mean(first, axis=-1, keepdims=True)
        var = jnp.mean(cen*cen, axis=-1, keepdims=True)
        normed = cen * lax.rsqrt(var + EPSILON) * gain_ref[...] + shift_ref[...]
        nhi, nlo = split(normed)
        def proj(w_ref):
            whi, wlo = split(w_ref[...])
            return dot(nhi, whi) + (dot(nhi, wlo) + dot(nlo, whi))
        q = (proj(wq_ref) + bq_ref[...]) * (8 ** -0.5)
        k = proj(wk_ref)
        v = proj(wv_ref) + bv_ref[...]
        lane = lax.broadcasted_iota(jnp.int32, (slots, 128), 1)
        for m in range(mols):
            sl = slice(m*slots, (m+1)*slots)
            qm = q[sl]
            qthi[m], qtlo[m] = split(jnp.transpose(qm))
            kt = jnp.transpose(k[sl])
            kthi[m], ktlo[m] = split(kt)
            vt = jnp.transpose(v[sl])
            vthi[m], vtlo[m] = split(vt)
            for t in range(groups // 2):
                tile = qm[:, t*128:(t+1)*128]
                rolled = pltpu.roll(tile, 64, 1)
                for half in range(2):
                    dup = jnp.where(lane < 64, tile, rolled) if half == 0 else jnp.where(lane < 64, rolled, tile)
                    hi, lo = split(dup)
                    hi32, lo32 = hi.astype(F32), lo.astype(F32)
                    ql[m, 2*t+half, :, 0:128] = jnp.where(lane < 64, hi32, lo32).astype(BF)
                    ql[m, 2*t+half, :, 128:256] = jnp.where(lane < 64, hi32, 0.0).astype(BF)
    per = groups // span
    m = s // per
    length = len_ref[m]
    col_live = lax.broadcasted_iota(jnp.int32, (slots, slots), 1) < length
    sub = lax.broadcasted_iota(jnp.int32, (16, 128), 0)
    zero16 = jnp.zeros((16, 128), BF)
    ones = jnp.ones((16, 256), BF)
    def one(i, carry):
        g = (s % per) * span + i
        h0 = i * 8
        lhs = ql[m, g]
        for p in range(4):
            row = pl.multiple_of(g*64 + 16*p, 16)
            khi = kthi[m, pl.ds(row, 16), :].astype(F32)
            klo = ktlo[m, pl.ds(row, 16), :].astype(F32)
            def blk(x):
                a = jnp.where(sub < 8, x, 0.0).astype(BF)
                b = jnp.where(sub >= 8, x, 0.0).astype(BF)
                return jnp.concatenate([a, b], axis=1)
            bhi, blo = blk(khi), blk(klo)
            z = jnp.concatenate([zero16, zero16], axis=1)
            rows = [bhi if i == p else z for i in range(4)]
            rows += rows
            rows += [blo if i == p else z for i in range(4)]
            rows += [z]*4
            rhs = jnp.concatenate(rows, axis=0)
            lg = dot(lhs, rhs)
            ehl = []
            for half in range(2):
                logits = lg[:, half*128:(half+1)*128] + bias_ref[0, h0 + 2*p+half].astype(F32)
                pair_ref[0, h0 + 2*p+half] = logits
                masked = jnp.where(col_live, logits, -1e30)
                top = jnp.max(masked, axis=1, keepdims=True)
                e = jnp.exp(masked - top)
                hi, lo = split(e)
                both = jnp.concatenate([hi, lo], axis=1)
                e_ref[0, h0 + 2*p+half] = both
                ehl.append(both)
            vhi = vthi[m, pl.ds(row, 16), :]
            vlo = vtlo[m, pl.ds(row, 16), :]
            lv = jnp.concatenate([jnp.concatenate([vhi, vhi], 1), jnp.concatenate([vlo, zero16], 1), ones], 0)
            out = dot_nt(lv, jnp.concatenate(ehl, 0))
            acc = out[0:16] + out[16:32]
            sums = out[32:48]
            inv = 1.0 / jnp.concatenate([sums[0:8, 0:128], sums[8:16, 128:256]], 0)
            linv_ref[m, pl.ds(row, 16), :] = inv
            mixt_ref[m, pl.ds(row, 16), :] = jnp.concatenate([acc[0:8, 0:128], acc[8:16, 128:256]], 0) * inv
        return carry

    if span == 1:
        one(0, 0)
    else:
        lax.fori_loop(0, span, one, 0)
    @pl.when(s == mols*groups // span - 1)
    def _():
        mix = jnp.concatenate([jnp.transpose(mixt_ref[m]) for m in range(mols)], 0)
        whi, wlo = split(wo_ref[...])
        mid = first_ref[...] + (mm3(mix, whi, wlo) + bo_ref[...])
        middle_ref[...] = mid
        mcen = mid - jnp.mean(mid, axis=-1, keepdims=True)
        mvar = jnp.mean(mcen*mcen, axis=-1, keepdims=True)
        normed_ref[...] = mcen * lax.rsqrt(mvar + EPSILON) * fgain_ref[...] + fshift_ref[...]

def attention_forward(lengths, types, feats, table, gain, shift, wq, bq, wk, wv, bv, wo, bo, fgain, fshift, bias):
    mols, slots = types.shape
    width = feats.shape[1]
    heads = bias.shape[1]
    groups = heads // 8
    rows = mols*slots
    full = lambda shape: pl.BlockSpec(shape, lambda s: (0,)*len(shape))
    vec = lambda v: v.reshape(1, -1)
    outs = [jax.ShapeDtypeStruct((mols, heads, slots, slots), F32),
            jax.ShapeDtypeStruct((mols, heads, slots, 2*slots), BF),
            jax.ShapeDtypeStruct((rows, width), F32)] + [jax.ShapeDtypeStruct((mols, width, slots), BF)]*6 + [jax.ShapeDtypeStruct((mols, width, slots), F32)]*2 + [jax.ShapeDtypeStruct((rows, width), F32)]*2
    blk = lambda w: pl.BlockSpec((1, 8*SPAN, slots, w), lambda s: (s // (groups // SPAN), s % (groups // SPAN), 0, 0))
    in_specs = [pl.BlockSpec(memory_space=pltpu.SMEM), full((mols,1,slots)), full((rows,width)), full(table.shape), full((1,width)), full((1,width)),
                full(wq.shape), full((1,width)), full(wk.shape), full(wv.shape), full((1,width)), full(wo.shape), full((1,width)), full((1,width)), full((1,width)), blk(slots)]
    return pl.pallas_call(functools.partial(fwd_kernel, span=SPAN), out_shape=outs, grid=(mols*groups // SPAN,), in_specs=in_specs,
        out_specs=[blk(slots), blk(2*slots), full((rows,width))] + [full((mols,width,slots))]*8 + [full((rows,width))]*2,
        scratch_shapes=[pltpu.VMEM((mols, groups, slots, 256), BF)],
        compiler_params=pltpu.CompilerParams(vmem_limit_bytes=67043328, dimension_semantics=("arbitrary",)),
        name="attention_forward",
    )(lengths, types.reshape(mols,1,slots), feats, table, vec(gain), vec(shift), wq, vec(bq), wk, wv, vec(bv), wo, vec(bo), vec(fgain), vec(fshift), bias)


LOGICAL = pl.DeviceIdType.LOGICAL


class Place:
    def __init__(self, dpbits):
        tensor, dp = lax.axis_index("tensor"), lax.axis_index("dp")
        me = dp * 4 + tensor
        self.bits, self.partners = {}, {}
        for axis, index, count, stride in (("tensor", tensor, 2, 1), ("dp", dp, dpbits, 4)):
            for bit in range(count):
                value = lax.rem(lax.div(index, 1 << bit), 2)
                self.bits[axis, bit] = value
                self.partners[axis, bit] = me + (1 - 2 * value) * (stride << bit)


class Exchange:
    def __init__(self, at, src, dst, sems, slot, stage, before=None, after=None):
        self.before, self.after = before, after
        self.copy = lambda: pltpu.make_async_remote_copy(
            src_ref=src(), dst_ref=dst(), send_sem=sems.at[0, slot], recv_sem=sems.at[1, slot],
            device_id=at.partners[stage], device_id_type=LOGICAL)

    def start(self):
        if self.before is not None:
            self.before()
        self.copy().start()

    def wait(self):
        self.copy().wait()
        if self.after is not None:
            self.after()


class Pause:
    def __init__(self, wait):
        self.wait = wait

    def start(self):
        pass


class Job:
    def __init__(self, at, buf, recv, sems, free, first_slot, rows, stages, done=None):
        self.done = done
        self.slots = 0
        self.recv_rows = 0
        self.steps = []
        plan = []
        numbers = []
        length = rows
        for stage in stages:
            halve = (length // 2) % 8 == 0
            part = length // 2 if halve else length
            plan.append((stage, halve, length, part, self.recv_rows))
            self.recv_rows += part
            length = part
        halved = [p[0] for p in plan if p[1]]

        def offset(count):
            off, size = 0, rows
            for axis, bit in halved[:count]:
                size //= 2
                off = off + at.bits[axis, bit] * size
            return off if isinstance(off, int) else pl.multiple_of(off, 8)

        depth = 0
        for stage, halve, length, part, place in plan:
            here = depth
            if halve:
                depth += 1

                def src(stage=stage, here=here, part=part):
                    return buf.at[pl.ds(pl.multiple_of(offset(here) + (1 - at.bits[stage]) * part, 8), part)]
            else:
                def src(here=here, part=part):
                    return buf.at[pl.ds(offset(here), part)]

            def dst(place=place, part=part):
                return recv.at[pl.ds(place, part)]

            def add(depth=depth, place=place, part=part, to=buf):
                mine = pl.ds(offset(depth), part)
                to[mine, :] = buf[mine, :] + recv[pl.ds(place, part), :]

            number = first_slot + self.slots

            def tell(number=number, stage=stage):
                pl.semaphore_signal(free.at[number], inc=1, device_id=at.partners[stage], device_id_type=LOGICAL)

            self.steps.append((Exchange(at, src, dst, sems, number, stage, after=tell if halve else None), add))
            numbers.append(number)
            self.slots += 1
        if plan[-1][1]:
            self.steps.append((Pause(lambda number=numbers[-1]: pl.semaphore_wait(free.at[number], 1)), None))
        for (stage, halve, length, part, place), number in zip(reversed(plan), reversed(numbers)):
            if not halve:
                continue

            def freed(number=number):
                pl.semaphore_wait(free.at[number], 1)

            def region(depth=depth, part=part):
                return buf.at[pl.ds(offset(depth), part)]

            if number == numbers[-1]:
                freed = None
            self.steps.append((Exchange(at, region, region, sems, first_slot + self.slots, stage, before=freed), None))
            self.slots += 1
            depth -= 1
        self.ticks = len(self.steps) + 1

    def tick(self, k):
        if k > 0:
            exchange, add = self.steps[k - 1]
            exchange.wait()
            if add is not None:
                add()
        if k < len(self.steps):
            self.steps[k][0].start()
        elif self.done is not None:
            self.done()


class Actions:
    def __init__(self, *functions):
        self.tick = lambda k: functions[k]()


def job_need(rows, stages):
    job = Job(None, None, None, None, None, 0, rows, stages)
    return job.recv_rows, job.slots


ORDERS = ("CXYZW", "CXZWY", "CYXZW", "CYZWX", "CZWXY", "CXZYW", "CZXYW", "CZYXW")
E_ORDERS = ("YZW", "ZWY", "ZYW")


def stages_of(order, dpbits):
    table = {"C": [("tensor", 0)], "X": [("tensor", 1)], "Y": [("dp", i) for i in range(dpbits - 2)],
             "Z": [("dp", dpbits - 2)], "W": [("dp", dpbits - 1)]}
    return [stage for token in order for stage in table[token]]


def stage_cost(stage, size):
    rate = 41.0e3
    if stage is None:
        return [], 1.0 + size
    axis, bit = stage
    if axis == "tensor":
        return ([("core", size / 700e3)], 0.9) if bit == 0 else ([("x", size / rate)], 2.3)
    if bit == 0:
        return [("y", size / rate)], 2.3
    if bit == 1:
        return [("outer", size / rate)], 2.3
    return [("outer", size / rate), ("inner", 2 * size / rate)], 2.9


def tick_order(segments, jobs):
    now, free, flying, points, current = 0.0, {}, [], [], []
    segments = list(segments)
    ended = set()

    def start(name, k):
        stage, size, _ = jobs[name][k]
        links, latency = stage_cost(stage, size)
        begin = max([now] + [free.get(link, 0.0) for link, _ in links])
        for link, length in links:
            free[link] = begin + length
        flying.append((begin + max([length for _, length in links], default=0.0) + latency, name, k))

    while segments or flying:
        ready = [f for f in flying if f[0] <= now]
        if ready:
            first = min(ready)
            flying.remove(first)
            _, name, k = first
            now += 0.2 + (jobs[name][k][1] / 1.5e6 if jobs[name][k][2] else 0.0)
            current.append((name, k + 1))
            if k + 1 < len(jobs[name]):
                start(name, k + 1)
            else:
                ended.add(name)
        elif segments and all(name in ended for name in segments[0][3]):
            points.append(current)
            current = []
            _, length, released, _ = segments.pop(0)
            now += length
            for name in released:
                start(name, 0)
        else:
            now = min(f[0] for f in flying)
    points.append(current)
    return points[1:]


def job_steps(rows, width, stages, hold=0.0):
    length, out, back = rows, [], []
    for stage in stages:
        halve = (length // 2) % 8 == 0
        length = length // 2 if halve else length
        out.append((stage, length * width * 4, True))
        if halve:
            back.append((stage, length * width * 4, False))
    return out + ([(None, hold, False)] if halve else []) + back[::-1]


def make_plan(config, dpbits, mols, groups, width, hidden, small):
    ne, ch, fs, no = config["ne"], config["ch"], config["fs"], config["no"]
    jobs, steps = {}, {}

    def add(name, kind, index, first, rows, stages, cols):
        jobs[name] = (kind, index, first, rows, stages)
        steps[name] = job_steps(rows, cols, stages, config["hold"].get(name, 0.0))

    for i in range(ne):
        n = (width + hidden) // ne
        add("e%d" % i, "e", 0, i * n, n, stages_of(E_ORDERS[config["eo"][i]], dpbits), width)
    for i in range(no):
        n = width // no
        add("o%d" % i, "o", 0, i * n, n, stages_of(ORDERS[config["oo"][i]], dpbits), width)
    for c in range(ch):
        for h in range(fs):
            n = 3 * width // fs
            add("f%d_%d" % (c, h), "f", c, h * n, n, stages_of(ORDERS[config["fo"][c * fs + h]], dpbits), width // ch)
    add("s", "s", 0, 0, small, stages_of(ORDERS[config["so"]], dpbits), width)
    add("b", "b", 0, 0, 8, stages_of("YZW", dpbits), hidden)
    q = ne // 4
    pos = config["pos"]
    segments = []

    def put(moment):
        for k in range(4):
            if pos[k] == moment:
                segments.append((("e", k), 0.65 if k < 2 else 1.3, ["e%d" % i for i in range(k * q, (k + 1) * q)], []))
        if pos[4] == moment:
            segments.append((("down",), 2.3, ["d"], []))

    swap = width * width * 2
    steps["d"] = [(("tensor", 0), swap, True), (("tensor", 1), swap, False)]
    steps["n"] = [(("tensor", 0), swap // 2, True), (("tensor", 1), swap // 2, False)]
    segments.append((("ffn",), 0.0, ["n", "b"], []))
    put(-2)
    segments.append((("pro1",), 1.2, ["o%d" % i for i in range(no)], ["n"]))
    put(-1)
    segments.append((("pro2",), 1.0, [], []))
    per = groups // ch
    for s in range(mols * groups):
        segments.append((("step", s), 0.9, [], []))
        if (s + 1) % (per * mols) == 0:
            c = s // (per * mols)
            segments.append((("chunk", c), 5.0 / ch, ["f%d_%d" % (c, h) for h in range(fs)], []))
        put(s)
    segments.append((("end",), 0.6, ["s"], []))
    return jobs, segments, tick_order(segments, steps)


def gelu_and_slope(x):
    cdf = 0.5 + 0.5 * lax.erf(x * (0.5 ** 0.5))
    return x * cdf, cdf + x * (jnp.exp(-0.5 * x * x) * (1.0 / math.sqrt(2.0 * math.pi)))


def mm3_nt(ahi, alo, bhi, blo):
    return dot_nt(ahi, bhi) + (dot_nt(ahi, blo) + dot_nt(alo, bhi))


def mm3_nn(ahi, alo, bhi, blo):
    return dot(ahi, bhi) + (dot(ahi, blo) + dot(alo, bhi))


def main_kernel(plan, *refs):
    refs = list(refs)
    take_n = lambda n: [refs.pop(0) for _ in range(n)]
    len_ref, types_ref, normed2_any = take_n(3)
    cot_refs = take_n(2)
    held_any = take_n(10)
    gain_ref, shift_ref, fgain_ref, bup_ref, bdown_ref = take_n(5)
    wup_any, wdown_any, wq_any, wk_any, wv_any, wo_any, pair_any, e_any = take_n(8)
    gpair, outv, gatv, eres, ores, fres, sres, bres = take_n(8)
    dl, qhi, qlo, khi, klo, vhi, vlo, dmhi, dmlo, dqt, dkt, dvt, maskc, dmid, energy = take_n(15)
    wq, wk, wv, wo, wuhi, wulo, wdhi, wdlo = take_n(8)
    gath, cots, duhi, dulo, pn, pd, rsn, rsd, nt, dn1 = take_n(10)
    ebuf, erecv, obuf, orecv, fbuf, frecv, sbuf, srecv, tbuf, tres, trecv, bbuf, brecv = take_n(13)
    middle_ref, first_ref, mixt_ref, linv_ref, pring, ering = take_n(6)
    rsems, free, lsems = take_n(3)
    assert not refs
    s = pl.program_id(0)
    mols, slots = types_ref.shape[0], types_ref.shape[2]
    groups = dl.shape[1]
    heads = groups * 8
    width = wo.shape[0]
    hidden = wuhi.shape[1]
    rows = mols * slots
    types = plan["types"]
    last = mols * groups - 1
    at = Place(plan["dpbits"])
    core, xbit = ("tensor", 0), ("tensor", 1)
    dpbits = [("dp", i) for i in range(plan["dpbits"])]
    wide = [core, xbit] + dpbits
    jobs, segments, points = plan["jobs"], plan["segments"], plan["points"]
    chunks = plan["chunks"]
    fcols = width // chunks

    tiles = [(r, c) for r in range(rows // 128) for c in range(hidden // 128)]

    across = hidden // 128

    def keep(base, b, x, top=0):
        for i, (r, c) in enumerate(tiles):
            if r < x.shape[0] // 128:
                gpair[0, base + b * len(tiles) + top * across + i] = x[r * 128:(r + 1) * 128, c * 128:(c + 1) * 128]

    def kept(base, b, top=0, n=rows // 128):
        parts = [gpair[0, base + b * len(tiles) + top * across + i] for i in range(n * across)]
        return jnp.concatenate([jnp.concatenate(parts[r * across:(r + 1) * across], 1) for r in range(n)], 0)

    ACT, DACT = 0, 4 * len(tiles)
    slot = [0]

    def swap(src, dst, stage):
        slot[0] += 1
        return Exchange(at, lambda: src, lambda: dst, rsems, slot[0] - 1, stage)

    hrows = rows // 2
    hpart = [pl.ds(i * hrows, hrows) for i in range(2)]
    n_core = swap(normed2_any, gath.at[1], core)
    n_x = [swap(normed2_any.at[h], gath.at[2, h], xbit) for h in hpart]
    c_core = swap(cot_refs[0], cots.at[1], core)
    c_diag = swap(cot_refs[1], cots.at[3], core)
    n_diag = [swap(gath.at[2, h], gath.at[3, h], core) for h in hpart]
    dn_core = swap(pn.at[1], rsn.at[0], core)
    dn_diag = [swap(pn.at[3, h], rsn.at[1, h], core) for h in hpart]
    dn_x = [swap(pn.at[2, h], rsn.at[2, h], xbit) for h in hpart]
    dd_core = swap(pd.at[1], rsd.at[0], core)
    dd_diag = swap(pd.at[3], rsd.at[1], core)
    dd_x = swap(pd.at[2], rsd.at[2], xbit)

    def make(buf, res, recv, nrows, stages):
        def done():
            res[...] = buf[...]
        job = Job(at, buf, recv, rsems, free, slot[0], nrows, stages, done)
        slot[0] += job.slots
        return job

    total_job = make(tbuf, tres, trecv, 8, wide)
    running = {}
    place = {"e": 0, "o": 0, "f": 0}
    for name, (kind, index, first_row, nrows, stages) in jobs.items():
        if kind == "s":
            running[name] = make(sbuf, sres, srecv, nrows, stages)
        elif kind == "b":
            running[name] = make(bbuf, bres, brecv, nrows, stages)
        else:
            need = job_need(nrows, stages)[0]
            if kind == "f":
                buf, res, recv = fbuf.at[index], fres.at[index], frecv
            else:
                buf, res, recv = {"e": (ebuf, eres, erecv), "o": (obuf, ores, orecv)}[kind]
            running[name] = make(buf.at[pl.ds(first_row, nrows)], res.at[pl.ds(first_row, nrows)], recv.at[pl.ds(place[kind], need)], nrows, stages)
            place[kind] += need
    assert slot[0] == plan["slots"], slot[0]
    half = width // 2

    def n_sum(i):
        dn_diag[i].wait()
        pn[2, hpart[i], :] = pn[2, hpart[i], :] + rsn[1, hpart[i], :]
        dn_x[i].start()

    def n_end():
        dn_core.wait()
        dn_x[0].wait()
        dn_x[1].wait()

    def d_begin():
        dd_diag.start()
        dd_core.start()

    def d_sum():
        dd_diag.wait()
        pd[2] = pd[2] + rsd[1]
        dd_x.start()

    def d_end():
        dd_core.wait()
        dd_x.wait()
        outv[...] = middle_ref[...] + bdown_ref[...] + (pd[0] + (rsd[0] + rsd[2]))

    running["n"] = Actions(dn_diag[1].start, functools.partial(n_sum, 1), n_end)
    running["d"] = Actions(d_begin, d_sum, d_end)

    cot_load = [pltpu.make_async_copy(cot_refs[b], cots.at[2 * b], lsems.at[b]) for b in range(2)]
    piece = width // rows
    up_load = [pltpu.make_async_copy(wup_any.at[pl.ds(i * rows, rows)], pn.at[i], lsems.at[4 + i]) for i in range(piece)]
    down_load = [pltpu.make_async_copy(wdown_any.at[pl.ds(i * rows, rows)], pn.at[2 + i], lsems.at[6 + i]) for i in range(piece)]
    load = [pltpu.make_async_copy(a, b, lsems.at[8 + i]) for i, (a, b) in enumerate(((wo_any, wo), (wq_any, wq), (wk_any, wk), (wv_any, wv)))]
    own_load = pltpu.make_async_copy(normed2_any, gath.at[0], lsems.at[12])
    held = (first_ref, middle_ref, qhi, qlo, khi, klo, vhi, vlo, mixt_ref, linv_ref)
    held_load = [pltpu.make_async_copy(a, b, lsems.at[13 + i]) for i, (a, b) in enumerate(zip(held_any, held))]
    depth = pring.shape[0]

    def ring(step):
        which = lax.rem(step, depth)
        mol, first_head = lax.rem(step, mols), lax.div(step, mols) * 8
        return [pltpu.make_async_copy(a.at[mol, pl.ds(first_head, 8)], r.at[which], lsems.at[23 + i * depth + which])
                for i, (a, r) in enumerate(((pair_any, pring), (e_any, ering)))]

    def seg_ffn():
        barrier = pltpu.get_barrier_semaphore()
        for stage in wide:
            pl.semaphore_signal(barrier, inc=1, device_id=at.partners[stage], device_id_type=LOGICAL)
        pl.semaphore_wait(barrier, len(wide))
        for copy in n_x:
            copy.start()
        c_core.start()
        c_diag.start()
        n_core.start()
        for copy in down_load + cot_load[:1] + up_load + cot_load[1:] + [own_load]:
            copy.start()
        square = jnp.zeros((1, 1), F32)
        for m in range(mols):
            f = jnp.full((1, 1), len_ref[m], jnp.int32).astype(F32)
            square = square + f * f
        tbuf[...] = jnp.broadcast_to(square, tbuf.shape)
        total_job.tick(0)
        bbuf[...] = jnp.zeros_like(bbuf)
        sbuf[...] = jnp.zeros_like(sbuf)
        for copy in down_load:
            copy.wait()
        for i in range(piece):
            part = pl.ds(i * rows, rows)
            wdhi[part, :], wdlo[part, :] = split(pn[2 + i])
        for copy in cot_load + up_load:
            copy.wait()
        for i in range(piece):
            part = pl.ds(i * rows, rows)
            wuhi[part, :], wulo[part, :] = split(pn[i])
        total_job.tick(1)
        for copy in held_load + load:
            copy.start()
        for step in range(depth - 1):
            for copy in ring(step):
                copy.start()

        def p1(b, carry):
            hi, lo = split(cots[b])
            keep(DACT, b, mm3_nt(hi, lo, wdhi[...], wdlo[...]))
            return carry

        lax.fori_loop(0, 2, lambda b, carry: p1(2 * b, carry), 0)
        c_core.wait()
        c_diag.wait()
        lax.fori_loop(0, 2, lambda b, carry: p1(2 * b + 1, carry), 0)
        own_load.wait()
        n_core.wait()
        total_job.tick(2)

        def p2(b, top=0, n=rows // 128):
            part = pl.ds(top * 128, n * 128)
            hi, lo = split(gath[b, part, :])
            upper = mm3_nn(hi, lo, wuhi[...], wulo[...]) + bup_ref[...]
            a, slope = gelu_and_slope(upper)
            keep(ACT, b, a, top)
            du = kept(DACT, b, top, n) * slope
            dhi, dlo = split(du)
            duhi[b, part, :] = dhi
            dulo[b, part, :] = dlo
            bbuf[...] = bbuf[...] + jnp.broadcast_to(jnp.sum(du, axis=0, keepdims=True), bbuf.shape)
            pn[b, part, :] = mm3_nt(dhi, dlo, wuhi[...], wulo[...])

        def p2_loop(b, carry):
            p2(b)
            return carry

        lax.fori_loop(0, 2, p2_loop, 0)
        dn_core.start()
        first_work()
        n = hrows // 128
        for i in range(2):
            n_x[i].wait()
            n_diag[i].start()
            p2(2, i * n, n)
            n_diag[i].wait()
            p2(3, i * n, n)
            total_job.tick(3 + i)
            if i == 0:
                dn_diag[0].start()
                n_sum(0)
        running["n"].tick(0)
        running["b"].tick(0)

    def first_work():
        for copy in held_load:
            copy.wait()
        first = first_ref[...]
        cen = first - jnp.mean(first, axis=-1, keepdims=True)
        rstd = lax.rsqrt(jnp.mean(cen * cen, axis=-1, keepdims=True) + EPSILON)
        normed = cen * rstd * gain_ref[...] + shift_ref[...]
        for m in range(mols):
            nt[:, m * slots:(m + 1) * slots] = jnp.transpose(normed[m * slots:(m + 1) * slots])
        dn1[...] = jnp.zeros_like(dn1)
        energy[...] = jnp.zeros_like(energy)
        for k in range(2):
            lax.fori_loop(0, 2, functools.partial(weight_part, k), 0)

    def down_part(b, carry):
        hi, lo = split(kept(ACT, b))
        pd[b] = mm3_nn(hi, lo, wdhi[...], wdlo[...])
        return carry

    def weight_part(k, b, carry):
        part = slice((k % 2) * half, (k % 2 + 1) * half)
        left = kept(ACT, b)[:, part] if k < 2 else gath[b, :, part]
        ahi, alo = split(jnp.transpose(left))
        if k < 2:
            chi, clo = split(cots[b])
        else:
            chi, clo = duhi[b], dulo[b]
        g = mm3_nn(ahi, alo, chi, clo)
        to = pl.ds(k * half, half)

        @pl.when(b == 0)
        def _():
            ebuf[to, :] = g

        @pl.when(b > 0)
        def _():
            ebuf[to, :] = ebuf[to, :] + g
        return carry

    def seg_e(k):
        lax.fori_loop(2 if k < 2 else 0, 4, functools.partial(weight_part, k), 0)
        q = plan["ne"] // 4
        for i in range(k * q, (k + 1) * q):
            running["e%d" % i].tick(0)

    def seg_down():
        lax.fori_loop(0, 4, down_part, 0)
        running["d"].tick(0)

    def small(i, value):
        sbuf[types + i:types + i + 1, :] = value

    def seg_pro1():
        mid = middle_ref[...]
        cen = mid - jnp.mean(mid, axis=-1, keepdims=True)
        rstd = lax.rsqrt(jnp.mean(cen * cen, axis=-1, keepdims=True) + EPSILON)
        xhat = cen * rstd
        c = pn[0] + (rsn[0] + rsn[2])
        small(0, jnp.sum(c * xhat, axis=0, keepdims=True))
        small(1, jnp.sum(c, axis=0, keepdims=True))
        cot = cots[0]
        small(2, jnp.sum(cot, axis=0, keepdims=True))
        ce = c * fgain_ref[...]
        dmiddle = cot + rstd * (ce - jnp.mean(ce, axis=-1, keepdims=True) - xhat * jnp.mean(ce * xhat, axis=-1, keepdims=True))
        dmid[...] = dmiddle
        small(3, jnp.sum(dmiddle, axis=0, keepdims=True))
        for copy in load:
            copy.wait()
        dhi, dlo = split(dmiddle)
        mhi, mlo = split(jnp.concatenate([mixt_ref[m] for m in range(mols)], 1))
        obuf[...] = mm3_nn(mhi, mlo, dhi, dlo)
        for i in range(plan["no"]):
            running["o%d" % i].tick(0)

    def seg_pro2():
        for k in range(5, total_job.ticks):
            total_job.tick(k)
        wohi, wolo = split(wo[...])
        dhi, dlo = split(dmid[...])
        dm = mm3_nt(dhi, dlo, wohi, wolo)
        lane = lax.broadcasted_iota(jnp.int32, (slots, 128), 1)
        rowi = lax.broadcasted_iota(jnp.int32, (slots, slots), 0)
        coli = lax.broadcasted_iota(jnp.int32, (slots, slots), 1)
        twice = 2.0 / (heads * tres[0:1, 0:slots])
        for m in range(mols):
            length = len_ref[m]
            maskc[m] = jnp.where(jnp.logical_and(rowi < length, coli < length), twice, 0.0)
            dmt = jnp.transpose(dm[m * slots:(m + 1) * slots]) * linv_ref[m]
            dmhi[m], dmlo[m] = split(dmt)
            prod = dmt * mixt_ref[m]
            delta = jnp.sum(prod.reshape(heads, 8, slots), axis=1)
            for g in range(groups):
                d8 = -delta[g * 8:(g + 1) * 8]
                x = jnp.concatenate([dmt[g * 64:(g + 1) * 64], d8, d8, jnp.zeros((48, slots), F32)], 0)
                y = jnp.transpose(x)
                yhi = y.astype(BF).astype(F32)
                ylo = y - yhi
                dl[m, g, :, 0:128] = jnp.where(lane < 64, yhi, pltpu.roll(ylo, 64, 1)).astype(BF)
                dl[m, g, :, 128:256] = jnp.where(lane < 72, yhi, ylo).astype(BF)

    def seg_chunk(c):
        part = slice(c * fcols, (c + 1) * fcols)
        nhi, nlo = split(nt[...])
        for i, t_ref in enumerate((dqt, dkt, dvt)):
            thi, tlo = split(jnp.concatenate([t_ref[mm, part, :] for mm in range(mols)], 1))
            fbuf[c, i * width:(i + 1) * width, :] = mm3_nt(nhi, nlo, thi, tlo)
        for h in range(plan["fs"]):
            running["f%d_%d" % (c, h)].tick(0)
        acc = dn1[...]
        for i, (t_ref, w) in enumerate(((dqt, wq), (dkt, wk), (dvt, wv))):
            nat = jnp.concatenate([jnp.transpose(t_ref[mm, part, :]) for mm in range(mols)], 0)
            if i != 1:
                r = types + (4 if i == 0 else 5)
                sbuf[r:r + 1, part] = jnp.sum(nat, axis=0, keepdims=True)
            ahi, alo = split(nat)
            whi, wlo = split(w[:, part])
            acc = acc + mm3_nt(ahi, alo, whi, wlo)
        dn1[...] = acc

    def seg_end():
        first = first_ref[...]
        cen = first - jnp.mean(first, axis=-1, keepdims=True)
        rstd = lax.rsqrt(jnp.mean(cen * cen, axis=-1, keepdims=True) + EPSILON)
        xhat = cen * rstd
        dn = dn1[...]
        small(6, jnp.sum(dn * xhat, axis=0, keepdims=True))
        small(7, jnp.sum(dn, axis=0, keepdims=True))
        ge = dn * gain_ref[...]
        gat = dmid[...] + rstd * (ge - jnp.mean(ge, axis=-1, keepdims=True) - xhat * jnp.mean(ge * xhat, axis=-1, keepdims=True))
        gatv[...] = gat
        acc = None
        for mm in range(mols):
            one = (lax.broadcasted_iota(jnp.int32, (types, slots), 0) == types_ref[mm]).astype(F32).astype(BF)
            for bits in split3(gat[mm * slots:(mm + 1) * slots]):
                part = dot(one, bits)
                acc = part if acc is None else acc + part
        sbuf[0:types, :] = acc
        total = jnp.sum(jnp.sum(energy[...], axis=0, keepdims=True), axis=1, keepdims=True) * 0.5
        small(8, jnp.broadcast_to(total, (1, width)))
        running["s"].tick(0)

    work = {"ffn": seg_ffn, "e": seg_e, "down": seg_down, "pro1": seg_pro1, "pro2": seg_pro2, "chunk": seg_chunk, "end": seg_end}
    before, after = [], {}
    step_now = None
    for (name, _, _, _), ticks in zip(segments, points):
        if name[0] == "step":
            step_now = name[1]
        else:
            to = before if step_now is None else after.setdefault(step_now, [])
            to.append(functools.partial(work[name[0]], *name[1:]))
        to = before if step_now is None else after.setdefault(step_now, [])
        to += [functools.partial(running[job].tick, k) for job, k in ticks]

    @pl.when(s == 0)
    def _():
        for fn in before:
            fn()

    g = s // mols
    m = s % mols
    lhs = dl[m, g]
    which = lax.rem(s, depth)
    for copy in ring(s):
        copy.wait()

    @pl.when(s + depth - 1 <= last)
    def _():
        for copy in ring(s + depth - 1):
            copy.start()

    sub = lax.broadcasted_iota(jnp.int32, (16, 128), 0)
    z = jnp.zeros((16, 256), BF)
    zero16 = jnp.zeros((16, 128), BF)
    mc = maskc[m]
    en = energy[...]
    for p in range(4):
        row = pl.multiple_of(g * 64 + 16 * p, 16)
        rows16 = pl.ds(row, 16)

        def blk(x):
            x = x.astype(F32)
            a = jnp.where(sub < 8, x, 0.0).astype(BF)
            b = jnp.where(sub >= 8, x, 0.0).astype(BF)
            return jnp.concatenate([a, b], axis=1)
        bhi, blo = blk(vhi[m, rows16, :]), blk(vlo[m, rows16, :])
        sel = jnp.concatenate([jnp.where(sub % 8 == 2 * p, 1.0, 0.0), jnp.where(sub % 8 == 2 * p + 1, 1.0, 0.0)], axis=1).astype(BF)
        rws = [bhi if i == p else z for i in range(4)]
        rws += rws
        rws += [blo if i == p else z for i in range(4)]
        rws += [sel, z, z, z]
        dp = dot(lhs, jnp.concatenate(rws, axis=0))
        gs = []
        es = []
        for hf in range(2):
            both = ering[which, 2 * p + hf]
            es.append(both)
            e = both[:, 0:128].astype(F32) + both[:, 128:256].astype(F32)
            logits = pring[which, 2 * p + hf]
            t = logits * mc
            en = en + t * logits
            gp = e * dp[:, hf * 128:(hf + 1) * 128] + t
            gpair[m, g * 8 + 2 * p + hf] = gp
            gs.append(split(gp))

        def rows_lhs(hi, lo):
            return jnp.concatenate([jnp.concatenate([hi, hi], 1), jnp.concatenate([lo, zero16], 1)], 0)

        def take(out):
            acc = out[0:16] + out[16:32]
            return jnp.concatenate([acc[0:8, 0:128], acc[8:16, 128:256]], 0)
        ecol = jnp.concatenate([jnp.concatenate([es[0][:, 0:128], es[1][:, 0:128]], 1), jnp.concatenate([es[0][:, 128:256], es[1][:, 128:256]], 1)], 0)
        dvt[m, rows16, :] = take(dot(rows_lhs(dmhi[m, rows16, :], dmlo[m, rows16, :]), ecol))
        gcol = jnp.concatenate([jnp.concatenate([gs[0][0], gs[1][0]], 1), jnp.concatenate([gs[0][1], gs[1][1]], 1)], 0)
        dkt[m, rows16, :] = take(dot(rows_lhs(qhi[m, rows16, :], qlo[m, rows16, :]), gcol))
        grow = jnp.concatenate([jnp.concatenate(gs[0], 1), jnp.concatenate(gs[1], 1)], 0)
        dqt[m, rows16, :] = take(dot_nt(rows_lhs(khi[m, rows16, :], klo[m, rows16, :]), grow)) * (8 ** -0.5)
    energy[...] = en

    for moment in sorted(after):
        def body(moment=moment):
            for fn in after[moment]:
                fn()
        pl.when(s == moment)(body)


CONFIG = dict(ne=8, ch=4, fs=2, no=1, eo=[0, 0, 0, 0, 0, 0, 0, 0], fo=[2, 5, 0, 0, 3, 0, 0, 6], oo=[0], so=4, pos=[-1, -2, 1, -2, -2], hold={'e1': 4, 'e4': 32, 'e5': 32, 'e3': 4, 'e0': 32, 'f1_1': 8, 'e7': 8, 'e2': 2, 'f1_0': 4, 'e6': 4})


def main_call(mesh, lengths, types, normed2, cots, held, gain, shift, fgain, bup, bdown,
              wup, wdown, wq, wk, wv, wo, pair, e, ntypes):
    mols, slots = types.shape
    rows, width = normed2.shape
    heads = pair.shape[1]
    groups = heads // 8
    hidden = wup.shape[1]
    dp = mesh.shape["dp"]
    dpbits = dp.bit_length() - 1
    assert (1 << dpbits) == dp and mesh.shape["tensor"] == 4
    small = -(-(ntypes + 9) // 64) * 64
    config = CONFIG if dpbits <= 3 else dict(ne=4, ch=1, fs=1, no=1, eo=[0] * 4, fo=[0], oo=[0], so=0, pos=[-2, -2, -2, -2, -2], hold={})
    jobs, segments, points = make_plan(config, dpbits, mols, groups, width, hidden, small)
    chunks = config["ch"]
    fcols = width // chunks
    needs = {"e": 0, "o": 0, "f": 0, "s": 0, "b": 0}
    stages = stages_of("CXYZW", dpbits)
    t_need = job_need(8, stages)
    nslots = 15 + t_need[1]
    for kind, index, first_row, nrows, order in jobs.values():
        need = job_need(nrows, order)
        needs[kind] += need[0]
        nslots += need[1]
    plan = dict(dpbits=dpbits, chunks=chunks, types=ntypes, slots=nslots, jobs=jobs, segments=segments, points=points,
                ne=config["ne"], no=config["no"], fs=config["fs"])
    V = pltpu.VMEM
    one = lambda shape: pl.BlockSpec(shape, lambda s: (0,) * len(shape), pipeline_mode=pl.Buffered(1))
    any_ = pl.BlockSpec(memory_space=pl.ANY)
    smem = pl.BlockSpec(memory_space=pltpu.SMEM)
    vmem = pl.BlockSpec(memory_space=pltpu.VMEM)
    vec = lambda v: v.reshape(1, -1)
    tt = (mols, width, slots)
    rw = (rows, width)
    in_specs = [smem, one((mols, 1, slots))] + [any_] * 13 + \
        [one((1, width))] * 3 + [one((1, hidden)), one((1, width))] + [any_] * 8
    ww = (width, width)
    ff = (width + hidden, width)
    outs = [V(pair.shape, F32), V(rw, F32), V(rw, F32), V(ff, F32), V(ww, F32), V((chunks, 3 * width, fcols), F32), V((small, width), F32), V((8, hidden), F32)]
    four = (4, rows, width)
    scratch = [V((mols, groups, slots, 256), BF)] + [V(tt, BF)] * 8 + [V(tt, F32)] * 3 + [V((mols, slots, slots), F32), V(rw, F32), V((slots, slots), F32)]
    scratch += [V(ww, F32)] * 4 + [V((width, hidden), BF)] * 2 + [V((hidden, width), BF)] * 2
    scratch += [V(four, F32)] * 2 + [V(four, BF)] * 2 + [V(four, F32)] * 2 + [V((3, rows, width), F32)] * 2 + [V((width, rows), F32), V(rw, F32)]
    scratch += [V(ff, F32), V((needs["e"], width), F32), V(ww, F32), V((needs["o"], width), F32)]
    scratch += [V((chunks, 3 * width, fcols), F32), V((needs["f"], fcols), F32), V((small, width), F32), V((needs["s"], width), F32)]
    scratch += [V((8, 128), F32)] * 2 + [V((t_need[0], 128), F32), V((8, hidden), F32), V((needs["b"], hidden), F32)]
    scratch += [V(rw, F32)] * 2 + [V(tt, F32)] * 2 + [V((DEPTH, 8, slots, slots), F32), V((DEPTH, 8, slots, 2 * slots), BF)]
    scratch += [pltpu.SemaphoreType.DMA((2, nslots)), pltpu.SemaphoreType.REGULAR((nslots,)), pltpu.SemaphoreType.DMA((23 + 2 * DEPTH,))]
    return pl.pallas_call(functools.partial(main_kernel, plan), out_shape=outs, grid=(mols * groups,), in_specs=in_specs, out_specs=[vmem] * 8,
        scratch_shapes=scratch,
        compiler_params=pltpu.CompilerParams(vmem_limit_bytes=VLIMIT, dimension_semantics=("arbitrary",), collective_id=0, has_side_effects=True),
        name="feed_forward_and_backward",
    )(lengths, types.reshape(mols, 1, slots), normed2, *cots, *held, vec(gain), vec(shift), vec(fgain), vec(bup), vec(bdown),
      wup, wdown, wq, wk, wv, wo, pair, e)


DEPTH = 4
VLIMIT = 47 * 1024 * 1024
SMALL_ROWS = (0, 1, 2, 3, 4, 5, 6, 7)


def finish_kernel(types, gpair, outv, gatv, eres, ores, fres, sres, bres, *refs):
    refs = list(refs)
    gp_out, atom_out, gatoms_out, gdown_out, gup_out, gwo_out, gwq_out, gwk_out, gwv_out, table_out = [refs.pop(0) for _ in range(10)]
    rows_out = [refs.pop(0) for _ in range(len(SMALL_ROWS))]
    gbup_out, pen_out, sems = refs
    width = outv.shape[1]
    hidden = eres.shape[0] - width
    copies = []

    def go(src, dst):
        copy = pltpu.make_async_copy(src, dst, sems.at[len(copies)])
        copy.start()
        copies.append(copy)

    for m in range(gpair.shape[0]):
        for h in range(0, gpair.shape[1], 16):
            go(gpair.at[m, pl.ds(h, 16)], gp_out.at[m, pl.ds(h, 16)])
    go(eres.at[pl.ds(0, hidden)], gdown_out)
    go(eres.at[pl.ds(hidden, width)], gup_out)
    go(ores, gwo_out)
    chunks, _, fcols = fres.shape
    for c in range(chunks):
        for j, out in enumerate((gwq_out, gwk_out, gwv_out)):
            go(fres.at[c, pl.ds(j * width, width)], out.at[:, pl.ds(c * fcols, fcols)])
    go(outv, atom_out)
    go(gatv, gatoms_out)
    go(sres.at[pl.ds(0, types)], table_out)
    for i, out in zip(SMALL_ROWS, rows_out):
        out[...] = sres[types + i, :]
    gbup_out[...] = bres[0, :]
    pen_out[0, 0] = jnp.sum(sres[types + 8:types + 9, 0:1])
    for copy in copies:
        copy.wait()


def finish(types, parts, width, hidden):
    gpair, outv, gatv, eres, ores, fres, sres, bres = parts
    S = jax.ShapeDtypeStruct
    any_ = pl.BlockSpec(memory_space=pl.ANY)
    vmem = pl.BlockSpec(memory_space=pltpu.VMEM)
    shapes = [gpair.shape, outv.shape, gatv.shape, (hidden, width), (width, hidden)] + [(width, width)] * 4 + [(types, width)]
    outs = [S(shape, F32) for shape in shapes] + [S((width,), F32)] * len(SMALL_ROWS) + [S((hidden,), F32), S((1, 1), F32)]
    ncopies = gpair.shape[0] * gpair.shape[1] // 16 + 6 + 3 * fres.shape[0]
    return pl.pallas_call(functools.partial(finish_kernel, types), out_shape=outs, in_specs=[vmem] * 8,
        out_specs=[any_] * 10 + [vmem] * (len(SMALL_ROWS) + 1) + [pl.BlockSpec(memory_space=pltpu.SMEM)],
        scratch_shapes=[pltpu.SemaphoreType.DMA((ncopies,))], compiler_params=pltpu.CompilerParams(vmem_limit_bytes=4 * 1024 * 1024),
        name="finish")(*parts)


def local(mesh, atom_types, lengths, atom_feats, pair_bias, out_cotangent, type_table, norm_gain, norm_shift, w_query, b_query,
          w_key, w_value, b_value, w_out, b_out, ffn_gain, ffn_shift, w_up, b_up, w_down, b_down):
    tensor = mesh.shape["tensor"]
    cots = [out_cotangent, lax.ppermute(out_cotangent, "tensor", [(i, i ^ 2) for i in range(tensor)])]
    pair_out, e, first, qhi, qlo, khi, klo, vhi, vlo, mixt, linv, middle, normed2 = attention_forward(
        lengths, atom_types, atom_feats, type_table, norm_gain, norm_shift, w_query, b_query, w_key, w_value, b_value, w_out, b_out,
        ffn_gain, ffn_shift, pair_bias)
    types = type_table.shape[0]
    parts = main_call(
        mesh, lengths, atom_types, normed2, cots, (first, middle, qhi, qlo, khi, klo, vhi, vlo, mixt, linv), norm_gain, norm_shift, ffn_gain, b_up, b_down,
        w_up, w_down, w_query, w_key, w_value, w_out, pair_out, e, types)
    (grad_pair, atom_out, grad_atoms, gwdown, gwup, gwo, gwq, gwk, gwv, table, g_fgain, g_fshift, g_bdown, g_bout, g_bq, g_bv, g_gain, g_shift,
     gbup, penalty) = finish(types, parts, w_up.shape[0], w_up.shape[1])
    return (atom_out, pair_out, penalty.reshape(()), grad_atoms, grad_pair, table, g_gain, g_shift, gwq, g_bq, gwk, gwv, g_bv,
            gwo, g_bout, g_fgain, g_fshift, gwup, gbup, gwdown, g_bdown)


def solution(mesh):
    in_specs = (
        P(("dp", "tensor"), None),
        P(("dp", "tensor")),
        P(("dp", "tensor"), None),
        P(("dp", "tensor"), None, None, None),
        P(("dp", "tensor"), None),
        P(),
        P(),
        P(),
        P(),
        P(),
        P(),
        P(),
        P(),
        P(),
        P(),
        P(),
        P(),
        P(None, "tensor"),
        P("tensor"),
        P("tensor", None),
        P(),
    )
    out_specs = (
        P(("dp", "tensor"), None),
        P(("dp", "tensor"), None, None, None),
        P(),
        P(("dp", "tensor"), None),
        P(("dp", "tensor"), None, None, None),
        P(),
        P(),
        P(),
        P(),
        P(),
        P(),
        P(),
        P(),
        P(),
        P(),
        P(),
        P(),
        P(None, "tensor"),
        P("tensor"),
        P("tensor", None),
        P(),
    )
    return jax.shard_map(functools.partial(local, mesh), mesh=mesh, in_specs=in_specs, out_specs=out_specs, check_vma=False)
```
